32 devices in a mesh: dp: 8 (over z, x), tensor: 4 (over y, core).
Axes of the slice: x: 2, y: 2, z: 4, core: 2. Of those that a mesh axis runs over, the one named last changes fastest.
Arguments:
- layer_input: bfloat16 [2048, 1024], P(('dp', 'tensor')), may hold values from -6 to 6
- seq_ids: int32 [8, 256], P('dp'), may hold values from 0 to 2, never falling along the last dimension, each value on 1 to 128 neighbouring positions
- expert_ids: int32 [2048, 8], P('dp'), may hold values from 0 to 31, all different within a row; in each aligned block of 256 rows (0 to 255, 256 to 511, ...) at most 128 rows name the same one
- out_grad: bfloat16 [2048, 1024], P(('dp', 'tensor')), may hold values from -6 to 6
- gain_attn: bfloat16 [1024], P('dp'), may hold values from 0.099609375 to 1.8984375
- gain_moe: bfloat16 [1024], P('dp'), may hold values from 0.099609375 to 1.8984375
- w_query: bfloat16 [1024, 1024], P('dp', 'tensor'), may hold values from -0.1875 to 0.1875
- w_key: bfloat16 [1024, 512], P('dp', 'tensor'), may hold values from -0.1875 to 0.1875
- w_value: bfloat16 [1024, 512], P('dp', 'tensor'), may hold values from -0.1875 to 0.1875
- w_output: bfloat16 [1024, 1024], P('tensor', 'dp'), may hold values from -0.75 to 0.75
- w_router: bfloat16 [1024, 32], P('dp'), may hold values from -0.046875 to 0.046875
- w_gate: bfloat16 [32, 1024, 512], P(None, 'dp', 'tensor'), may hold values from -0.1875 to 0.1875
- w_up: bfloat16 [32, 1024, 512], P(None, 'dp', 'tensor'), may hold values from -0.1875 to 0.1875
- w_down: bfloat16 [32, 512, 1024], P(None, 'tensor', 'dp'), may hold values from -2 to 2
Outputs:
- layer_output: bfloat16 [2048, 1024], P(('dp', 'tensor'))
- input_grad: bfloat16 [2048, 1024], P(('dp', 'tensor'))
- grad_gain_attn: float32 [1024], P('dp')
- grad_gain_moe: float32 [1024], P('dp')
- grad_query: float32 [1024, 1024], P('dp', 'tensor')
- grad_key: float32 [1024, 512], P('dp', 'tensor')
- grad_value: float32 [1024, 512], P('dp', 'tensor')
- grad_output: float32 [1024, 1024], P('tensor', 'dp')
- grad_router: float32 [1024, 32], P('dp')
- grad_gate: float32 [32, 1024, 512], P(None, 'dp', 'tensor')
- grad_up: float32 [32, 1024, 512], P(None, 'dp', 'tensor')
- grad_down: float32 [32, 512, 1024], P(None, 'tensor', 'dp')
The draws below stay inside these ranges and needn't reach their ends.
Inputs may be any that keep to these rules, and one draw needn't show every extreme that they name: `seq_ids`: in each row the sequence number never falls; each of the 3 sequences holds 1 to 128 tokens and one holds exactly 128. `expert_ids`: each row names 8 different experts. Within each aligned block of 256 rows no expert is named by more than 128 rows, a bound that some block reaches.
All inputs are finite; a program needn't handle non-finite values.
Results may differ from the reference program's by a relative error of at most 0.018.
Values may be sent and summed in bfloat16 or wider, within the bound.
No kernel may reach another device: no remote copies, remote signals or barrier semaphores. Data moves between devices by JAX's collectives and lax.ppermute only.
A program may use at most 192 MiB of HBM per device.

```python
import math
import jax
import jax.numpy as jnp
import numpy as np
from jax import lax

D = 1024
H = 16
KV = 8
HD = 64
E = 32
FF = 512
TOP = 8
TOK_DEV = 256
TOKENS = 2048
BLOCKS = 8
CAP = 128
SEGS = 3
MAXLEN = 128


def shard_levels(key, dims, split, least, largest):
    level = 1.0
    for dim, parts in split:
        draws = jax.random.uniform(jax.random.fold_in(jax.random.fold_in(key, 6), dim), (parts,), jnp.float32, least / len(split), largest / len(split))
        level = level * jnp.repeat(jnp.exp(draws), dims[dim] // parts).reshape((-1,) + (1,) * (len(dims) - 1 - dim))
    return level


def profile(number_of, total, most, slope):
    portions = [(1 << 20) // math.isqrt(grade ** slope) + 1 for grade in range(2, number_of + 1)]
    surplus, counts = total - most - (number_of - 1), [1] * (number_of - 1)
    while surplus > 0:
        candidates = [i for i in range(number_of - 1) if counts[i] < most]
        mass, remaining = sum([portions[i] for i in candidates]), surplus
        for i in candidates:
            more = min(most - counts[i], max(1, remaining * portions[i] // mass), surplus)
            counts[i] = counts[i] + more
            surplus = surplus - more
    return np.array([most] + counts)


def uneven(rng, number_of, total, most, lean):
    if number_of == 2:
        one = jax.random.randint(rng, (), max(1, total - most), min(most, total - 1) + 1)
        return jnp.stack([one, total - one])
    lengths = jnp.asarray(profile(number_of, total, most, lean), jnp.int32)
    twos = (number_of - 1) // 2
    donor, taker = lengths[1:1 + 2 * twos:2], lengths[2:2 + 2 * twos:2]
    margin = jnp.minimum(donor - 1, most - taker)
    shifted = jax.random.randint(jax.random.fold_in(rng, 1), (twos,), 0, 1 << 20) % (margin + 1)
    lengths = lengths.at[1:1 + 2 * twos:2].set(donor - shifted).at[2:2 + 2 * twos:2].set(taker + shifted)
    return lengths[jax.random.permutation(jax.random.fold_in(rng, 2), number_of)]


def assign_block(rng, own, number, rows, count, top, limit, lean):
    order = jax.random.permutation(rng, count)
    packed, ordinary = portions_of(count, rows * top, limit, lean, True), portions_of(count, rows * top, limit, lean, False)
    places = jnp.arange(count)

    def named(sizes, rotation):
        used = int((sizes > 0).sum())
        fixed = max(1, used // 4)
        passed = fixed + (places - fixed + rotation * (used - fixed)) % max(1, count - fixed)
        return jnp.zeros((count,), jnp.int32).at[order[jnp.where(places < fixed, places, passed)]].set(jnp.asarray(sizes, jnp.int32))

    sizes = jnp.where(number % 4 == 0, named(packed, number // 4), named(ordinary, number - number // 4 - 1))
    mixed = jax.random.permutation(jax.random.fold_in(own, 3), count)
    giver, sink = mixed[0:count // 2 * 2:2], mixed[1:count // 2 * 2:2]
    slack = jnp.minimum(sizes[giver] - 1, limit - sizes[sink]) // 2
    slack = jnp.where((giver == order[0]) | (sink == order[0]) | (sizes[sink] == 0), 0, jnp.maximum(slack, 0))
    passed = jax.random.randint(jax.random.fold_in(own, 4), (count // 2,), 0, 1 << 20) % (slack + 1)
    sizes = sizes.at[giver].add(-passed).at[sink].add(passed)
    labels = jnp.searchsorted(jnp.cumsum(sizes), jnp.arange(rows * top), side="right").astype(jnp.int32)
    listing = labels.reshape(top, rows).T
    listing = listing[jax.random.permutation(jax.random.fold_in(own, 1), rows)]
    rotation = jax.random.randint(jax.random.fold_in(own, 2), (rows, 1), 0, top)
    return jnp.take_along_axis(listing, (jnp.arange(top)[None, :] + rotation) % top, axis=1)


def portions_of(amount, total, most, lean, full):
    portions = [(1 << 20) // math.isqrt(standing ** lean) + 1 for standing in range(1, amount + 1)]
    largest = most if full else min(most, max(-(-total // amount), total * portions[0] // sum(portions)))
    least = 1 if total - largest >= amount - 1 else 0
    given, rest = [largest] + [least] * (amount - 1), total - largest - least * (amount - 1)
    while rest > 0:
        free = [i for i in range(1, amount) if given[i] < largest] or [i for i in range(1, amount) if given[i] < most]
        whole, remaining = sum([portions[i] for i in free]), rest
        for i in free:
            addition = min(most - given[i], max(1, remaining * portions[i] // whole), rest)
            given[i] = given[i] + addition
            rest = rest - addition
    return np.array(given)


def bell_draw(rng, extent, scale, bound, cuts=(), held_as=jnp.bfloat16):
    drawn = jax.random.normal(rng, extent, jnp.float32) * scale
    if len(cuts) > 0:
        drawn = shard_levels(rng, extent, cuts, -0.22, 0.18) * drawn
    return jnp.clip(drawn, min=-bound, max=bound).astype(held_as)


def setup_inputs(seed: int = 0) -> dict:
    splits = jax.random.split(jax.random.key(seed), 15)
    layer_input = bell_draw(splits[0], (TOKENS, D), 1.0, 6.0, ((0, 32),))
    seq_ids = jax.vmap(lambda own: jnp.searchsorted(jnp.cumsum(uneven(own, SEGS, TOK_DEV, MAXLEN, 2)), jnp.arange(TOK_DEV), side="right"))(jax.random.split(splits[1], BLOCKS)).reshape((BLOCKS, TOK_DEV)).astype(jnp.int32)
    expert_ids_keys = jax.random.split(jax.random.fold_in(splits[2], 1), TOKENS // TOK_DEV)
    expert_ids_turns = jax.random.permutation(jax.random.fold_in(splits[2], 3), TOKENS // TOK_DEV)
    expert_ids = jax.vmap(lambda own, number: assign_block(jax.random.fold_in(splits[2], 2), own, number, TOK_DEV, E, TOP, CAP, 2))(expert_ids_keys, expert_ids_turns).reshape((TOKENS, TOP))
    out_grad = bell_draw(splits[3], (TOKENS, D), 1.0, 6.0, ((0, 32),))
    gain_attn = jnp.clip(1.0 + 0.18 * jax.random.normal(splits[4], (D,), jnp.float32), 0.099609375, 1.8984375).astype(jnp.bfloat16)
    gain_moe = jnp.clip(1.0 + 0.18 * jax.random.normal(splits[5], (D,), jnp.float32), 0.099609375, 1.8984375).astype(jnp.bfloat16)
    w_query = bell_draw(splits[6], (D, H * HD), D ** -0.5, 0.1875, ((0, 8), (1, 4)))
    w_key = bell_draw(splits[7], (D, KV * HD), D ** -0.5, 0.1875, ((0, 8), (1, 4)))
    w_value = bell_draw(splits[8], (D, KV * HD), D ** -0.5, 0.1875, ((0, 8), (1, 4)))
    w_output = bell_draw(splits[9], (H * HD, D), (H * HD // 16) ** -0.5, 0.75, ((0, 4), (1, 8)))
    w_router = bell_draw(splits[10], (D, E), (D * 16) ** -0.5, 0.046875, ((0, 8),))
    w_gate = bell_draw(splits[11], (E, D, FF), D ** -0.5, 0.1875, ((1, 8), (2, 4)))
    w_up = bell_draw(splits[12], (E, D, FF), D ** -0.5, 0.1875, ((1, 8), (2, 4)))
    w_down = bell_draw(splits[13], (E, FF, D), (max(1, FF // 64)) ** -0.5, 2.0, ((1, 4), (2, 8)))
    return dict(layer_input=layer_input, seq_ids=seq_ids, expert_ids=expert_ids, out_grad=out_grad, gain_attn=gain_attn, gain_moe=gain_moe, w_query=w_query, w_key=w_key, w_value=w_value, w_output=w_output, w_router=w_router, w_gate=w_gate, w_up=w_up, w_down=w_down)


eps_norm = 1e-05
score_scale = 0.125
rope_base = 10000.0

def rms_forward(values, gain_vec):
    inverse = lax.rsqrt(lax.optimization_barrier(jnp.mean(values * values, axis=-1, keepdims=True)) + eps_norm)
    normed = values * inverse
    return (normed, inverse, (normed * gain_vec.astype(jnp.float32)).astype(jnp.bfloat16))

def rms_backward(upstream, normed, inverse, gain_vec):
    scaled = upstream * gain_vec.astype(jnp.float32)
    gain_grad = lax.optimization_barrier(jnp.sum(upstream * normed, axis=0))
    through = inverse * (scaled - normed * lax.optimization_barrier(jnp.mean(scaled * normed, axis=-1, keepdims=True)))
    return (through, gain_grad)

def rotary_tables(segment, head_size):
    length = segment.shape[0]
    places = jnp.arange(length, dtype=jnp.int32)
    change = jnp.concatenate([jnp.ones((1,), dtype=bool), segment[1:] != segment[:-1]])
    starts = lax.cummax(jnp.where(change, places, 0), axis=0)
    position = (places - starts).astype(jnp.float32)
    half_size = head_size // 2
    frequency = rope_base ** (-2.0 * jnp.arange(half_size, dtype=jnp.float32) / head_size)
    angles = position[:, None] * frequency[None, :]
    return (jnp.cos(angles), jnp.sin(angles))

def rotate(values, cosine, sine_table, rot_sign):
    shape_in = values.shape
    flattened = values.reshape(shape_in[0], -1, shape_in[-1])
    half_size = shape_in[-1] // 2
    first_half = flattened[..., :half_size]
    second_half = flattened[..., half_size:]
    cos_part = cosine[:, None, :]
    sin_part = rot_sign * sine_table[:, None, :]
    joined = jnp.concatenate([first_half * cos_part - second_half * sin_part, second_half * cos_part + first_half * sin_part], axis=-1)
    return joined.reshape(shape_in)

def attention_forward(query, key_rows, value_rows, allowed):
    scores = jnp.einsum('tkgd,skd->kgts', query.astype(jnp.float32), key_rows.astype(jnp.float32)) * score_scale
    exponent = jnp.where(allowed, jnp.exp(scores), 0.0)
    log_total = jnp.log(lax.optimization_barrier(jnp.sum(exponent, axis=-1, keepdims=True)))
    weights = jnp.where(allowed, jnp.exp(scores - log_total), 0.0).astype(jnp.bfloat16)
    attended = jnp.einsum('kgts,skd->tkgd', weights.astype(jnp.float32), value_rows.astype(jnp.float32))
    return (attended.astype(jnp.bfloat16), log_total)

def attention_backward(query, key_rows, value_rows, allowed, log_total, attended, attended_grad):
    scores = jnp.einsum('tkgd,skd->kgts', query.astype(jnp.float32), key_rows.astype(jnp.float32)) * score_scale
    probs = jnp.where(allowed, jnp.exp(scores - log_total), 0.0)
    probs_low = probs.astype(jnp.bfloat16)
    row_delta = lax.optimization_barrier(jnp.sum(attended_grad.astype(jnp.float32) * attended.astype(jnp.float32), axis=-1))
    row_delta = jnp.transpose(row_delta, (1, 2, 0))[..., None]
    prob_grad = jnp.einsum('tkgd,skd->kgts', attended_grad.astype(jnp.float32), value_rows.astype(jnp.float32))
    score_grad = (probs * (prob_grad - row_delta) * score_scale).astype(jnp.bfloat16)
    query_grad = jnp.einsum('kgts,skd->tkgd', score_grad.astype(jnp.float32), key_rows.astype(jnp.float32))
    key_grad = jnp.einsum('kgts,tkgd->skd', score_grad.astype(jnp.float32), query.astype(jnp.float32))
    value_grad = jnp.einsum('kgts,tkgd->skd', probs_low.astype(jnp.float32), attended_grad.astype(jnp.float32))
    return (query_grad, key_grad, value_grad)

def dispatch(expert_ids, experts, capacity):
    tok_count = expert_ids.shape[0]
    member = lax.optimization_barrier(jnp.sum((expert_ids[:, :, None] == jnp.arange(experts, dtype=jnp.int32)[None, None, :]).astype(jnp.int32), axis=1))
    earlier = jnp.cumsum(member, axis=0) - member
    rank_of = jnp.take_along_axis(earlier, expert_ids, axis=1)
    slot_of = (expert_ids * capacity + rank_of).astype(jnp.int32)
    token_of = jnp.broadcast_to(jnp.arange(tok_count, dtype=jnp.int32)[:, None], expert_ids.shape)
    slot_token = jnp.full((experts * capacity,), tok_count, dtype=jnp.int32).at[slot_of.reshape(-1)].set(token_of.reshape(-1))
    return (slot_of, slot_token)

def silu_backward(hidden_grad, gate_pre, up_pre):
    sigmoid_gate = jax.nn.sigmoid(gate_pre)
    gate_pre_grad = (hidden_grad * up_pre * sigmoid_gate * (1.0 + gate_pre * (1.0 - sigmoid_gate))).astype(jnp.bfloat16)
    up_pre_grad = (hidden_grad * gate_pre * sigmoid_gate).astype(jnp.bfloat16)
    return (gate_pre_grad, up_pre_grad)

def block_pass(weights, layer_input, segment, expert_ids, out_grad):
    gain_attn, gain_moe, w_query, w_key, w_value, w_output, w_router, w_gate, w_up, w_down = weights
    tok_count = layer_input.shape[0]
    grouping = H // KV
    inputs_f = layer_input.astype(jnp.float32)
    normed_one, inverse_one, hidden_one = rms_forward(inputs_f, gain_attn)
    cosine, sine_table = rotary_tables(segment, HD)
    places = jnp.arange(tok_count, dtype=jnp.int32)
    allowed = (segment[:, None] == segment[None, :]) & (places[:, None] >= places[None, :])
    query_pre = jnp.dot(hidden_one, w_query, preferred_element_type=jnp.float32).reshape(tok_count, KV, grouping, HD)
    query = rotate(query_pre, cosine, sine_table, 1.0).astype(jnp.bfloat16)
    key_pre = jnp.dot(hidden_one, w_key, preferred_element_type=jnp.float32).reshape(tok_count, KV, HD)
    key_rows = rotate(key_pre, cosine, sine_table, 1.0).astype(jnp.bfloat16)
    value_rows = jnp.dot(hidden_one, w_value, preferred_element_type=jnp.float32).reshape(tok_count, KV, HD).astype(jnp.bfloat16)
    attended, log_total = attention_forward(query, key_rows, value_rows, allowed)
    flat_out = attended.reshape(tok_count, H * HD)
    residual = inputs_f + jnp.dot(flat_out, w_output, preferred_element_type=jnp.float32)
    normed_two, inverse_two, hidden_two = rms_forward(residual, gain_moe)
    logits = jnp.dot(hidden_two, w_router, preferred_element_type=jnp.float32)
    exponent = jnp.exp(logits)
    router = exponent / lax.optimization_barrier(jnp.sum(exponent, axis=-1, keepdims=True))
    gates = jnp.take_along_axis(router, expert_ids, axis=1).astype(jnp.bfloat16)
    slot_of, slot_token = dispatch(expert_ids, E, CAP)
    slot_gate = jnp.zeros((E * CAP,), jnp.float32).at[slot_of.reshape(-1)].set(gates.reshape(-1).astype(jnp.float32)).reshape(E, CAP)
    rows_pad = jnp.concatenate([hidden_two, jnp.zeros((1, D), jnp.bfloat16)], axis=0)
    expert_rows = rows_pad[slot_token].reshape(E, CAP, D)
    gate_pre = jnp.einsum('ecd,edf->ecf', expert_rows.astype(jnp.float32), w_gate.astype(jnp.float32))
    up_pre = jnp.einsum('ecd,edf->ecf', expert_rows.astype(jnp.float32), w_up.astype(jnp.float32))
    hidden = (jax.nn.silu(gate_pre) * up_pre).astype(jnp.bfloat16)
    expert_out = jnp.einsum('ecf,efd->ecd', hidden.astype(jnp.float32), w_down.astype(jnp.float32))
    weighted = (expert_out * slot_gate[..., None]).reshape(-1, D)
    mixed = jnp.zeros((tok_count + 1, D), jnp.float32).at[slot_token].add(weighted)[:tok_count]
    layer_output = (residual + mixed).astype(jnp.bfloat16)
    grad_pad = jnp.concatenate([out_grad, jnp.zeros((1, D), jnp.bfloat16)], axis=0)
    grad_rows = grad_pad[slot_token].reshape(E, CAP, D)
    raw_grad = jnp.einsum('ecd,efd->ecf', grad_rows.astype(jnp.float32), w_down.astype(jnp.float32))
    gate_grad = lax.optimization_barrier(jnp.sum(hidden.astype(jnp.float32) * raw_grad, axis=-1))
    hidden_grad = raw_grad * slot_gate[..., None]
    scaled_out = (grad_rows.astype(jnp.float32) * slot_gate[..., None]).astype(jnp.bfloat16)
    down_grad = jnp.einsum('ecf,ecd->efd', hidden.astype(jnp.float32), scaled_out.astype(jnp.float32))
    gate_pre_grad, up_pre_grad = silu_backward(hidden_grad, gate_pre, up_pre)
    rows_grad = jnp.einsum('ecf,edf->ecd', gate_pre_grad.astype(jnp.float32), w_gate.astype(jnp.float32))
    rows_grad = rows_grad + jnp.einsum('ecf,edf->ecd', up_pre_grad.astype(jnp.float32), w_up.astype(jnp.float32))
    gate_w_grad = jnp.einsum('ecd,ecf->edf', expert_rows.astype(jnp.float32), gate_pre_grad.astype(jnp.float32))
    up_w_grad = jnp.einsum('ecd,ecf->edf', expert_rows.astype(jnp.float32), up_pre_grad.astype(jnp.float32))
    hidden_two_grad = jnp.zeros((tok_count + 1, D), jnp.float32).at[slot_token].add(rows_grad.reshape(-1, D))[:tok_count]
    gate_grads = gate_grad.reshape(-1)[slot_of]
    choose = (expert_ids[:, :, None] == jnp.arange(E, dtype=jnp.int32)[None, None, :]).astype(jnp.float32)
    prob_grad = lax.optimization_barrier(jnp.sum(gate_grads[:, :, None] * choose, axis=1))
    logit_grad = (router * (prob_grad - lax.optimization_barrier(jnp.sum(router * prob_grad, axis=-1, keepdims=True)))).astype(jnp.bfloat16)
    hidden_two_grad = hidden_two_grad + jnp.dot(logit_grad, w_router.T, preferred_element_type=jnp.float32)
    router_grad = jnp.dot(hidden_two.T, logit_grad, preferred_element_type=jnp.float32)
    through_two, gain_moe_grad = rms_backward(hidden_two_grad, normed_two, inverse_two, gain_moe)
    residual_grad = out_grad.astype(jnp.float32) + through_two
    residual_low = residual_grad.astype(jnp.bfloat16)
    attended_grad = jnp.dot(residual_low, w_output.T, preferred_element_type=jnp.float32).astype(jnp.bfloat16)
    attended_grad = attended_grad.reshape(tok_count, KV, grouping, HD)
    output_w_grad = jnp.dot(flat_out.T, residual_low, preferred_element_type=jnp.float32)
    query_grad, key_grad, value_grad = attention_backward(query, key_rows, value_rows, allowed, log_total, attended, attended_grad)
    query_low = rotate(query_grad, cosine, sine_table, -1.0).astype(jnp.bfloat16).reshape(tok_count, -1)
    key_low = rotate(key_grad, cosine, sine_table, -1.0).astype(jnp.bfloat16).reshape(tok_count, -1)
    value_low = value_grad.astype(jnp.bfloat16).reshape(tok_count, -1)
    query_w_grad = jnp.dot(hidden_one.T, query_low, preferred_element_type=jnp.float32)
    key_w_grad = jnp.dot(hidden_one.T, key_low, preferred_element_type=jnp.float32)
    value_w_grad = jnp.dot(hidden_one.T, value_low, preferred_element_type=jnp.float32)
    hidden_one_grad = jnp.dot(query_low, w_query.T, preferred_element_type=jnp.float32)
    hidden_one_grad = hidden_one_grad + jnp.dot(key_low, w_key.T, preferred_element_type=jnp.float32)
    hidden_one_grad = hidden_one_grad + jnp.dot(value_low, w_value.T, preferred_element_type=jnp.float32)
    through_one, gain_attn_grad = rms_backward(hidden_one_grad, normed_one, inverse_one, gain_attn)
    input_grad = (residual_grad + through_one).astype(jnp.bfloat16)
    grads = (gain_attn_grad, gain_moe_grad, query_w_grad, key_w_grad, value_w_grad, output_w_grad, router_grad, gate_w_grad, up_w_grad, down_grad)
    return (layer_output, input_grad, grads)

def reference(layer_input, seq_ids, expert_ids, out_grad, gain_attn, gain_moe, w_query, w_key, w_value, w_output, w_router, w_gate, w_up, w_down):
    weights = (gain_attn, gain_moe, w_query, w_key, w_value, w_output, w_router, w_gate, w_up, w_down)
    zero_grads = tuple((jnp.zeros(weight.shape, jnp.float32) for weight in weights))

    def one_block(totals, block):
        block_input, block_seq, block_ids, block_grad = block
        layer_out, block_input_grad, grads = block_pass(weights, block_input, block_seq, block_ids, block_grad)
        return (tuple((total + grad_term for total, grad_term in zip(totals, grads))), (layer_out, block_input_grad))
    blocks = (layer_input.reshape(BLOCKS, TOK_DEV, D), seq_ids, expert_ids.reshape(BLOCKS, TOK_DEV, TOP), out_grad.reshape(BLOCKS, TOK_DEV, D))
    totals, outputs = lax.scan(one_block, zero_grads, blocks)
    return (outputs[0].reshape(TOKENS, D), outputs[1].reshape(TOKENS, D), totals[0], totals[1], totals[2], totals[3], totals[4], totals[5], totals[6], totals[7], totals[8], totals[9])
```

```python
import functools

import jax
import jax.numpy as jnp
import numpy as np
from jax import lax
from jax.experimental import pallas as pl
from jax.experimental.pallas import tpu as pltpu
from jax.sharding import PartitionSpec as P

HD = 64
CAP = 128
LANES = 128

eps_norm = 1e-05
score_scale = 0.125
rope_base = 10000.0

BF = jnp.bfloat16
F32 = jnp.float32


def mm(a, b, ca, cb):
    return lax.dot_general(a, b, (((ca,), (cb,)), ((), ())), preferred_element_type=F32)


def call(kernel, name, outs, scratch=(), smem=0):
    def run(*args):
        in_specs = [pl.BlockSpec(memory_space=pltpu.SMEM)] * smem
        in_specs += [pl.BlockSpec(memory_space=pltpu.VMEM)] * (len(args) - smem)
        return pl.pallas_call(
            kernel,
            out_shape=[jax.ShapeDtypeStruct(s, d) for s, d in outs],
            in_specs=in_specs,
            out_specs=[pl.BlockSpec(memory_space=pltpu.VMEM)] * len(outs),
            scratch_shapes=[pltpu.VMEM(s, d) for s, d in scratch],
            name=name,
        )(*args)

    return run


def split_refs(refs, *counts):
    parts, at = [], 0
    for count in counts:
        parts.append(refs[at : at + count])
        at += count
    return parts


def norm_parts(values):
    inverse = lax.rsqrt(jnp.mean(values * values, axis=-1, keepdims=True) + eps_norm)
    return values * inverse, inverse


def norm_backward(upstream, normed, inverse, gain):
    scaled = upstream * gain
    return inverse * (scaled - normed * jnp.mean(scaled * normed, axis=-1, keepdims=True))


def rotate_lanes(values, cosine, signed_sine):
    width = values.shape[1]
    half = HD // 2
    lane = lax.broadcasted_iota(jnp.int32, values.shape, 1)
    ahead = pltpu.roll(values, width - half, 1)
    behind = pltpu.roll(values, half, 1)
    partner = jnp.where(lane % HD < half, ahead, behind)
    copies = width // LANES
    return values * jnp.concatenate([cosine] * copies, 1) + partner * jnp.concatenate(
        [signed_sine] * copies, 1
    )


def allowed_pairs(seg_col, seg_row, length):
    rows = lax.broadcasted_iota(jnp.int32, (length, length), 0)
    cols = lax.broadcasted_iota(jnp.int32, (length, length), 1)
    return (seg_col == seg_row) & (rows >= cols)


def attn_fwd_kernel(peers, dims, *refs):
    n_q, n_kv = dims
    (idx,), (x,), w_in, (cos, sin, seg_c, seg_r), outs = split_refs(refs, 1, 1, peers, 4, 7)
    wall, gains, qkv, att, log_out, part, hid = outs
    rows = w_in[0].shape[0]
    for m in range(peers):
        at = pl.multiple_of(jnp.bitwise_xor(idx[0], m) * rows, rows)
        wall[pl.ds(at, rows), :] = w_in[m][...]
    qk_w = (n_q + n_kv) * HD
    all_w = (n_q + 2 * n_kv) * HD
    o_at = all_w + n_q * HD
    misc_t = jnp.transpose(wall[:, o_at : o_at + LANES].astype(F32))
    gains[...] = misc_t[32:40, :]
    gain = misc_t[32:33, :]
    normed, _ = norm_parts(x[...].astype(F32))
    hidden = (normed * gain).astype(BF)
    hid[...] = hidden
    pre = jnp.dot(hidden, wall[:, :all_w], preferred_element_type=F32)
    qk = rotate_lanes(pre[:, :qk_w], cos[...], sin[...]).astype(BF)
    value = pre[:, qk_w:].astype(BF)
    qkv[...] = jnp.concatenate([qk, value], 1)
    length = x.shape[0]
    allowed = allowed_pairs(seg_c[...], seg_r[...], length)
    group = n_q // n_kv
    outs_h, logs = [], []
    for h in range(n_q):
        g = h // group
        q_h = qk[:, h * HD : (h + 1) * HD]
        k_g = qk[:, (n_q + g) * HD : (n_q + g + 1) * HD]
        v_g = value[:, g * HD : (g + 1) * HD]
        scores = mm(q_h, k_g, 1, 1) * score_scale
        total = jnp.sum(jnp.where(allowed, jnp.exp(scores), 0.0), axis=-1, keepdims=True)
        log_total = jnp.log(total)
        probs = jnp.where(allowed, jnp.exp(scores - log_total), 0.0).astype(BF)
        outs_h.append(jnp.dot(probs, v_g, preferred_element_type=F32).astype(BF))
        logs.append(log_total)
    flat = jnp.concatenate(outs_h, 1)
    att[...] = flat
    lane = lax.broadcasted_iota(jnp.int32, (length, LANES), 1)
    packed = jnp.zeros((length, LANES), F32)
    for h in range(n_q):
        packed = jnp.where(lane == h, logs[h], packed)
    log_out[...] = packed
    part[...] = mm(flat, wall[:, all_w:o_at], 1, 1).astype(BF)


def post_attn_kernel(experts, shares, part, x, gains, misc, res, router, msg):
    own = x.shape[0]
    width = x.shape[1]
    total = x[...].astype(F32)
    for s in range(shares):
        total = total + part[s * own : (s + 1) * own, :].astype(F32)
    res[...] = total
    normed, _ = norm_parts(total)
    h2 = (normed * gains[1:2, :]).astype(BF)
    logits = jnp.dot(h2, misc[...], preferred_element_type=F32)
    lane = lax.broadcasted_iota(jnp.int32, logits.shape, 1)
    exponent = jnp.where(lane < experts, jnp.exp(logits), 0.0)
    probs = exponent / jnp.sum(exponent, axis=-1, keepdims=True)
    router[...] = probs
    msg[:, :width] = h2
    msg[:, width:] = probs.astype(BF)


def onehot_kernel(peers, shares, idx, ids, grads, *outs):
    gt = outs[0]
    slots = outs[1:]
    length = ids.shape[0]
    lane = lax.broadcasted_iota(jnp.int32, (length, LANES), 1)
    expert = jnp.bitwise_xor(idx[0], lane) * shares + idx[1]
    ids_v = ids[...]
    member = jnp.zeros((length, LANES), F32)
    for k in range(ids_v.shape[1]):
        hit = (ids_v[:, k : k + 1] == expert) & (lane < peers)
        member = member + jnp.where(hit, 1.0, 0.0)
    r = lax.broadcasted_iota(jnp.int32, (length, length), 0)
    c = lax.broadcasted_iota(jnp.int32, (length, length), 1)
    lower = jnp.where(r > c, 1.0, 0.0).astype(BF)
    rank = jnp.dot(lower, member.astype(BF), preferred_element_type=F32)
    place = jnp.where(member > 0.0, rank, -1.0)
    slot = lane.astype(F32)
    for m in range(peers):
        hot = jnp.where(place[:, m : m + 1] == slot, 1.0, 0.0).astype(BF)
        gt[:, m * CAP : (m + 1) * CAP] = hot
        slots[m][...] = mm(hot, grads[...], 0, 0).astype(BF)


def dispatch_kernel(peers, gt, rows, *slots):
    for m in range(peers):
        slots[m][...] = mm(gt[:, m * CAP : (m + 1) * CAP], rows[...], 0, 0).astype(BF)


def gate_column(router_cols, expert):
    values = router_cols.astype(F32)
    lane = lax.broadcasted_iota(jnp.int32, values.shape, 1)
    return jnp.sum(jnp.where(lane == expert, values, 0.0), axis=-1, keepdims=True)


def load_down(pieces, down, dps, shares, at):
    for d in range(dps):
        for t in range(shares):
            down[t * 128 : (t + 1) * 128, d * 128 : (d + 1) * 128] = pieces[
                d * shares + t, at : at + 128, :
            ]


def expert_main_kernel(peers, shares, step, *refs):
    (idx,), rows_in, grads_in, (pieces,), rg_out, (hid, gpu), scratch = split_refs(
        refs, 1, peers, peers, 1, peers, 2, 5
    )
    rows, grads, wgu, down, back = scratch
    ff = shares * 128
    width = grads.shape[1]
    for m in range(peers):
        rows[m * CAP : (m + 1) * CAP, :] = rows_in[m][...]
        grads[m * CAP : (m + 1) * CAP, :] = grads_in[m][...]
    dps = width // 128
    for d in range(dps):
        for t in range(shares):
            p = d * shares + t
            wgu[d * 128 : (d + 1) * 128, t * 128 : (t + 1) * 128] = pieces[p, 0:128, :]
            wgu[d * 128 : (d + 1) * 128, ff + t * 128 : ff + (t + 1) * 128] = pieces[
                p, 128:256, :
            ]
    load_down(pieces, down, dps, shares, 256)
    expert = idx[0] * shares + idx[1]

    def body(c, carry):
        at = pl.ds(pl.multiple_of(c * step, step), step)
        gate = gate_column(rows[at, width:], expert)
        pre = jnp.dot(rows[at, :width], wgu[...], preferred_element_type=F32)
        raw = mm(grads[at, :], down[...], 1, 1)
        gate_pre = pre[:, :ff]
        up_pre = pre[:, ff:]
        sig = jax.nn.sigmoid(gate_pre)
        silu = gate_pre * sig
        hidden = (silu * up_pre).astype(BF)
        hid[at, :] = hidden
        gate_grad = jnp.sum(hidden.astype(F32) * raw, axis=-1, keepdims=True)
        hidden_grad = raw * gate
        gp = (hidden_grad * up_pre * sig * (1.0 + gate_pre * (1.0 - sig))).astype(BF)
        up = (hidden_grad * silu).astype(BF)
        both = jnp.concatenate([gp, up], 1)
        gpu[at, :] = both
        back[at, :width] = mm(both, wgu[...], 1, 1).astype(BF)
        lane = lax.broadcasted_iota(jnp.int32, (step, LANES), 1)
        back[at, width:] = jnp.where(lane == expert, gate_grad, 0.0).astype(BF)
        return carry

    lax.fori_loop(0, peers * CAP // step, body, 0)
    for m in range(peers):
        rg_out[m][...] = back[m * CAP : (m + 1) * CAP, :]


def expert_rest_kernel(peers, shares, step, *refs):
    (idx,), rows_in, grads_in, (pieces, hid, gpu), y_out, (grad_pieces,), scratch = split_refs(
        refs, 1, peers, peers, 3, peers, 1, 4
    )
    rows, scaled, down, y_all = scratch
    width = y_all.shape[1]
    dps = width // 128
    expert = idx[0] * shares + idx[1]
    load_down(pieces, down, dps, shares, 256)
    for m in range(peers):
        part = slice(m * CAP, (m + 1) * CAP)
        gate = gate_column(rows_in[m][:, width:], expert)
        rows[part, :] = rows_in[m][:, :width]
        scaled[part, :] = (grads_in[m][...].astype(F32) * gate).astype(BF)

    for m in range(peers):
        gate = gate_column(rows_in[m][:, width:], expert)
        out = jnp.dot(hid[m * CAP : (m + 1) * CAP, :], down[...], preferred_element_type=F32)
        y_out[m][...] = (out * gate).astype(BF)

    def body(c, carry):
        at = pl.ds(pl.multiple_of(c * step, step), step)
        both = mm(rows[:, at], gpu[...], 0, 0).astype(BF)
        down_g = mm(hid[...], scaled[:, at], 0, 0).astype(BF)
        for s in range(step // 128):
            for t in range(shares):
                p = (c * (step // 128) + s) * shares + t
                r = slice(s * 128, (s + 1) * 128)
                grad_pieces[p, 0:128, :] = both[r, t * 128 : (t + 1) * 128]
                grad_pieces[p, 128:256, :] = both[r, (shares + t) * 128 : (shares + t + 1) * 128]
                grad_pieces[p, 256:384, :] = down_g[t * 128 : (t + 1) * 128, r]
        return carry

    lax.fori_loop(0, width // step, body, 0)


def combine_kernel(peers, *refs):
    (gt,), slots, (out,), (all_slots,) = split_refs(refs, 1, peers, 1, 1)
    for m in range(peers):
        all_slots[m * CAP : (m + 1) * CAP, :] = slots[m][...]
    out[...] = jnp.dot(gt[...], all_slots[...], preferred_element_type=F32).astype(BF)


def hi_lo_rows(row, count):
    hi = row.astype(BF)
    lo = (row - hi.astype(F32)).astype(BF)
    place = lax.broadcasted_iota(jnp.int32, (count, row.shape[1]), 0)
    out = jnp.where(place == 0, hi.astype(F32), jnp.where(place == 1, lo.astype(F32), 0.0))
    return out.astype(BF)


def moe_back_kernel(shares, back, router, res, gains, misc, out_grad, rgrad, msg):
    own, width = res.shape
    total = jnp.zeros((own, back.shape[1]), F32)
    for s in range(shares):
        total = total + back[s * own : (s + 1) * own, :].astype(F32)
    upstream = total[:, :width]
    prob_grad = total[:, width:]
    probs = router[...]
    logit = (probs * (prob_grad - jnp.sum(probs * prob_grad, axis=-1, keepdims=True))).astype(BF)
    upstream = upstream + mm(logit, misc[...], 1, 1)
    normed, inverse = norm_parts(res[...])
    gain_grad = jnp.sum(upstream * normed, axis=0, keepdims=True)
    grad = out_grad[...].astype(F32) + norm_backward(upstream, normed, inverse, gains[1:2, :])
    rgrad[...] = grad
    msg[0:own, :width] = grad.astype(BF)
    msg[0:own, width:] = logit
    msg[own:, :width] = hi_lo_rows(gain_grad, msg.shape[0] - own)
    msg[own:, width:] = jnp.zeros((msg.shape[0] - own, LANES), BF)


def attn_bwd_kernel(peers, shares, dims, *refs):
    n_q, n_kv = dims
    ins, g_out, (msg2,), (sums,) = split_refs(refs, 13, peers, 1, 1)
    idx, msg, wall, qkv, att, logs, cos, sin, seg_c, seg_r, hid, rows2, x = ins
    length, width = x.shape
    own = length // shares
    span = msg.shape[0] // shares
    qk_w = (n_q + n_kv) * HD
    all_w = (n_q + 2 * n_kv) * HD
    o_at = all_w + n_q * HD
    resid = jnp.concatenate([msg[s * span : s * span + own, :width] for s in range(shares)], 0)
    logit = jnp.concatenate([msg[s * span : s * span + own, width:] for s in range(shares)], 0)
    gain_moe = jnp.zeros((1, width), F32)
    for s in range(shares):
        extra = msg[s * span + own : (s + 1) * span, :width].astype(F32)
        gain_moe = gain_moe + jnp.sum(extra, axis=0, keepdims=True)
    att_grad = jnp.dot(resid, wall[:, all_w:o_at], preferred_element_type=F32).astype(BF)
    allowed = allowed_pairs(seg_c[...], seg_r[...], length)
    group = n_q // n_kv
    lane = lax.broadcasted_iota(jnp.int32, (length, LANES), 1)
    log_all = logs[...]
    q_grads, k_grads, v_grads = [], [], []
    for g in range(n_kv):
        k_g = qkv[:, (n_q + g) * HD : (n_q + g + 1) * HD]
        v_g = qkv[:, qk_w + g * HD : qk_w + (g + 1) * HD]
        k_sum = jnp.zeros((length, HD), F32)
        v_sum = jnp.zeros((length, HD), F32)
        for h in range(g * group, (g + 1) * group):
            cut = slice(h * HD, (h + 1) * HD)
            q_h = qkv[:, cut]
            log_h = jnp.sum(jnp.where(lane == h, log_all, 0.0), axis=-1, keepdims=True)
            scores = mm(q_h, k_g, 1, 1) * score_scale
            probs = jnp.where(allowed, jnp.exp(scores - log_h), 0.0)
            a_h = att_grad[:, cut]
            delta = jnp.sum(
                a_h.astype(F32) * att[:, cut].astype(F32), axis=-1, keepdims=True
            )
            prob_grad = mm(a_h, v_g, 1, 1)
            s_grad = (probs * (prob_grad - delta) * score_scale).astype(BF)
            q_grads.append(jnp.dot(s_grad, k_g, preferred_element_type=F32))
            k_sum = k_sum + mm(s_grad, q_h, 0, 0)
            v_sum = v_sum + mm(probs.astype(BF), a_h, 0, 0)
        k_grads.append(k_sum)
        v_grads.append(v_sum)
    qk_grad = jnp.concatenate(q_grads + k_grads, 1)
    qk_low = rotate_lanes(qk_grad, cos[...], -sin[...]).astype(BF)
    low = jnp.concatenate([qk_low, jnp.concatenate(v_grads, 1).astype(BF)], 1)
    sums[:, :all_w] = mm(hid[...], low, 0, 0)
    sums[:, all_w:o_at] = mm(resid, att[...], 0, 0)
    place = lax.broadcasted_iota(jnp.int32, (LANES, width), 0)
    gain_hi = gain_moe.astype(BF).astype(F32)
    rows = jnp.where(place == 32, gain_hi, jnp.where(place == 33, gain_moe - gain_hi, 0.0))
    sums[:, o_at:] = mm(rows2[:, :width], logit, 0, 0) + jnp.transpose(rows)
    depth = g_out[0].shape[0]
    for m in range(peers):
        at = pl.multiple_of(jnp.bitwise_xor(idx[0], m) * depth, depth)
        g_out[m][...] = sums[pl.ds(at, depth), :].astype(BF)
    partial = mm(low, wall[:, :all_w], 1, 1)
    normed, _ = norm_parts(x[...].astype(F32))
    extra = hi_lo_rows(jnp.sum(partial * normed, axis=0, keepdims=True), span - own)
    low_part = partial.astype(BF)
    for s in range(shares):
        msg2[s * span : s * span + own, :] = low_part[s * own : (s + 1) * own, :]
        msg2[s * span + own : (s + 1) * span, :] = extra


def input_grad_kernel(shares, msg2, x, gains, rgrad, out, gain_out):
    own, width = x.shape
    span = msg2.shape[0] // shares
    upstream = jnp.zeros((own, width), F32)
    gain_sum = jnp.zeros((1, width), F32)
    for s in range(shares):
        upstream = upstream + msg2[s * span : s * span + own, :].astype(F32)
        extra = msg2[s * span + own : (s + 1) * span, :].astype(F32)
        gain_sum = gain_sum + jnp.sum(extra, axis=0, keepdims=True)
    normed, inverse = norm_parts(x[...].astype(F32))
    through = norm_backward(upstream, normed, inverse, gains[0:1, :])
    out[...] = (rgrad[...] + through).astype(BF)
    gain_out[...] = jnp.broadcast_to(gain_sum, gain_out.shape)


def layer_out_kernel(shares, mixed, res, out):
    own = res.shape[0]
    total = jnp.zeros(res.shape, F32)
    for s in range(shares):
        total = total + mixed[s * own : (s + 1) * own, :].astype(F32)
    out[...] = (res[...] + total).astype(BF)


def swap(values, peers):
    got = [values[0]]
    for m in range(1, peers):
        got.append(lax.ppermute(values[m], "dp", [(i, i ^ m) for i in range(peers)]))
    return got


def per_device(
    rep,
    layer_input,
    seq_ids,
    expert_ids,
    out_grad,
    gain_attn,
    gain_moe,
    w_query,
    w_key,
    w_value,
    w_output,
    w_router,
    w_gate,
    w_up,
    w_down,
):
    peers = lax.axis_size("dp")
    shares = lax.axis_size("tensor")
    own, width = layer_input.shape
    experts = w_gate.shape[0]
    length = seq_ids.shape[1]
    depth = width // peers
    q_w, kv_w = w_query.shape[1], w_key.shape[1]
    dims = (q_w // HD, kv_w // HD)
    all_w = q_w + 2 * kv_w
    pack_w = all_w + q_w + LANES
    slots = peers * CAP
    wide = width + LANES
    idx = jnp.stack([lax.axis_index("dp"), lax.axis_index("tensor")]).astype(jnp.int32)

    local = w_router.shape[0]
    pack = jnp.concatenate(
        [
            w_query,
            w_key,
            w_value,
            w_output.T,
            w_router,
            gain_attn[:, None],
            gain_moe[:, None],
            jnp.zeros((local, LANES - experts - 2), BF),
        ],
        axis=1,
    )
    if rep > 1:
        pack = lax.all_gather(pack, "rep", axis=0, tiled=True)
    packs = swap([pack] * peers, peers)

    x_all = lax.all_gather(layer_input, "tensor", axis=0, tiled=True)
    segment = seq_ids[0]
    before = jnp.sum((segment[None, :] < segment[:, None]).astype(jnp.int32), axis=1)
    position = (jnp.arange(length, dtype=jnp.int32) - before).astype(F32)
    lane = jnp.arange(LANES, dtype=jnp.int32) % HD
    half = HD // 2
    frequency = rope_base ** (-2.0 * (lane % half).astype(F32) / HD)
    angles = position[:, None] * frequency[None, :]
    cosine = jnp.cos(angles)
    sine = jnp.where(lane[None, :] < half, -1.0, 1.0) * jnp.sin(angles)
    seg_c = segment[:, None]
    seg_r = segment[None, :]

    wall, gains, qkv, att, logs, part, hid = call(
        functools.partial(attn_fwd_kernel, peers, dims),
        "attn_fwd",
        [
            ((width, pack_w), BF),
            ((8, width), F32),
            ((length, all_w), BF),
            ((length, q_w), BF),
            ((length, LANES), F32),
            ((length, width), BF),
            ((length, width), BF),
        ],
        smem=1,
    )(idx, x_all, *packs, cosine, sine, seg_c, seg_r)

    grads_all = lax.all_gather(out_grad, "tensor", axis=0, tiled=True)
    gt, *grad_slots = call(
        functools.partial(onehot_kernel, peers, shares),
        "onehot",
        [((length, slots), BF)] + [((CAP, width), BF)] * peers,
        smem=1,
    )(idx, expert_ids, grads_all)
    grad_in = swap(grad_slots, peers)

    experts_pack = jnp.concatenate(
        [w_gate, w_up, w_down if rep == 1 else jnp.swapaxes(w_down, 1, 2)], axis=1
    )
    experts_pack, _ = lax.optimization_barrier((experts_pack, packs))
    pieces = lax.all_to_all(
        experts_pack, ("dp", "tensor"), split_axis=0, concat_axis=0, tiled=True
    )
    if rep > 1:
        cut = pieces.reshape(experts, 3, w_gate.shape[1], w_gate.shape[2])
        cut = lax.all_gather(cut, "rep", axis=2, tiled=True)
        cut = jnp.stack([cut[:, 0], cut[:, 1], jnp.swapaxes(cut[:, 2], 1, 2)], axis=1)
        pieces = cut.reshape(experts, 3 * depth, w_gate.shape[2])

    misc = wall[:, all_w + q_w :]
    part = lax.all_to_all(part, "tensor", split_axis=0, concat_axis=0, tiled=True)
    res, router, msg = call(
        functools.partial(post_attn_kernel, experts, shares),
        "post_attn",
        [((own, width), F32), ((own, LANES), F32), ((own, wide), BF)],
    )(part, layer_input, gains, misc)
    rows_all = lax.all_gather(msg, "tensor", axis=0, tiled=True)
    row_slots = call(
        functools.partial(dispatch_kernel, peers), "dispatch", [((CAP, wide), BF)] * peers
    )(gt, rows_all)
    rows_in = swap(row_slots, peers)

    ff = w_gate.shape[2] * shares
    *row_back, hidden, gate_up = call(
        functools.partial(expert_main_kernel, peers, shares, 256),
        "expert_main",
        [((CAP, wide), BF)] * peers + [((slots, ff), BF), ((slots, 2 * ff), BF)],
        scratch=[
            ((slots, wide), BF),
            ((slots, width), BF),
            ((width, 2 * ff), BF),
            ((ff, width), BF),
            ((slots, wide), BF),
        ],
        smem=1,
    )(idx, *rows_in, *grad_in, pieces)
    back_in = swap(row_back, peers)
    *y_slots, grad_pieces = call(
        functools.partial(expert_rest_kernel, peers, shares, 256),
        "expert_rest",
        [((CAP, width), BF)] * peers + [((experts, 384, LANES), BF)],
        scratch=[
            ((slots, width), BF),
            ((slots, width), BF),
            ((ff, width), BF),
            ((slots, width), BF),
        ],
        smem=1,
    )(idx, *rows_in, *grad_in, pieces, hidden, gate_up)

    (row_grad,) = call(
        functools.partial(combine_kernel, peers),
        "combine_rows",
        [((length, wide), BF)],
        scratch=[((slots, wide), BF)],
    )(gt, *back_in)
    row_grad = lax.all_to_all(row_grad, "tensor", split_axis=0, concat_axis=0, tiled=True)
    rgrad, msg = call(
        functools.partial(moe_back_kernel, shares),
        "moe_back",
        [((own, width), F32), ((own + 16, wide), BF)],
    )(row_grad, router, res, gains, misc, out_grad)
    msg_all = lax.all_gather(msg, "tensor", axis=0, tiled=True)

    *w_grads, msg2 = call(
        functools.partial(attn_bwd_kernel, peers, shares, dims),
        "attn_bwd",
        [((depth, pack_w), BF)] * peers + [((shares * (own + 16), width), BF)],
        scratch=[((width, pack_w), F32)],
        smem=1,
    )(idx, msg_all, wall, qkv, att, logs, cosine, sine, seg_c, seg_r, hid, rows_all, x_all)
    w_sums = swap(w_grads, peers)
    total = sum(piece.astype(F32) for piece in w_sums)
    if rep > 1:
        total = lax.psum_scatter(total, "rep", scatter_dimension=0, tiled=True)

    msg2 = lax.all_to_all(msg2, "tensor", split_axis=0, concat_axis=0, tiled=True)
    input_grad, gain_rows = call(
        functools.partial(input_grad_kernel, shares),
        "input_grad",
        [((own, width), BF), ((8, width), F32)],
    )(msg2, layer_input, gains, rgrad)
    gain_cut = gain_rows[:1].reshape(peers, depth)
    gain_cut = lax.all_to_all(gain_cut, "dp", split_axis=0, concat_axis=0, tiled=True)
    gain_attn_grad = jnp.sum(gain_cut, axis=0)
    if rep > 1:
        gain_attn_grad = lax.psum_scatter(gain_attn_grad, "rep", scatter_dimension=0, tiled=True)

    y_in = swap(y_slots, peers)
    (mixed,) = call(
        functools.partial(combine_kernel, peers),
        "combine_out",
        [((length, width), BF)],
        scratch=[((slots, width), BF)],
    )(gt, *y_in)
    mixed = lax.all_to_all(mixed, "tensor", split_axis=0, concat_axis=0, tiled=True)
    (layer_output,) = call(
        functools.partial(layer_out_kernel, shares), "layer_out", [((own, width), BF)]
    )(mixed, res)

    if rep > 1:
        cut = grad_pieces.reshape(experts, 3, depth, LANES)
        cut = jnp.stack([cut[:, 0], cut[:, 1], jnp.swapaxes(cut[:, 2], 1, 2)], axis=1)
        cut = lax.psum_scatter(cut, "rep", scatter_dimension=2, tiled=True)
        grad_pieces = cut.reshape(experts, -1, LANES)
    grads = lax.all_to_all(
        grad_pieces, ("dp", "tensor"), split_axis=0, concat_axis=0, tiled=True
    ).astype(F32)
    third = grads.shape[1] // 3
    down_grad = grads[:, 2 * third :]
    if rep > 1:
        down_grad = jnp.swapaxes(down_grad, 1, 2)
    o_at = all_w + q_w
    return (
        layer_output,
        input_grad,
        gain_attn_grad,
        total[:, o_at + experts] + total[:, o_at + experts + 1],
        total[:, :q_w],
        total[:, q_w : q_w + kv_w],
        total[:, q_w + kv_w : all_w],
        total[:, all_w:o_at].T,
        total[:, o_at : o_at + experts],
        grads[:, :third],
        grads[:, third : 2 * third],
        down_grad,
    )


def solution(mesh):
    shares = mesh.shape["tensor"]
    peers = 32 // shares
    rep = mesh.shape["dp"] // peers
    dp = "dp"
    if rep > 1:
        devices = np.asarray(mesh.devices).reshape(peers, rep, shares)
        mesh = jax.sharding.Mesh(devices, ("dp", "rep", "tensor"))
        dp = ("dp", "rep")
    both = ("dp", "tensor") if rep == 1 else ("dp", "rep", "tensor")
    in_specs = (
        P(both, None),
        P(dp, None),
        P(dp, None),
        P(both, None),
        P(dp),
        P(dp),
        P(dp, "tensor"),
        P(dp, "tensor"),
        P(dp, "tensor"),
        P("tensor", dp),
        P(dp, None),
        P(None, dp, "tensor"),
        P(None, dp, "tensor"),
        P(None, "tensor", dp),
    )
    out_specs = (
        P(both, None),
        P(both, None),
        P(dp),
        P(dp),
        P(dp, "tensor"),
        P(dp, "tensor"),
        P(dp, "tensor"),
        P("tensor", dp),
        P(dp, None),
        P(None, dp, "tensor"),
        P(None, dp, "tensor"),
        P(None, "tensor", dp),
    )
    return jax.shard_map(
        functools.partial(per_device, rep),
        mesh=mesh,
        in_specs=in_specs,
        out_specs=out_specs,
        check_vma=False,
    )
```

```python
import functools

import jax
import jax.numpy as jnp
import numpy as np
from jax import lax
from jax.experimental import pallas as pl
from jax.experimental.pallas import tpu as pltpu
from jax.sharding import PartitionSpec as P


HD = 64
CAP = 128
LANES = 128

eps_norm = 1e-05
score_scale = 0.125
rope_base = 10000.0

BF = jnp.bfloat16
F32 = jnp.float32


def mm(a, b, ca, cb):
    return lax.dot_general(a, b, (((ca,), (cb,)), ((), ())), preferred_element_type=F32)


def call(kernel, outs, scratch=(), smem=0):
    def run(*args):
        in_specs = [pl.BlockSpec(memory_space=pltpu.SMEM)] * smem
        in_specs += [pl.BlockSpec(memory_space=pltpu.VMEM)] * (len(args) - smem)
        return pl.pallas_call(
            kernel,
            out_shape=[jax.ShapeDtypeStruct(s, d) for s, d in outs],
            in_specs=in_specs,
            out_specs=[pl.BlockSpec(memory_space=pltpu.VMEM)] * len(outs),
            scratch_shapes=[pltpu.VMEM(s, d) for s, d in scratch],
        )(*args)

    return run


def split_refs(refs, *counts):
    parts, at = [], 0
    for count in counts:
        parts.append(refs[at : at + count])
        at += count
    return parts


def norm_parts(values):
    inverse = lax.rsqrt(jnp.mean(values * values, axis=-1, keepdims=True) + eps_norm)
    return values * inverse, inverse


def norm_backward(upstream, normed, inverse, gain):
    scaled = upstream * gain
    return inverse * (scaled - normed * jnp.mean(scaled * normed, axis=-1, keepdims=True))


def rotate_lanes(values, cosine, signed_sine):
    width = values.shape[1]
    half = HD // 2
    lane = lax.broadcasted_iota(jnp.int32, values.shape, 1)
    ahead = pltpu.roll(values, width - half, 1)
    behind = pltpu.roll(values, half, 1)
    partner = jnp.where(lane % HD < half, ahead, behind)
    copies = width // LANES
    return values * jnp.concatenate([cosine] * copies, 1) + partner * jnp.concatenate(
        [signed_sine] * copies, 1
    )


def allowed_pairs(seg_col, seg_row, length):
    rows = lax.broadcasted_iota(jnp.int32, (length, length), 0)
    cols = lax.broadcasted_iota(jnp.int32, (length, length), 1)
    return (seg_col == seg_row) & (rows >= cols)


def scatter_rows(whole, parts, own):
    span = parts[0].shape[0]
    for s, out in enumerate(parts):
        at = pl.multiple_of(jnp.bitwise_xor(own, s) * span, span)
        out[...] = whole[pl.ds(at, span), :].astype(out.dtype)


def attn_fwd_kernel(peers, shares, dims, *refs):
    n_q, n_kv = dims
    (idx,), (x,), w_in, (cos, sin, seg_c, seg_r), parts, outs, (part,) = split_refs(
        refs, 1, 1, peers, 4, shares, 6, 1
    )
    wall, gains, qkv, att, log_out, hid = outs
    rows = w_in[0].shape[0]
    for m in range(peers):
        at = pl.multiple_of(jnp.bitwise_xor(idx[0], m) * rows, rows)
        wall[pl.ds(at, rows), :] = w_in[m][...]
    qk_w = (n_q + n_kv) * HD
    all_w = (n_q + 2 * n_kv) * HD
    o_at = all_w + n_q * HD
    misc_t = jnp.transpose(wall[:, o_at : o_at + LANES].astype(F32))
    gains[...] = misc_t[32:40, :]
    gain = misc_t[32:33, :]
    normed, _ = norm_parts(x[...].astype(F32))
    hidden = (normed * gain).astype(BF)
    hid[...] = hidden
    pre = jnp.dot(hidden, wall[:, :all_w], preferred_element_type=F32)
    qk = rotate_lanes(pre[:, :qk_w], cos[...], sin[...]).astype(BF)
    value = pre[:, qk_w:].astype(BF)
    qkv[...] = jnp.concatenate([qk, value], 1)
    length = x.shape[0]
    allowed = allowed_pairs(seg_c[...], seg_r[...], length)
    group = n_q // n_kv
    outs_h, logs = [], []
    for h in range(n_q):
        g = h // group
        q_h = qk[:, h * HD : (h + 1) * HD]
        k_g = qk[:, (n_q + g) * HD : (n_q + g + 1) * HD]
        v_g = value[:, g * HD : (g + 1) * HD]
        scores = mm(q_h, k_g, 1, 1) * score_scale
        total = jnp.sum(jnp.where(allowed, jnp.exp(scores), 0.0), axis=-1, keepdims=True)
        log_total = jnp.log(total)
        probs = jnp.where(allowed, jnp.exp(scores - log_total), 0.0).astype(BF)
        outs_h.append(jnp.dot(probs, v_g, preferred_element_type=F32).astype(BF))
        logs.append(log_total)
    flat = jnp.concatenate(outs_h, 1)
    att[...] = flat
    lane = lax.broadcasted_iota(jnp.int32, (length, LANES), 1)
    packed = jnp.zeros((length, LANES), F32)
    for h in range(n_q):
        packed = jnp.where(lane == h, logs[h], packed)
    log_out[...] = packed
    part[...] = mm(flat, wall[:, all_w:o_at], 1, 1)
    scatter_rows(part, parts, idx[1])


def post_attn_kernel(experts, shares, *refs):
    parts, (x, gains, misc, res, router, msg) = split_refs(refs, shares, 6)
    width = x.shape[1]
    total = x[...].astype(F32)
    for part in parts:
        total = total + part[...].astype(F32)
    res[...] = total
    normed, _ = norm_parts(total)
    h2 = (normed * gains[1:2, :]).astype(BF)
    logits = jnp.dot(h2, misc[...], preferred_element_type=F32)
    lane = lax.broadcasted_iota(jnp.int32, logits.shape, 1)
    exponent = jnp.where(lane < experts, jnp.exp(logits), 0.0)
    probs = exponent / jnp.sum(exponent, axis=-1, keepdims=True)
    router[...] = probs
    msg[:, :width] = h2
    msg[:, width:] = probs.astype(BF)


def onehot_kernel(peers, shares, idx, ids, grads, *outs):
    gt = outs[0]
    slots = outs[1:]
    length = ids.shape[0]
    lane = lax.broadcasted_iota(jnp.int32, (length, LANES), 1)
    expert = jnp.bitwise_xor(idx[0], lane) * shares + idx[1]
    ids_v = ids[...]
    member = jnp.zeros((length, LANES), F32)
    for k in range(ids_v.shape[1]):
        hit = (ids_v[:, k : k + 1] == expert) & (lane < peers)
        member = member + jnp.where(hit, 1.0, 0.0)
    r = lax.broadcasted_iota(jnp.int32, (length, length), 0)
    c = lax.broadcasted_iota(jnp.int32, (length, length), 1)
    lower = jnp.where(r > c, 1.0, 0.0).astype(BF)
    rank = jnp.dot(lower, member.astype(BF), preferred_element_type=F32)
    place = jnp.where(member > 0.0, rank, -1.0)
    slot = lane.astype(F32)
    for m in range(peers):
        hot = jnp.where(place[:, m : m + 1] == slot, 1.0, 0.0).astype(BF)
        gt[:, m * CAP : (m + 1) * CAP] = hot
        slots[m][...] = mm(hot, grads[...], 0, 0).astype(BF)


def dispatch_kernel(peers, gt, rows, *slots):
    for m in range(peers):
        slots[m][...] = mm(gt[:, m * CAP : (m + 1) * CAP], rows[...], 0, 0).astype(BF)


def gate_column(router_cols, expert):
    values = router_cols.astype(F32)
    lane = lax.broadcasted_iota(jnp.int32, values.shape, 1)
    return jnp.sum(jnp.where(lane == expert, values, 0.0), axis=-1, keepdims=True)


def load_down(own, pieces, down, shares):
    for m, piece in enumerate(pieces):
        at = pl.ds(pl.multiple_of(jnp.bitwise_xor(own, m) * 128, 128), 128)
        for t in range(shares):
            down[t * 128 : (t + 1) * 128, at] = piece[t, 256:384, :]


def weight_pack_kernel(peers, shares, idx, gate, up, down, *outs):
    for s in range(shares):
        for m in range(peers):
            e = jnp.bitwise_xor(idx[0], m) * shares + jnp.bitwise_xor(idx[1], s)
            for k, w in enumerate((gate, up, down)):
                outs[s][m, k * 128 : (k + 1) * 128, :] = w[e]


def regroup_kernel(peers, shares, *refs):
    ins, outs = split_refs(refs, shares, peers)
    for m in range(peers):
        for s in range(shares):
            outs[m][s] = ins[s][m]


def weight_grad_kernel(peers, shares, idx, *refs):
    ins, outs = split_refs(refs, peers, 3)
    for m in range(peers):
        for s in range(shares):
            e = jnp.bitwise_xor(idx[0], m) * shares + jnp.bitwise_xor(idx[1], s)
            for k in range(3):
                outs[k][e] = ins[m][s, k * 128 : (k + 1) * 128, :].astype(F32)


def expert_main_kernel(peers, shares, step, *refs):
    (idx,), rows_in, grads_in, pieces, rg_out, (hid, gpu), scratch = split_refs(
        refs, 1, peers, peers, peers, peers, 2, 5
    )
    rows, grads, wgu, down, back = scratch
    ff = shares * 128
    width = grads.shape[1]
    for m in range(peers):
        rows[m * CAP : (m + 1) * CAP, :] = rows_in[m][...]
        grads[m * CAP : (m + 1) * CAP, :] = grads_in[m][...]
    for m, piece in enumerate(pieces):
        at = pl.ds(pl.multiple_of(jnp.bitwise_xor(idx[0], m) * 128, 128), 128)
        for t in range(shares):
            wgu[at, t * 128 : (t + 1) * 128] = piece[t, 0:128, :]
            wgu[at, ff + t * 128 : ff + (t + 1) * 128] = piece[t, 128:256, :]
    load_down(idx[0], pieces, down, shares)
    expert = idx[0] * shares + idx[1]

    def body(c, carry):
        at = pl.ds(pl.multiple_of(c * step, step), step)
        gate = gate_column(rows[at, width:], expert)
        pre = jnp.dot(rows[at, :width], wgu[...], preferred_element_type=F32)
        raw = mm(grads[at, :], down[...], 1, 1)
        gate_pre = pre[:, :ff]
        up_pre = pre[:, ff:]
        sig = jax.nn.sigmoid(gate_pre)
        silu = gate_pre * sig
        hidden = (silu * up_pre).astype(BF)
        hid[at, :] = hidden
        gate_grad = jnp.sum(hidden.astype(F32) * raw, axis=-1, keepdims=True)
        hidden_grad = raw * gate
        gp = (hidden_grad * up_pre * sig * (1.0 + gate_pre * (1.0 - sig))).astype(BF)
        up = (hidden_grad * silu).astype(BF)
        both = jnp.concatenate([gp, up], 1)
        gpu[at, :] = both
        back[at, :width] = mm(both, wgu[...], 1, 1).astype(BF)
        lane = lax.broadcasted_iota(jnp.int32, (step, LANES), 1)
        back[at, width:] = jnp.where(lane == expert, gate_grad, 0.0).astype(BF)
        return carry

    lax.fori_loop(0, peers * CAP // step, body, 0)
    for m in range(peers):
        rg_out[m][...] = back[m * CAP : (m + 1) * CAP, :]


def expert_rest_kernel(peers, shares, step, *refs):
    (idx,), rows_in, grads_in, pieces, (hid, gpu), y_out, grad_out, scratch = split_refs(
        refs, 1, peers, peers, peers, 2, peers, shares, 3
    )
    rows, scaled, down = scratch
    width = rows.shape[1]
    expert = idx[0] * shares + idx[1]
    load_down(idx[0], pieces, down, shares)
    for m in range(peers):
        part = slice(m * CAP, (m + 1) * CAP)
        gate = gate_column(rows_in[m][:, width:], expert)
        rows[part, :] = rows_in[m][:, :width]
        scaled[part, :] = (grads_in[m][...].astype(F32) * gate).astype(BF)

    for m in range(peers):
        gate = gate_column(rows_in[m][:, width:], expert)
        out = jnp.dot(hid[m * CAP : (m + 1) * CAP, :], down[...], preferred_element_type=F32)
        y_out[m][...] = (out * gate).astype(BF)

    def body(c, carry):
        at = pl.ds(pl.multiple_of(c * step, step), step)
        both = mm(rows[:, at], gpu[...], 0, 0).astype(BF)
        down_g = mm(hid[...], scaled[:, at], 0, 0).astype(BF)
        for s in range(step // 128):
            for t in range(shares):
                m = jnp.bitwise_xor(c * (step // 128) + s, idx[0])
                r = slice(s * 128, (s + 1) * 128)
                out = grad_out[t]
                out[m, 0:128, :] = both[r, t * 128 : (t + 1) * 128]
                out[m, 128:256, :] = both[r, (shares + t) * 128 : (shares + t + 1) * 128]
                out[m, 256:384, :] = down_g[t * 128 : (t + 1) * 128, r]
        return carry

    lax.fori_loop(0, width // step, body, 0)


def combine_kernel(peers, shares, *refs):
    (idx, gt), slots, parts, (all_slots, total) = split_refs(refs, 2, peers, shares, 2)
    for m in range(peers):
        all_slots[m * CAP : (m + 1) * CAP, :] = slots[m][...]
    total[...] = jnp.dot(gt[...], all_slots[...], preferred_element_type=F32)
    scatter_rows(total, parts, idx[1])


def hi_lo_rows(row, count):
    hi = row.astype(BF)
    lo = (row - hi.astype(F32)).astype(BF)
    place = lax.broadcasted_iota(jnp.int32, (count, row.shape[1]), 0)
    out = jnp.where(place == 0, hi.astype(F32), jnp.where(place == 1, lo.astype(F32), 0.0))
    return out.astype(BF)


def moe_back_kernel(shares, *refs):
    backs, (router, res, gains, misc, out_grad, rgrad, msg) = split_refs(refs, shares, 7)
    own, width = res.shape
    total = backs[0][...].astype(F32)
    for back in backs[1:]:
        total = total + back[...].astype(F32)
    upstream = total[:, :width]
    prob_grad = total[:, width:]
    probs = router[...]
    logit = (probs * (prob_grad - jnp.sum(probs * prob_grad, axis=-1, keepdims=True))).astype(BF)
    upstream = upstream + mm(logit, misc[...], 1, 1)
    normed, inverse = norm_parts(res[...])
    gain_grad = jnp.sum(upstream * normed, axis=0, keepdims=True)
    grad = out_grad[...].astype(F32) + norm_backward(upstream, normed, inverse, gains[1:2, :])
    rgrad[...] = grad
    msg[0:own, :width] = grad.astype(BF)
    msg[0:own, width:] = logit
    msg[own:, :width] = hi_lo_rows(gain_grad, msg.shape[0] - own)
    msg[own:, width:] = jnp.zeros((msg.shape[0] - own, LANES), BF)


def attn_bwd_kernel(peers, shares, dims, *refs):
    n_q, n_kv = dims
    ins, g_out, msg2, (sums, partial) = split_refs(refs, 13, peers, shares, 2)
    idx, msg, wall, qkv, att, logs, cos, sin, seg_c, seg_r, hid, rows2, x = ins
    length, width = x.shape
    own = length // shares
    span = msg.shape[0] // shares
    qk_w = (n_q + n_kv) * HD
    all_w = (n_q + 2 * n_kv) * HD
    o_at = all_w + n_q * HD
    resid = jnp.concatenate([msg[s * span : s * span + own, :width] for s in range(shares)], 0)
    logit = jnp.concatenate([msg[s * span : s * span + own, width:] for s in range(shares)], 0)
    gain_moe = jnp.zeros((1, width), F32)
    for s in range(shares):
        extra = msg[s * span + own : (s + 1) * span, :width].astype(F32)
        gain_moe = gain_moe + jnp.sum(extra, axis=0, keepdims=True)
    att_grad = jnp.dot(resid, wall[:, all_w:o_at], preferred_element_type=F32).astype(BF)
    allowed = allowed_pairs(seg_c[...], seg_r[...], length)
    group = n_q // n_kv
    lane = lax.broadcasted_iota(jnp.int32, (length, LANES), 1)
    log_all = logs[...]
    q_grads, k_grads, v_grads = [], [], []
    for g in range(n_kv):
        k_g = qkv[:, (n_q + g) * HD : (n_q + g + 1) * HD]
        v_g = qkv[:, qk_w + g * HD : qk_w + (g + 1) * HD]
        k_sum = jnp.zeros((length, HD), F32)
        v_sum = jnp.zeros((length, HD), F32)
        for h in range(g * group, (g + 1) * group):
            cut = slice(h * HD, (h + 1) * HD)
            q_h = qkv[:, cut]
            log_h = jnp.sum(jnp.where(lane == h, log_all, 0.0), axis=-1, keepdims=True)
            scores = mm(q_h, k_g, 1, 1) * score_scale
            probs = jnp.where(allowed, jnp.exp(scores - log_h), 0.0)
            a_h = att_grad[:, cut]
            delta = jnp.sum(
                a_h.astype(F32) * att[:, cut].astype(F32), axis=-1, keepdims=True
            )
            prob_grad = mm(a_h, v_g, 1, 1)
            s_grad = (probs * (prob_grad - delta) * score_scale).astype(BF)
            q_grads.append(jnp.dot(s_grad, k_g, preferred_element_type=F32))
            k_sum = k_sum + mm(s_grad, q_h, 0, 0)
            v_sum = v_sum + mm(probs.astype(BF), a_h, 0, 0)
        k_grads.append(k_sum)
        v_grads.append(v_sum)
    qk_grad = jnp.concatenate(q_grads + k_grads, 1)
    qk_low = rotate_lanes(qk_grad, cos[...], -sin[...]).astype(BF)
    low = jnp.concatenate([qk_low, jnp.concatenate(v_grads, 1).astype(BF)], 1)
    sums[:, :all_w] = mm(hid[...], low, 0, 0)
    sums[:, all_w:o_at] = mm(resid, att[...], 0, 0)
    place = lax.broadcasted_iota(jnp.int32, (LANES, width), 0)
    gain_hi = gain_moe.astype(BF).astype(F32)
    rows = jnp.where(place == 32, gain_hi, jnp.where(place == 33, gain_moe - gain_hi, 0.0))
    sums[:, o_at:] = mm(rows2[:, :width], logit, 0, 0) + jnp.transpose(rows)
    depth = g_out[0].shape[0]
    for m in range(peers):
        at = pl.multiple_of(jnp.bitwise_xor(idx[0], m) * depth, depth)
        g_out[m][...] = sums[pl.ds(at, depth), :].astype(BF)
    partial[...] = mm(low, wall[:, :all_w], 1, 1)
    normed, _ = norm_parts(x[...].astype(F32))
    extra = hi_lo_rows(jnp.sum(partial[...] * normed, axis=0, keepdims=True), span - own)
    scatter_rows(partial, [out.at[0:own, :] for out in msg2], idx[1])
    for out in msg2:
        out[own:, :] = extra


def input_grad_kernel(shares, *refs):
    msgs, (x, gains, rgrad, out, gain_out) = split_refs(refs, shares, 5)
    own, width = x.shape
    upstream = jnp.zeros((own, width), F32)
    gain_sum = jnp.zeros((1, width), F32)
    for msg in msgs:
        upstream = upstream + msg[0:own, :].astype(F32)
        gain_sum = gain_sum + jnp.sum(msg[own:, :].astype(F32), axis=0, keepdims=True)
    normed, inverse = norm_parts(x[...].astype(F32))
    through = norm_backward(upstream, normed, inverse, gains[0:1, :])
    out[...] = (rgrad[...] + through).astype(BF)
    gain_out[...] = jnp.broadcast_to(gain_sum, gain_out.shape)


def layer_out_kernel(shares, *refs):
    parts, (res, out) = split_refs(refs, shares, 2)
    total = res[...]
    for part in parts:
        total = total + part[...].astype(F32)
    out[...] = total.astype(BF)


def swap(values, axis):
    got = [values[0]]
    for m in range(1, len(values)):
        got.append(lax.ppermute(values[m], axis, [(i, i ^ m) for i in range(len(values))]))
    return got


def per_device(
    rep,
    layer_input,
    seq_ids,
    expert_ids,
    out_grad,
    gain_attn,
    gain_moe,
    w_query,
    w_key,
    w_value,
    w_output,
    w_router,
    w_gate,
    w_up,
    w_down,
):
    peers = lax.axis_size("dp")
    shares = lax.axis_size("tensor")
    own, width = layer_input.shape
    experts = w_gate.shape[0]
    length = seq_ids.shape[1]
    depth = width // peers
    q_w, kv_w = w_query.shape[1], w_key.shape[1]
    dims = (q_w // HD, kv_w // HD)
    all_w = q_w + 2 * kv_w
    pack_w = all_w + q_w + LANES
    slots = peers * CAP
    wide = width + LANES
    idx = jnp.stack([lax.axis_index("dp"), lax.axis_index("tensor")]).astype(jnp.int32)

    local = w_router.shape[0]
    pack = jnp.concatenate(
        [
            w_query,
            w_key,
            w_value,
            w_output.T,
            w_router,
            gain_attn[:, None],
            gain_moe[:, None],
            jnp.zeros((local, LANES - experts - 2), BF),
        ],
        axis=1,
    )
    if rep > 1:
        pack = lax.all_gather(pack, "rep", axis=0, tiled=True)
    packs = swap([pack] * peers, "dp")

    if rep > 1:
        w_gate = lax.all_gather(w_gate, "rep", axis=1, tiled=True)
        w_up = lax.all_gather(w_up, "rep", axis=1, tiled=True)
        w_down = lax.all_gather(w_down, "rep", axis=2, tiled=True)
    weight_parts = call(
        functools.partial(weight_pack_kernel, peers, shares),
        [((peers, 384, LANES), BF)] * shares,
        smem=1,
    )(idx, w_gate, w_up, w_down)
    weight_parts = swap(weight_parts, "tensor")

    x_all = lax.all_gather(layer_input, "tensor", axis=0, tiled=True)
    segment = seq_ids[0]
    before = jnp.sum((segment[None, :] < segment[:, None]).astype(jnp.int32), axis=1)
    position = (jnp.arange(length, dtype=jnp.int32) - before).astype(F32)
    lane = jnp.arange(LANES, dtype=jnp.int32) % HD
    half = HD // 2
    frequency = rope_base ** (-2.0 * (lane % half).astype(F32) / HD)
    angles = position[:, None] * frequency[None, :]
    cosine = jnp.cos(angles)
    sine = jnp.where(lane[None, :] < half, -1.0, 1.0) * jnp.sin(angles)
    seg_c = segment[:, None]
    seg_r = segment[None, :]

    grads_all = lax.all_gather(out_grad, "tensor", axis=0, tiled=True)
    gt, *grad_slots = call(
        functools.partial(onehot_kernel, peers, shares),
        [((length, slots), BF)] + [((CAP, width), BF)] * peers,
        smem=1,
    )(idx, expert_ids, grads_all)
    x_all, grad_slots = lax.optimization_barrier((x_all, grad_slots))
    grad_in = swap(grad_slots, "dp")

    *parts, wall, gains, qkv, att, logs, hid = call(
        functools.partial(attn_fwd_kernel, peers, shares, dims),
        [((own, width), BF)] * shares
        + [
            ((width, pack_w), BF),
            ((8, width), F32),
            ((length, all_w), BF),
            ((length, q_w), BF),
            ((length, LANES), F32),
            ((length, width), BF),
        ],
        scratch=[((length, width), F32)],
        smem=1,
    )(idx, x_all, *packs, cosine, sine, seg_c, seg_r)

    misc = wall[:, all_w + q_w :]
    parts = swap(parts, "tensor")
    weight_parts = call(
        functools.partial(regroup_kernel, peers, shares), [((shares, 384, LANES), BF)] * peers
    )(*weight_parts)
    pieces = swap(weight_parts, "dp")
    res, router, msg = call(
        functools.partial(post_attn_kernel, experts, shares),
        [((own, width), F32), ((own, LANES), F32), ((own, wide), BF)],
    )(*parts, layer_input, gains, misc)
    rows_all = lax.all_gather(msg, "tensor", axis=0, tiled=True)
    row_slots = call(
        functools.partial(dispatch_kernel, peers), [((CAP, wide), BF)] * peers
    )(gt, rows_all)
    rows_in = swap(row_slots, "dp")

    ff = w_gate.shape[2] * shares
    *row_back, hidden, gate_up = call(
        functools.partial(expert_main_kernel, peers, shares, 256),
        [((CAP, wide), BF)] * peers + [((slots, ff), BF), ((slots, 2 * ff), BF)],
        scratch=[
            ((slots, wide), BF),
            ((slots, width), BF),
            ((width, 2 * ff), BF),
            ((ff, width), BF),
            ((slots, wide), BF),
        ],
        smem=1,
    )(idx, *rows_in, *grad_in, *pieces)
    back_in = swap(row_back, "dp")
    rest = call(
        functools.partial(expert_rest_kernel, peers, shares, 256),
        [((CAP, width), BF)] * peers + [((peers, 384, LANES), BF)] * shares,
        scratch=[((slots, width), BF), ((slots, width), BF), ((ff, width), BF)],
        smem=1,
    )(idx, *rows_in, *grad_in, *pieces, hidden, gate_up)

    y_slots, grad_parts = rest[:peers], rest[peers:]
    grad_parts = swap(grad_parts, "tensor")
    back_in, y_slots = lax.optimization_barrier((back_in, y_slots))
    y_in = swap(y_slots, "dp")
    row_grad = call(
        functools.partial(combine_kernel, peers, shares),
        [((own, wide), BF)] * shares,
        scratch=[((slots, wide), BF), ((length, wide), F32)],
        smem=1,
    )(idx, gt, *back_in)
    row_grad = swap(row_grad, "tensor")
    grad_parts = call(
        functools.partial(regroup_kernel, peers, shares), [((shares, 384, LANES), BF)] * peers
    )(*grad_parts)
    grad_parts = swap(grad_parts, "dp")
    rgrad, msg = call(
        functools.partial(moe_back_kernel, shares), [((own, width), F32), ((own + 16, wide), BF)]
    )(*row_grad, router, res, gains, misc, out_grad)
    msg_all = lax.all_gather(msg, "tensor", axis=0, tiled=True)

    outs = call(
        functools.partial(attn_bwd_kernel, peers, shares, dims),
        [((depth, pack_w), BF)] * peers + [((own + 16, width), BF)] * shares,
        scratch=[((width, pack_w), F32), ((length, width), F32)],
        smem=1,
    )(idx, msg_all, wall, qkv, att, logs, cosine, sine, seg_c, seg_r, hid, rows_all, x_all)
    w_grads, msg2 = outs[:peers], outs[peers:]
    w_sums = swap(w_grads, "dp")
    total = sum(piece.astype(F32) for piece in w_sums)
    if rep > 1:
        total = lax.psum_scatter(total, "rep", scatter_dimension=0, tiled=True)

    msg2 = swap(msg2, "tensor")
    input_grad, gain_rows = call(
        functools.partial(input_grad_kernel, shares), [((own, width), BF), ((8, width), F32)]
    )(*msg2, layer_input, gains, rgrad)
    gain_cut = gain_rows[:1].reshape(peers, depth)
    gain_cut = lax.all_to_all(gain_cut, "dp", split_axis=0, concat_axis=0, tiled=True)
    gain_attn_grad = jnp.sum(gain_cut, axis=0)
    if rep > 1:
        gain_attn_grad = lax.psum_scatter(gain_attn_grad, "rep", scatter_dimension=0, tiled=True)

    mixed = call(
        functools.partial(combine_kernel, peers, shares),
        [((own, width), BF)] * shares,
        scratch=[((slots, width), BF), ((length, width), F32)],
        smem=1,
    )(idx, gt, *y_in)
    mixed = swap(mixed, "tensor")
    (layer_output,) = call(
        functools.partial(layer_out_kernel, shares), [((own, width), BF)]
    )(*mixed, res)

    gate_grad, up_grad, down_grad = call(
        functools.partial(weight_grad_kernel, peers, shares),
        [((experts, 128, LANES), F32)] * 3,
        smem=1,
    )(idx, *grad_parts)
    if rep > 1:
        gate_grad = lax.psum_scatter(gate_grad, "rep", scatter_dimension=1, tiled=True)
        up_grad = lax.psum_scatter(up_grad, "rep", scatter_dimension=1, tiled=True)
        down_grad = lax.psum_scatter(down_grad, "rep", scatter_dimension=2, tiled=True)
    o_at = all_w + q_w
    return (
        layer_output,
        input_grad,
        gain_attn_grad,
        total[:, o_at + experts] + total[:, o_at + experts + 1],
        total[:, :q_w],
        total[:, q_w : q_w + kv_w],
        total[:, q_w + kv_w : all_w],
        total[:, all_w:o_at].T,
        total[:, o_at : o_at + experts],
        gate_grad,
        up_grad,
        down_grad,
    )


def solution(mesh):
    shares = mesh.shape["tensor"]
    peers = 32 // shares
    rep = mesh.shape["dp"] // peers
    dp = "dp"
    if rep > 1:
        devices = np.asarray(mesh.devices).reshape(peers, rep, shares)
        mesh = jax.sharding.Mesh(devices, ("dp", "rep", "tensor"))
        dp = ("dp", "rep")
    both = ("dp", "tensor") if rep == 1 else ("dp", "rep", "tensor")
    in_specs = (
        P(both, None),
        P(dp, None),
        P(dp, None),
        P(both, None),
        P(dp),
        P(dp),
        P(dp, "tensor"),
        P(dp, "tensor"),
        P(dp, "tensor"),
        P("tensor", dp),
        P(dp, None),
        P(None, dp, "tensor"),
        P(None, dp, "tensor"),
        P(None, "tensor", dp),
    )
    out_specs = (
        P(both, None),
        P(both, None),
        P(dp),
        P(dp),
        P(dp, "tensor"),
        P(dp, "tensor"),
        P(dp, "tensor"),
        P("tensor", dp),
        P(dp, None),
        P(None, dp, "tensor"),
        P(None, dp, "tensor"),
        P(None, "tensor", dp),
    )

    def body(*args):
        return per_device(rep, *args)

    return jax.shard_map(
        body, mesh=mesh, in_specs=in_specs, out_specs=out_specs, check_vma=False
    )
```

```python
import functools

import jax
import jax.numpy as jnp
import numpy as np
from jax import lax
from jax.experimental import pallas as pl
from jax.experimental.pallas import tpu as pltpu
from jax.sharding import PartitionSpec as P


HD = 64
CAP = 128
LANES = 128

eps_norm = 1e-05
score_scale = 0.125
rope_base = 10000.0

TOKEN_BITS = (4, 2, 1)
QKV_BITS = (4, 2, 1)
REST_BITS = (1, 4, 2)

BF = jnp.bfloat16
F32 = jnp.float32


def mm(a, b, ca, cb):
    return lax.dot_general(a, b, (((ca,), (cb,)), ((), ())), preferred_element_type=F32)


def call(kernel, outs, scratch=(), smem=0):
    def run(*args):
        in_specs = [pl.BlockSpec(memory_space=pltpu.SMEM)] * smem
        in_specs += [pl.BlockSpec(memory_space=pltpu.VMEM)] * (len(args) - smem)
        return pl.pallas_call(
            kernel,
            out_shape=[jax.ShapeDtypeStruct(s, d) for s, d in outs],
            in_specs=in_specs,
            out_specs=[pl.BlockSpec(memory_space=pltpu.VMEM)] * len(outs),
            scratch_shapes=[pltpu.VMEM(s, d) for s, d in scratch],
        )(*args)

    return run


def split_refs(refs, *counts):
    parts, at = [], 0
    for count in counts:
        parts.append(refs[at : at + count])
        at += count
    return parts


def norm_parts(values):
    inverse = lax.rsqrt(jnp.mean(values * values, axis=-1, keepdims=True) + eps_norm)
    return values * inverse, inverse


def norm_backward(upstream, normed, inverse, gain):
    scaled = upstream * gain
    return inverse * (scaled - normed * jnp.mean(scaled * normed, axis=-1, keepdims=True))


def rotate_lanes(values, cosine, signed_sine):
    width = values.shape[1]
    half = HD // 2
    lane = lax.broadcasted_iota(jnp.int32, values.shape, 1)
    ahead = pltpu.roll(values, width - half, 1)
    behind = pltpu.roll(values, half, 1)
    partner = jnp.where(lane % HD < half, ahead, behind)
    copies = width // LANES
    return values * jnp.concatenate([cosine] * copies, 1) + partner * jnp.concatenate(
        [signed_sine] * copies, 1
    )


def allowed_pairs(seg_col, seg_row, length):
    rows = lax.broadcasted_iota(jnp.int32, (length, length), 0)
    cols = lax.broadcasted_iota(jnp.int32, (length, length), 1)
    return (seg_col == seg_row) & (rows >= cols)


def visit_order(bits):
    order = [0]
    for bit in bits:
        order = order + [m ^ bit for m in order]
    return order


def scatter_rows(whole, parts, own):
    span = parts[0].shape[0]
    for s, out in enumerate(parts):
        at = pl.multiple_of(jnp.bitwise_xor(own, s) * span, span)
        out[...] = whole[pl.ds(at, span), :].astype(out.dtype)


def attn_fwd_kernel(peers, shares, dims, *refs):
    n_q, n_kv = dims
    (idx,), (x,), w_in, (cos, sin, seg_c, seg_r), parts, outs, (part,) = split_refs(
        refs, 1, 1, 4, 4, shares, 6, 1
    )
    wall, gains, qkv, att, log_out, hid = outs
    rows = wall.shape[0] // peers
    column = 0
    for pair, bits in ((w_in[:2], QKV_BITS), (w_in[2:], REST_BITS)):
        cols = slice(column, column + pair[0].shape[1])
        column = column + pair[0].shape[1]
        for k, m in enumerate(visit_order(bits)):
            at = pl.multiple_of(jnp.bitwise_xor(idx[0], m) * rows, rows)
            got = pair[k // (peers // 2)]
            k = k % (peers // 2)
            wall[pl.ds(at, rows), cols] = got[k * rows : (k + 1) * rows, :]
    qk_w = (n_q + n_kv) * HD
    all_w = (n_q + 2 * n_kv) * HD
    o_at = all_w + n_q * HD
    misc_t = jnp.transpose(wall[:, o_at : o_at + LANES].astype(F32))
    gains[...] = misc_t[32:40, :]
    gain = misc_t[32:33, :]
    normed, _ = norm_parts(x[...].astype(F32))
    hidden = (normed * gain).astype(BF)
    hid[...] = hidden
    pre = jnp.dot(hidden, wall[:, :all_w], preferred_element_type=F32)
    qk = rotate_lanes(pre[:, :qk_w], cos[...], sin[...]).astype(BF)
    value = pre[:, qk_w:].astype(BF)
    qkv[...] = jnp.concatenate([qk, value], 1)
    length = x.shape[0]
    allowed = allowed_pairs(seg_c[...], seg_r[...], length)
    group = n_q // n_kv
    outs_h, logs = [], []
    for h in range(n_q):
        g = h // group
        q_h = qk[:, h * HD : (h + 1) * HD]
        k_g = qk[:, (n_q + g) * HD : (n_q + g + 1) * HD]
        v_g = value[:, g * HD : (g + 1) * HD]
        scores = mm(q_h, k_g, 1, 1) * score_scale
        total = jnp.sum(jnp.where(allowed, jnp.exp(scores), 0.0), axis=-1, keepdims=True)
        log_total = jnp.log(total)
        probs = jnp.where(allowed, jnp.exp(scores - log_total), 0.0).astype(BF)
        outs_h.append(jnp.dot(probs, v_g, preferred_element_type=F32).astype(BF))
        logs.append(log_total)
    flat = jnp.concatenate(outs_h, 1)
    att[...] = flat
    lane = lax.broadcasted_iota(jnp.int32, (length, LANES), 1)
    packed = jnp.zeros((length, LANES), F32)
    for h in range(n_q):
        packed = jnp.where(lane == h, logs[h], packed)
    log_out[...] = packed
    part[...] = mm(flat, wall[:, all_w:o_at], 1, 1)
    scatter_rows(part, parts, idx[1])


def post_attn_kernel(experts, shares, *refs):
    parts, (x, ids, gains, misc, res, router, msg) = split_refs(refs, shares, 7)
    width = x.shape[1]
    total = x[...].astype(F32)
    for part in parts:
        total = total + part[...].astype(F32)
    res[...] = total
    normed, _ = norm_parts(total)
    h2 = (normed * gains[1:2, :]).astype(BF)
    logits = jnp.dot(h2, misc[...], preferred_element_type=F32)
    lane = lax.broadcasted_iota(jnp.int32, logits.shape, 1)
    exponent = jnp.where(lane < experts, jnp.exp(logits), 0.0)
    probs = exponent / jnp.sum(exponent, axis=-1, keepdims=True)
    router[...] = probs
    msg[:, :width] = h2
    ids_v = ids[...]
    member = jnp.zeros(probs.shape, F32)
    for k in range(ids_v.shape[1]):
        member = member + jnp.where(ids_v[:, k : k + 1] + experts == lane, 1.0, 0.0)
    msg[:, width:] = (probs + member).astype(BF)


def gate_column(router_cols, expert):
    values = router_cols.astype(F32)
    lane = lax.broadcasted_iota(jnp.int32, values.shape, 1)
    return jnp.sum(jnp.where(lane == expert, values, 0.0), axis=-1, keepdims=True)


def load_down(own, pieces, down, shares):
    for m, piece in enumerate(pieces):
        at = pl.ds(pl.multiple_of(jnp.bitwise_xor(own, m) * 128, 128), 128)
        for t in range(shares):
            down[t * 128 : (t + 1) * 128, at] = piece[t, 256:384, :]


def weight_pack_kernel(peers, shares, idx, gate, up, down, *outs):
    for s in range(shares):
        for m in range(peers):
            e = jnp.bitwise_xor(idx[0], m) * shares + jnp.bitwise_xor(idx[1], s)
            for k, w in enumerate((gate, up, down)):
                outs[s][m, k * 128 : (k + 1) * 128, :] = w[e]


def regroup_kernel(peers, shares, *refs):
    ins, outs = split_refs(refs, shares, peers)
    for m in range(peers):
        for s in range(shares):
            outs[m][s] = ins[s][m]


def weight_grad_kernel(peers, shares, idx, *refs):
    ins, outs = split_refs(refs, peers, 3)
    for m in range(peers):
        for s in range(shares):
            e = jnp.bitwise_xor(idx[0], m) * shares + jnp.bitwise_xor(idx[1], s)
            for k in range(3):
                outs[k][e] = ins[m][s, k * 128 : (k + 1) * 128, :].astype(F32)


def expert_main_kernel(peers, shares, experts, *refs):
    (idx,), rows_in, grads_in, pieces, back, outs, (wgu, down) = split_refs(
        refs, 1, shares, shares, peers, shares, 7, 2
    )
    rows_out, scaled_out, hid, gpu, hot_out, gate_out, near_out = outs
    ff = shares * 128
    width = grads_in[0].shape[1]
    span = rows_in[0].shape[0] // peers
    block = shares * span
    for m, piece in enumerate(pieces):
        at = pl.ds(pl.multiple_of(jnp.bitwise_xor(idx[0], m) * 128, 128), 128)
        for t in range(shares):
            wgu[at, t * 128 : (t + 1) * 128] = piece[t, 0:128, :]
            wgu[at, ff + t * 128 : ff + (t + 1) * 128] = piece[t, 128:256, :]
    load_down(idx[0], pieces, down, shares)
    for s in range(shares):
        near_out[s * span : (s + 1) * span, :] = rows_in[s][0:span, :width]
    expert = idx[0] * shares + idx[1]
    r = lax.broadcasted_iota(jnp.int32, (block, block), 0)
    c = lax.broadcasted_iota(jnp.int32, (block, block), 1)
    lower = jnp.where(r > c, 1.0, 0.0).astype(BF)
    slot = lax.broadcasted_iota(jnp.int32, (block, CAP), 1)
    lane = lax.broadcasted_iota(jnp.int32, (2 * CAP, LANES), 1)

    def body(step, carry):
        slots, grads = [], []
        for half in range(2):
            k = step * 2 + half
            at = pl.ds(pl.multiple_of(k * span, span), span)
            tokens = jnp.concatenate([ref[at, :] for ref in rows_in], 0)
            cotangents = jnp.concatenate([ref[at, :] for ref in grads_in], 0)
            tail = tokens[:, width:].astype(F32)
            member = jnp.where(slot == expert + experts, tail, 0.0)
            rank = jnp.dot(lower, member.astype(BF), preferred_element_type=F32)
            rank = jnp.sum(jnp.where(slot == expert + experts, rank, 0.0), -1, keepdims=True)
            is_member = jnp.sum(member, axis=-1, keepdims=True) > 0.0
            place = jnp.where(is_member, rank, -1.0)
            hot = jnp.where(place == slot.astype(F32), 1.0, 0.0).astype(BF)
            hot_out[pl.ds(pl.multiple_of(k * block, block), block), :] = hot
            slots.append(mm(hot, tokens, 0, 0).astype(BF))
            grads.append(mm(hot, cotangents, 0, 0).astype(BF))
        rows = jnp.concatenate(slots, 0)
        grad_rows = jnp.concatenate(grads, 0)
        at = pl.ds(pl.multiple_of(step * 2 * CAP, 2 * CAP), 2 * CAP)
        gate = gate_column(rows[:, width:], expert)
        rows = rows[:, :width]
        rows_out[at, :] = rows
        scaled_out[at, :] = (grad_rows.astype(F32) * gate).astype(BF)
        gate_out[at, :] = jnp.broadcast_to(gate, (2 * CAP, LANES))
        pre = jnp.dot(rows, wgu[...], preferred_element_type=F32)
        raw = mm(grad_rows, down[...], 1, 1)
        gate_pre = pre[:, :ff]
        up_pre = pre[:, ff:]
        sig = jax.nn.sigmoid(gate_pre)
        silu = gate_pre * sig
        hidden = (silu * up_pre).astype(BF)
        hid[at, :] = hidden
        gate_grad = jnp.sum(hidden.astype(F32) * raw, axis=-1, keepdims=True)
        hidden_grad = raw * gate
        gp = (hidden_grad * up_pre * sig * (1.0 + gate_pre * (1.0 - sig))).astype(BF)
        up = (hidden_grad * silu).astype(BF)
        both = jnp.concatenate([gp, up], 1)
        gpu[at, :] = both
        row_grad = mm(both, wgu[...], 1, 1).astype(BF)
        tail_grad = jnp.where(lane == expert, gate_grad, 0.0).astype(BF)
        for half in range(2):
            k = step * 2 + half
            hot = hot_out[pl.ds(pl.multiple_of(k * block, block), block), :]
            cut = slice(half * CAP, (half + 1) * CAP)
            to = pl.ds(pl.multiple_of(k * span, span), span)
            spread = jnp.dot(hot, row_grad[cut, :], preferred_element_type=F32).astype(BF)
            tail = jnp.dot(hot, tail_grad[cut, :], preferred_element_type=F32).astype(BF)
            for s in range(shares):
                back[s][to, :width] = spread[s * span : (s + 1) * span, :]
                back[s][to, width:] = tail[s * span : (s + 1) * span, :]
        return carry

    lax.fori_loop(0, peers // 2, body, 0)


def expert_rest_kernel(peers, shares, step, *refs):
    (idx,), pieces, ins, y_out, grad_out, (down,) = split_refs(
        refs, 1, peers, 6, shares, shares, 1
    )
    rows, scaled, hid, gpu, hot_in, gate_in = ins
    width = rows.shape[1]
    span = y_out[0].shape[0] // peers
    block = shares * span
    load_down(idx[0], pieces, down, shares)

    def out_rows(k, carry):
        at = pl.ds(pl.multiple_of(k * CAP, CAP), CAP)
        out = jnp.dot(hid[at, :], down[...], preferred_element_type=F32)
        out = (out * gate_in[at, 0:1]).astype(BF)
        hot = hot_in[pl.ds(pl.multiple_of(k * block, block), block), :]
        spread = jnp.dot(hot, out, preferred_element_type=F32).astype(BF)
        to = pl.ds(pl.multiple_of(k * span, span), span)
        for s in range(shares):
            y_out[s][to, :] = spread[s * span : (s + 1) * span, :]
        return carry

    lax.fori_loop(0, peers, out_rows, 0)

    def body(c, carry):
        at = pl.ds(pl.multiple_of(c * step, step), step)
        both = mm(rows[:, at], gpu[...], 0, 0).astype(BF)
        down_g = mm(hid[...], scaled[:, at], 0, 0).astype(BF)
        for s in range(step // 128):
            for t in range(shares):
                m = jnp.bitwise_xor(c * (step // 128) + s, idx[0])
                r = slice(s * 128, (s + 1) * 128)
                out = grad_out[t]
                out[m, 0:128, :] = both[r, t * 128 : (t + 1) * 128]
                out[m, 128:256, :] = both[r, (shares + t) * 128 : (shares + t + 1) * 128]
                out[m, 256:384, :] = down_g[t * 128 : (t + 1) * 128, r]
        return carry

    lax.fori_loop(0, width // step, body, 0)


def hi_lo_rows(row, count):
    hi = row.astype(BF)
    lo = (row - hi.astype(F32)).astype(BF)
    place = lax.broadcasted_iota(jnp.int32, (count, row.shape[1]), 0)
    out = jnp.where(place == 0, hi.astype(F32), jnp.where(place == 1, lo.astype(F32), 0.0))
    return out.astype(BF)


def moe_back_kernel(*refs):
    backs, (router, res, gains, misc, out_grad, rgrad, msg) = split_refs(refs, 2, 7)
    own, width = res.shape
    total = backs[0][...].astype(F32) + backs[1][...].astype(F32)
    upstream = total[:, :width]
    prob_grad = total[:, width:]
    probs = router[...]
    logit = (probs * (prob_grad - jnp.sum(probs * prob_grad, axis=-1, keepdims=True))).astype(BF)
    upstream = upstream + mm(logit, misc[...], 1, 1)
    normed, inverse = norm_parts(res[...])
    gain_grad = jnp.sum(upstream * normed, axis=0, keepdims=True)
    grad = out_grad[...].astype(F32) + norm_backward(upstream, normed, inverse, gains[1:2, :])
    rgrad[...] = grad
    msg[0:own, :width] = grad.astype(BF)
    msg[0:own, width:] = logit
    msg[own:, :width] = hi_lo_rows(gain_grad, msg.shape[0] - own)
    msg[own:, width:] = jnp.zeros((msg.shape[0] - own, LANES), BF)


def attn_bwd_kernel(peers, shares, dims, *refs):
    n_q, n_kv = dims
    ins, g_out, msg2, (sums, partial) = split_refs(refs, 13, 2, shares, 2)
    idx, msg, wall, qkv, att, logs, cos, sin, seg_c, seg_r, hid, rows2, x = ins
    length, width = x.shape
    own = length // shares
    span = msg.shape[0] // shares
    qk_w = (n_q + n_kv) * HD
    all_w = (n_q + 2 * n_kv) * HD
    o_at = all_w + n_q * HD
    resid = jnp.concatenate([msg[s * span : s * span + own, :width] for s in range(shares)], 0)
    starts = [jnp.bitwise_xor(idx[1], s) * span for s in range(shares)]
    logit = jnp.concatenate(
        [msg[pl.ds(pl.multiple_of(at, 16), own), width:] for at in starts], 0
    )
    gain_moe = jnp.zeros((1, width), F32)
    for s in range(shares):
        extra = msg[s * span + own : (s + 1) * span, :width].astype(F32)
        gain_moe = gain_moe + jnp.sum(extra, axis=0, keepdims=True)
    att_grad = jnp.dot(resid, wall[:, all_w:o_at], preferred_element_type=F32).astype(BF)
    allowed = allowed_pairs(seg_c[...], seg_r[...], length)
    group = n_q // n_kv
    lane = lax.broadcasted_iota(jnp.int32, (length, LANES), 1)
    log_all = logs[...]
    q_grads, k_grads, v_grads = [], [], []
    for g in range(n_kv):
        k_g = qkv[:, (n_q + g) * HD : (n_q + g + 1) * HD]
        v_g = qkv[:, qk_w + g * HD : qk_w + (g + 1) * HD]
        k_sum = jnp.zeros((length, HD), F32)
        v_sum = jnp.zeros((length, HD), F32)
        for h in range(g * group, (g + 1) * group):
            cut = slice(h * HD, (h + 1) * HD)
            q_h = qkv[:, cut]
            log_h = jnp.sum(jnp.where(lane == h, log_all, 0.0), axis=-1, keepdims=True)
            scores = mm(q_h, k_g, 1, 1) * score_scale
            probs = jnp.where(allowed, jnp.exp(scores - log_h), 0.0)
            a_h = att_grad[:, cut]
            delta = jnp.sum(
                a_h.astype(F32) * att[:, cut].astype(F32), axis=-1, keepdims=True
            )
            prob_grad = mm(a_h, v_g, 1, 1)
            s_grad = (probs * (prob_grad - delta) * score_scale).astype(BF)
            q_grads.append(jnp.dot(s_grad, k_g, preferred_element_type=F32))
            k_sum = k_sum + mm(s_grad, q_h, 0, 0)
            v_sum = v_sum + mm(probs.astype(BF), a_h, 0, 0)
        k_grads.append(k_sum)
        v_grads.append(v_sum)
    qk_grad = jnp.concatenate(q_grads + k_grads, 1)
    qk_low = rotate_lanes(qk_grad, cos[...], -sin[...]).astype(BF)
    low = jnp.concatenate([qk_low, jnp.concatenate(v_grads, 1).astype(BF)], 1)
    sums[:, :all_w] = mm(hid[...], low, 0, 0)
    sums[:, all_w:o_at] = mm(resid, att[...], 0, 0)
    place = lax.broadcasted_iota(jnp.int32, (LANES, width), 0)
    gain_hi = gain_moe.astype(BF).astype(F32)
    rows = jnp.where(place == 32, gain_hi, jnp.where(place == 33, gain_moe - gain_hi, 0.0))
    sums[:, o_at:] = mm(rows2[...], logit, 0, 0) + jnp.transpose(rows)
    depth = width // peers
    for k, m in enumerate(visit_order(TOKEN_BITS)):
        at = pl.multiple_of(jnp.bitwise_xor(idx[0], m) * depth, depth)
        out = g_out[k // (peers // 2)]
        k = k % (peers // 2)
        out[k * depth : (k + 1) * depth, :] = sums[pl.ds(at, depth), :].astype(BF)
    partial[...] = mm(low, wall[:, :all_w], 1, 1)
    normed, _ = norm_parts(x[...].astype(F32))
    extra = hi_lo_rows(jnp.sum(partial[...] * normed, axis=0, keepdims=True), span - own)
    scatter_rows(partial, [out.at[0:own, :] for out in msg2], idx[1])
    for out in msg2:
        out[own:, :] = extra


def input_grad_kernel(shares, *refs):
    msgs, (x, gains, rgrad, out, gain_out) = split_refs(refs, shares, 5)
    own, width = x.shape
    upstream = jnp.zeros((own, width), F32)
    gain_sum = jnp.zeros((1, width), F32)
    for msg in msgs:
        upstream = upstream + msg[0:own, :].astype(F32)
        gain_sum = gain_sum + jnp.sum(msg[own:, :].astype(F32), axis=0, keepdims=True)
    normed, inverse = norm_parts(x[...].astype(F32))
    through = norm_backward(upstream, normed, inverse, gains[0:1, :])
    out[...] = (rgrad[...] + through).astype(BF)
    gain_out[...] = jnp.broadcast_to(gain_sum, gain_out.shape)


def layer_out_kernel(first, second, res, out):
    total = first[...].astype(F32) + second[...].astype(F32)
    out[...] = (res[...] + total).astype(BF)


def swap(values, axis):
    got = [values[0]]
    for m in range(1, len(values)):
        got.append(lax.ppermute(values[m], axis, [(i, i ^ m) for i in range(len(values))]))
    return got


def permute(value, axis, bit):
    count = lax.axis_size(axis)
    return lax.ppermute(value, axis, [(i, i ^ bit) for i in range(count)])


def gather_dp(value, bits):
    for at, bit in enumerate(bits):
        got = permute(value, "dp", bit)
        if at == len(bits) - 1:
            return value, got
        value = jnp.concatenate([value, got], 0)


def gather_all(value):
    first = jnp.concatenate(gather_dp(value, TOKEN_BITS), 0)
    across = permute(first, "tensor", 2)
    beside = permute(first, "tensor", 1)
    return first, beside, across, permute(across, "tensor", 1)


def reduce_dp(even, odd, other=None):
    got = permute(odd, "dp", 1)
    even = even + got if other is None else even + other + got
    half = even.shape[0] // 2
    even = even[:half] + permute(even[half:], "dp", 2)
    half = half // 2
    return even[:half], permute(even[half:], "dp", 4)


def reduce_all(parts):
    half = parts[0].shape[0] // 2
    own = permute(parts[1], "tensor", 1)
    far = permute(parts[3], "tensor", 1)
    far_odd = permute(parts[2][half:] + far[half:], "tensor", 2)
    far_even = permute(parts[2][:half] + far[:half], "tensor", 2)
    odd = parts[0][half:] + own[half:] + far_odd
    return reduce_dp(parts[0][:half] + own[:half], odd, far_even)


def per_device(
    rep,
    layer_input,
    seq_ids,
    expert_ids,
    out_grad,
    gain_attn,
    gain_moe,
    w_query,
    w_key,
    w_value,
    w_output,
    w_router,
    w_gate,
    w_up,
    w_down,
):
    peers = lax.axis_size("dp")
    shares = lax.axis_size("tensor")
    own, width = layer_input.shape
    experts = w_gate.shape[0]
    length = seq_ids.shape[1]
    depth = width // peers
    q_w, kv_w = w_query.shape[1], w_key.shape[1]
    dims = (q_w // HD, kv_w // HD)
    all_w = q_w + 2 * kv_w
    pack_w = all_w + q_w + LANES
    slots = peers * CAP
    wide = width + LANES
    idx = jnp.stack([lax.axis_index("dp"), lax.axis_index("tensor")]).astype(jnp.int32)

    local = w_router.shape[0]
    pack_a = jnp.concatenate([w_query, w_key, w_value], axis=1)
    tail = [w_router, gain_attn[:, None], gain_moe[:, None]]
    tail.append(jnp.zeros((local, LANES - experts - 2), BF))
    pack_b = jnp.concatenate([w_output.T] + tail, axis=1)
    if rep > 1:
        pack_a = lax.all_gather(pack_a, "rep", axis=0, tiled=True)
        pack_b = lax.all_gather(pack_b, "rep", axis=0, tiled=True)
    packs = gather_dp(pack_a, QKV_BITS) + gather_dp(pack_b, REST_BITS)

    x_all = lax.all_gather(layer_input, "tensor", axis=0, tiled=True)

    if rep > 1:
        w_gate = lax.all_gather(w_gate, "rep", axis=1, tiled=True)
        w_up = lax.all_gather(w_up, "rep", axis=1, tiled=True)
        w_down = lax.all_gather(w_down, "rep", axis=2, tiled=True)
    weight_parts = call(
        functools.partial(weight_pack_kernel, peers, shares),
        [((peers, 384, LANES), BF)] * shares,
        smem=1,
    )(idx, w_gate, w_up, w_down)
    weight_parts, x_all = lax.optimization_barrier((weight_parts, x_all))
    weight_parts = swap(weight_parts, "tensor")
    grads_in = gather_all(out_grad)

    segment = seq_ids[0]
    before = jnp.sum((segment[None, :] < segment[:, None]).astype(jnp.int32), axis=1)
    position = (jnp.arange(length, dtype=jnp.int32) - before).astype(F32)
    lane = jnp.arange(LANES, dtype=jnp.int32) % HD
    half = HD // 2
    frequency = rope_base ** (-2.0 * (lane % half).astype(F32) / HD)
    angles = position[:, None] * frequency[None, :]
    cosine = jnp.cos(angles)
    sine = jnp.where(lane[None, :] < half, -1.0, 1.0) * jnp.sin(angles)
    seg_c = segment[:, None]
    seg_r = segment[None, :]

    *parts, wall, gains, qkv, att, logs, hid = call(
        functools.partial(attn_fwd_kernel, peers, shares, dims),
        [((own, width), BF)] * shares
        + [
            ((width, pack_w), BF),
            ((8, width), F32),
            ((length, all_w), BF),
            ((length, q_w), BF),
            ((length, LANES), F32),
            ((length, width), BF),
        ],
        scratch=[((length, width), F32)],
        smem=1,
    )(idx, x_all, *packs, cosine, sine, seg_c, seg_r)

    misc = wall[:, all_w + q_w :]
    ids_own = lax.dynamic_slice_in_dim(expert_ids, lax.axis_index("tensor") * own, own, 0)
    parts = swap(parts, "tensor")
    weight_parts = call(
        functools.partial(regroup_kernel, peers, shares), [((shares, 384, LANES), BF)] * peers
    )(*weight_parts)
    pieces = swap(weight_parts, "dp")
    res, router, msg = call(
        functools.partial(post_attn_kernel, experts, shares),
        [((own, width), F32), ((own, LANES), F32), ((own, wide), BF)],
    )(*parts, layer_input, ids_own, gains, misc)
    rows_in = gather_all(msg)

    ff = w_gate.shape[2] * shares
    outs = call(
        functools.partial(expert_main_kernel, peers, shares, experts),
        [((peers * own, wide), BF)] * shares
        + [
            ((slots, width), BF),
            ((slots, width), BF),
            ((slots, ff), BF),
            ((slots, 2 * ff), BF),
            ((peers * length, CAP), BF),
            ((slots, LANES), F32),
            ((length, width), BF),
        ],
        scratch=[((width, 2 * ff), BF), ((ff, width), BF)],
        smem=1,
    )(idx, *rows_in, *grads_in, *pieces)
    row_back, saved, rows_near = outs[:shares], outs[shares:-1], outs[-1]
    back = reduce_all(row_back)
    rest = call(
        functools.partial(expert_rest_kernel, peers, shares, 256),
        [((peers * own, width), BF)] * shares + [((peers, 384, LANES), BF)] * shares,
        scratch=[((ff, width), BF)],
        smem=1,
    )(idx, *pieces, *saved)
    y_parts, grad_parts = rest[:shares], rest[shares:]
    grad_parts = swap(grad_parts, "tensor")
    mixed = reduce_all(y_parts)
    grad_parts = call(
        functools.partial(regroup_kernel, peers, shares), [((shares, 384, LANES), BF)] * peers
    )(*grad_parts)
    grad_parts = swap(grad_parts, "dp")
    rgrad, msg = call(
        moe_back_kernel, [((own, width), F32), ((own + 16, wide), BF)]
    )(*back, router, res, gains, misc, out_grad)
    msg_all = lax.all_gather(msg, "tensor", axis=0, tiled=True)

    outs = call(
        functools.partial(attn_bwd_kernel, peers, shares, dims),
        [((width // 2, pack_w), BF)] * 2 + [((own + 16, width), BF)] * shares,
        scratch=[((width, pack_w), F32), ((length, width), F32)],
        smem=1,
    )(idx, msg_all, wall, qkv, att, logs, cosine, sine, seg_c, seg_r, hid, rows_near, x_all)
    msg2 = outs[2:]
    w_sums = reduce_dp(outs[0], outs[1])
    total = w_sums[0].astype(F32) + w_sums[1].astype(F32)
    if rep > 1:
        total = lax.psum_scatter(total, "rep", scatter_dimension=0, tiled=True)

    msg2 = swap(msg2, "tensor")
    input_grad, gain_rows = call(
        functools.partial(input_grad_kernel, shares), [((own, width), BF), ((8, width), F32)]
    )(*msg2, layer_input, gains, rgrad)
    gain_cut = gain_rows[:1].reshape(peers, depth)
    gain_cut = lax.all_to_all(gain_cut, "dp", split_axis=0, concat_axis=0, tiled=True)
    gain_attn_grad = jnp.sum(gain_cut, axis=0)
    if rep > 1:
        gain_attn_grad = lax.psum_scatter(gain_attn_grad, "rep", scatter_dimension=0, tiled=True)

    (layer_output,) = call(layer_out_kernel, [((own, width), BF)])(*mixed, res)

    gate_grad, up_grad, down_grad = call(
        functools.partial(weight_grad_kernel, peers, shares),
        [((experts, 128, LANES), F32)] * 3,
        smem=1,
    )(idx, *grad_parts)
    if rep > 1:
        gate_grad = lax.psum_scatter(gate_grad, "rep", scatter_dimension=1, tiled=True)
        up_grad = lax.psum_scatter(up_grad, "rep", scatter_dimension=1, tiled=True)
        down_grad = lax.psum_scatter(down_grad, "rep", scatter_dimension=2, tiled=True)
    o_at = all_w + q_w
    return (
        layer_output,
        input_grad,
        gain_attn_grad,
        total[:, o_at + experts] + total[:, o_at + experts + 1],
        total[:, :q_w],
        total[:, q_w : q_w + kv_w],
        total[:, q_w + kv_w : all_w],
        total[:, all_w:o_at].T,
        total[:, o_at : o_at + experts],
        gate_grad,
        up_grad,
        down_grad,
    )


def solution(mesh):
    shares = mesh.shape["tensor"]
    peers = 32 // shares
    rep = mesh.shape["dp"] // peers
    dp = "dp"
    if rep > 1:
        devices = np.asarray(mesh.devices).reshape(peers, rep, shares)
        mesh = jax.sharding.Mesh(devices, ("dp", "rep", "tensor"))
        dp = ("dp", "rep")
    both = ("dp", "tensor") if rep == 1 else ("dp", "rep", "tensor")
    in_specs = (
        P(both, None),
        P(dp, None),
        P(dp, None),
        P(both, None),
        P(dp),
        P(dp),
        P(dp, "tensor"),
        P(dp, "tensor"),
        P(dp, "tensor"),
        P("tensor", dp),
        P(dp, None),
        P(None, dp, "tensor"),
        P(None, dp, "tensor"),
        P(None, "tensor", dp),
    )
    out_specs = (
        P(both, None),
        P(both, None),
        P(dp),
        P(dp),
        P(dp, "tensor"),
        P(dp, "tensor"),
        P(dp, "tensor"),
        P("tensor", dp),
        P(dp, None),
        P(None, dp, "tensor"),
        P(None, dp, "tensor"),
        P(None, "tensor", dp),
    )

    def body(*args):
        return per_device(rep, *args)

    return jax.shard_map(
        body, mesh=mesh, in_specs=in_specs, out_specs=out_specs, check_vma=False
    )
```

```python
import functools

import jax
import jax.numpy as jnp
import numpy as np
from jax import lax
from jax.experimental import pallas as pl
from jax.experimental.pallas import tpu as pltpu
from jax.sharding import PartitionSpec as P


HD = 64
CAP = 128
LANES = 128

eps_norm = 1e-05
score_scale = 0.125
rope_base = 10000.0

TOKEN_BITS = (4, 2, 1)
QKV_BITS = (4, 2, 1)
REST_BITS = (1, 4, 2)

BF = jnp.bfloat16
F32 = jnp.float32


def mm(a, b, ca, cb):
    return lax.dot_general(a, b, (((ca,), (cb,)), ((), ())), preferred_element_type=F32)


def call(kernel, outs, scratch=(), smem=0):
    def run(*args):
        in_specs = [pl.BlockSpec(memory_space=pltpu.SMEM)] * smem
        in_specs += [pl.BlockSpec(memory_space=pltpu.VMEM)] * (len(args) - smem)
        return pl.pallas_call(
            kernel,
            out_shape=[jax.ShapeDtypeStruct(s, d) for s, d in outs],
            in_specs=in_specs,
            out_specs=[pl.BlockSpec(memory_space=pltpu.VMEM)] * len(outs),
            scratch_shapes=[pltpu.VMEM(s, d) for s, d in scratch],
        )(*args)

    return run


def split_refs(refs, *counts):
    parts, at = [], 0
    for count in counts:
        parts.append(refs[at : at + count])
        at += count
    return parts


def norm_parts(values):
    inverse = lax.rsqrt(jnp.mean(values * values, axis=-1, keepdims=True) + eps_norm)
    return values * inverse, inverse


def norm_backward(upstream, normed, inverse, gain):
    scaled = upstream * gain
    return inverse * (scaled - normed * jnp.mean(scaled * normed, axis=-1, keepdims=True))


def rotate_lanes(values, cosine, signed_sine):
    width = values.shape[1]
    half = HD // 2
    lane = lax.broadcasted_iota(jnp.int32, values.shape, 1)
    ahead = pltpu.roll(values, width - half, 1)
    behind = pltpu.roll(values, half, 1)
    partner = jnp.where(lane % HD < half, ahead, behind)
    copies = width // LANES
    return values * jnp.concatenate([cosine] * copies, 1) + partner * jnp.concatenate(
        [signed_sine] * copies, 1
    )


def allowed_pairs(seg_col, seg_row, length):
    rows = lax.broadcasted_iota(jnp.int32, (length, length), 0)
    cols = lax.broadcasted_iota(jnp.int32, (length, length), 1)
    return (seg_col == seg_row) & (rows >= cols)


def visit_order(bits):
    order = [0]
    for bit in bits:
        order = order + [m ^ bit for m in order]
    return order


def scatter_rows(whole, parts, own):
    span = parts[0].shape[0]
    for s, out in enumerate(parts):
        at = pl.multiple_of(jnp.bitwise_xor(own, s) * span, span)
        out[...] = whole[pl.ds(at, span), :].astype(out.dtype)


def attn_fwd_kernel(peers, shares, dims, *refs):
    n_q, n_kv = dims
    (idx,), x_in, w_in, (cos, sin, seg_c, seg_r), parts, outs, (part,) = split_refs(
        refs, 1, shares, 4, 4, shares, 8, 1
    )
    wall, gains, qkv, att, log_out, hid, x, misc = outs
    own = x_in[0].shape[0]
    for s, got in enumerate(x_in):
        at = pl.multiple_of(jnp.bitwise_xor(idx[1], s) * own, own)
        x[pl.ds(at, own), :] = got[...]
    rows = wall.shape[0] // peers
    column = 0
    for pair, bits in ((w_in[:2], QKV_BITS), (w_in[2:], REST_BITS)):
        cols = slice(column, column + pair[0].shape[1])
        column = column + pair[0].shape[1]
        for k, m in enumerate(visit_order(bits)):
            at = pl.multiple_of(jnp.bitwise_xor(idx[0], m) * rows, rows)
            got = pair[k // (peers // 2)]
            k = k % (peers // 2)
            wall[pl.ds(at, rows), cols] = got[k * rows : (k + 1) * rows, :]
    qk_w = (n_q + n_kv) * HD
    all_w = (n_q + 2 * n_kv) * HD
    o_at = all_w + n_q * HD
    misc[...] = wall[:, o_at : o_at + LANES]
    misc_t = jnp.transpose(wall[:, o_at : o_at + LANES].astype(F32))
    gains[...] = misc_t[32:40, :]
    gain = misc_t[32:33, :]
    normed, _ = norm_parts(x[...].astype(F32))
    hidden = (normed * gain).astype(BF)
    hid[...] = hidden
    pre = jnp.dot(hidden, wall[:, :all_w], preferred_element_type=F32)
    qk = rotate_lanes(pre[:, :qk_w], cos[...], sin[...]).astype(BF)
    value = pre[:, qk_w:].astype(BF)
    qkv[...] = jnp.concatenate([qk, value], 1)
    length = x.shape[0]
    allowed = allowed_pairs(seg_c[...], seg_r[...], length)
    group = n_q // n_kv
    outs_h, logs = [], []
    for h in range(n_q):
        g = h // group
        q_h = qk[:, h * HD : (h + 1) * HD]
        k_g = qk[:, (n_q + g) * HD : (n_q + g + 1) * HD]
        v_g = value[:, g * HD : (g + 1) * HD]
        scores = mm(q_h, k_g, 1, 1) * score_scale
        total = jnp.sum(jnp.where(allowed, jnp.exp(scores), 0.0), axis=-1, keepdims=True)
        log_total = jnp.log(total)
        probs = jnp.where(allowed, jnp.exp(scores - log_total), 0.0).astype(BF)
        outs_h.append(jnp.dot(probs, v_g, preferred_element_type=F32).astype(BF))
        logs.append(log_total)
    flat = jnp.concatenate(outs_h, 1)
    att[...] = flat
    lane = lax.broadcasted_iota(jnp.int32, (length, LANES), 1)
    packed = jnp.zeros((length, LANES), F32)
    for h in range(n_q):
        packed = jnp.where(lane == h, logs[h], packed)
    log_out[...] = packed
    part[...] = mm(flat, wall[:, all_w:o_at], 1, 1)
    scatter_rows(part, parts, idx[1])


def post_attn_kernel(experts, shares, *refs):
    parts, (x, ids, gains, misc, res, router, msg) = split_refs(refs, shares, 7)
    width = x.shape[1]
    total = x[...].astype(F32)
    for part in parts:
        total = total + part[...].astype(F32)
    res[...] = total
    normed, _ = norm_parts(total)
    h2 = (normed * gains[1:2, :]).astype(BF)
    logits = jnp.dot(h2, misc[...], preferred_element_type=F32)
    lane = lax.broadcasted_iota(jnp.int32, logits.shape, 1)
    exponent = jnp.where(lane < experts, jnp.exp(logits), 0.0)
    probs = exponent / jnp.sum(exponent, axis=-1, keepdims=True)
    router[...] = probs
    msg[:, :width] = h2
    ids_v = ids[...]
    member = jnp.zeros(probs.shape, F32)
    for k in range(ids_v.shape[1]):
        member = member + jnp.where(ids_v[:, k : k + 1] + experts == lane, 1.0, 0.0)
    msg[:, width:] = (probs + member).astype(BF)


def gate_column(router_cols, expert):
    values = router_cols.astype(F32)
    lane = lax.broadcasted_iota(jnp.int32, values.shape, 1)
    return jnp.sum(jnp.where(lane == expert, values, 0.0), axis=-1, keepdims=True)


def load_down(own, pieces, down, shares):
    for m, piece in enumerate(pieces):
        at = pl.ds(pl.multiple_of(jnp.bitwise_xor(own, m) * 128, 128), 128)
        for t in range(shares):
            down[t * 128 : (t + 1) * 128, at] = piece[t, 256:384, :]


def weight_pack_kernel(peers, shares, idx, gate, up, down, *outs):
    for s in range(shares):
        for m in range(peers):
            e = jnp.bitwise_xor(idx[0], m) * shares + jnp.bitwise_xor(idx[1], s)
            for k, w in enumerate((gate, up, down)):
                outs[s][m, k * 128 : (k + 1) * 128, :] = w[e]


def regroup_kernel(peers, shares, *refs):
    ins, outs = split_refs(refs, shares, peers)
    for m in range(peers):
        for s in range(shares):
            outs[m][s] = ins[s][m]


def weight_grad_kernel(peers, shares, idx, *refs):
    ins, outs = split_refs(refs, peers, 3)
    for m in range(peers):
        for s in range(shares):
            e = jnp.bitwise_xor(idx[0], m) * shares + jnp.bitwise_xor(idx[1], s)
            for k in range(3):
                outs[k][e] = ins[m][s, k * 128 : (k + 1) * 128, :].astype(F32)


def expert_main_kernel(peers, shares, experts, *refs):
    (idx,), rows_in, grads_in, pieces, back, outs, (wgu, down) = split_refs(
        refs, 1, shares, shares, peers, shares, 7, 2
    )
    rows_out, scaled_out, hid, gpu, hot_out, gate_out, near_out = outs
    ff = shares * 128
    width = grads_in[0].shape[1]
    span = rows_in[0].shape[0] // peers
    block = shares * span
    for m, piece in enumerate(pieces):
        at = pl.ds(pl.multiple_of(jnp.bitwise_xor(idx[0], m) * 128, 128), 128)
        for t in range(shares):
            wgu[at, t * 128 : (t + 1) * 128] = piece[t, 0:128, :]
            wgu[at, ff + t * 128 : ff + (t + 1) * 128] = piece[t, 128:256, :]
    load_down(idx[0], pieces, down, shares)
    for s in range(shares):
        near_out[s * span : (s + 1) * span, :] = rows_in[s][0:span, :width]
    expert = idx[0] * shares + idx[1]
    r = lax.broadcasted_iota(jnp.int32, (block, block), 0)
    c = lax.broadcasted_iota(jnp.int32, (block, block), 1)
    lower = jnp.where(r > c, 1.0, 0.0).astype(BF)
    slot = lax.broadcasted_iota(jnp.int32, (block, CAP), 1)
    lane = lax.broadcasted_iota(jnp.int32, (2 * CAP, LANES), 1)

    def body(step, carry):
        slots, grads = [], []
        for half in range(2):
            k = step * 2 + half
            at = pl.ds(pl.multiple_of(k * span, span), span)
            tokens = jnp.concatenate([ref[at, :] for ref in rows_in], 0)
            cotangents = jnp.concatenate([ref[at, :] for ref in grads_in], 0)
            tail = tokens[:, width:].astype(F32)
            member = jnp.where(slot == expert + experts, tail, 0.0)
            rank = jnp.dot(lower, member.astype(BF), preferred_element_type=F32)
            rank = jnp.sum(jnp.where(slot == expert + experts, rank, 0.0), -1, keepdims=True)
            is_member = jnp.sum(member, axis=-1, keepdims=True) > 0.0
            place = jnp.where(is_member, rank, -1.0)
            hot = jnp.where(place == slot.astype(F32), 1.0, 0.0).astype(BF)
            hot_out[pl.ds(pl.multiple_of(k * block, block), block), :] = hot
            slots.append(mm(hot, tokens, 0, 0).astype(BF))
            grads.append(mm(hot, cotangents, 0, 0).astype(BF))
        rows = jnp.concatenate(slots, 0)
        grad_rows = jnp.concatenate(grads, 0)
        at = pl.ds(pl.multiple_of(step * 2 * CAP, 2 * CAP), 2 * CAP)
        gate = gate_column(rows[:, width:], expert)
        rows = rows[:, :width]
        rows_out[at, :] = rows
        scaled_out[at, :] = (grad_rows.astype(F32) * gate).astype(BF)
        gate_out[at, :] = jnp.broadcast_to(gate, (2 * CAP, LANES))
        pre = jnp.dot(rows, wgu[...], preferred_element_type=F32)
        raw = mm(grad_rows, down[...], 1, 1)
        gate_pre = pre[:, :ff]
        up_pre = pre[:, ff:]
        sig = jax.nn.sigmoid(gate_pre)
        silu = gate_pre * sig
        hidden = (silu * up_pre).astype(BF)
        hid[at, :] = hidden
        gate_grad = jnp.sum(hidden.astype(F32) * raw, axis=-1, keepdims=True)
        hidden_grad = raw * gate
        gp = (hidden_grad * up_pre * sig * (1.0 + gate_pre * (1.0 - sig))).astype(BF)
        up = (hidden_grad * silu).astype(BF)
        both = jnp.concatenate([gp, up], 1)
        gpu[at, :] = both
        row_grad = mm(both, wgu[...], 1, 1).astype(BF)
        tail_grad = jnp.where(lane == expert, gate_grad, 0.0).astype(BF)
        for half in range(2):
            k = step * 2 + half
            hot = hot_out[pl.ds(pl.multiple_of(k * block, block), block), :]
            cut = slice(half * CAP, (half + 1) * CAP)
            to = pl.ds(pl.multiple_of(k * span, span), span)
            spread = jnp.dot(hot, row_grad[cut, :], preferred_element_type=F32).astype(BF)
            tail = jnp.dot(hot, tail_grad[cut, :], preferred_element_type=F32).astype(BF)
            for s in range(shares):
                back[s][to, :width] = spread[s * span : (s + 1) * span, :]
                back[s][to, width:] = tail[s * span : (s + 1) * span, :]
        return carry

    lax.fori_loop(0, peers // 2, body, 0)


def expert_rest_kernel(peers, shares, step, *refs):
    (idx,), pieces, ins, y_out, grad_out, (down,) = split_refs(
        refs, 1, peers, 6, shares, shares, 1
    )
    rows, scaled, hid, gpu, hot_in, gate_in = ins
    width = rows.shape[1]
    span = y_out[0].shape[0] // peers
    block = shares * span
    load_down(idx[0], pieces, down, shares)

    def out_rows(k, carry):
        at = pl.ds(pl.multiple_of(k * CAP, CAP), CAP)
        out = jnp.dot(hid[at, :], down[...], preferred_element_type=F32)
        out = (out * gate_in[at, 0:1]).astype(BF)
        hot = hot_in[pl.ds(pl.multiple_of(k * block, block), block), :]
        spread = jnp.dot(hot, out, preferred_element_type=F32).astype(BF)
        to = pl.ds(pl.multiple_of(k * span, span), span)
        for s in range(shares):
            y_out[s][to, :] = spread[s * span : (s + 1) * span, :]
        return carry

    lax.fori_loop(0, peers, out_rows, 0)

    def body(c, carry):
        at = pl.ds(pl.multiple_of(c * step, step), step)
        both = mm(rows[:, at], gpu[...], 0, 0).astype(BF)
        down_g = mm(hid[...], scaled[:, at], 0, 0).astype(BF)
        for s in range(step // 128):
            for t in range(shares):
                m = jnp.bitwise_xor(c * (step // 128) + s, idx[0])
                r = slice(s * 128, (s + 1) * 128)
                out = grad_out[t]
                out[m, 0:128, :] = both[r, t * 128 : (t + 1) * 128]
                out[m, 128:256, :] = both[r, (shares + t) * 128 : (shares + t + 1) * 128]
                out[m, 256:384, :] = down_g[t * 128 : (t + 1) * 128, r]
        return carry

    lax.fori_loop(0, width // step, body, 0)


def hi_lo_rows(row, count):
    hi = row.astype(BF)
    lo = (row - hi.astype(F32)).astype(BF)
    place = lax.broadcasted_iota(jnp.int32, (count, row.shape[1]), 0)
    out = jnp.where(place == 0, hi.astype(F32), jnp.where(place == 1, lo.astype(F32), 0.0))
    return out.astype(BF)


def moe_back_kernel(*refs):
    backs, (router, res, gains, misc, out_grad, rgrad, msg) = split_refs(refs, 2, 7)
    own, width = res.shape
    total = backs[0][...].astype(F32) + backs[1][...].astype(F32)
    upstream = total[:, :width]
    prob_grad = total[:, width:]
    probs = router[...]
    logit = (probs * (prob_grad - jnp.sum(probs * prob_grad, axis=-1, keepdims=True))).astype(BF)
    upstream = upstream + mm(logit, misc[...], 1, 1)
    normed, inverse = norm_parts(res[...])
    gain_grad = jnp.sum(upstream * normed, axis=0, keepdims=True)
    grad = out_grad[...].astype(F32) + norm_backward(upstream, normed, inverse, gains[1:2, :])
    rgrad[...] = grad
    msg[0:own, :width] = grad.astype(BF)
    msg[0:own, width:] = logit
    msg[own:, :width] = hi_lo_rows(gain_grad, msg.shape[0] - own)
    msg[own:, width:] = jnp.zeros((msg.shape[0] - own, LANES), BF)


def attn_bwd_kernel(peers, shares, dims, *refs):
    n_q, n_kv = dims
    ins, g_out, msg2, (sums, partial) = split_refs(refs, 13, 2, shares, 2)
    idx, msg, wall, qkv, att, logs, cos, sin, seg_c, seg_r, hid, rows2, x = ins
    length, width = x.shape
    own = length // shares
    span = msg.shape[0] // shares
    qk_w = (n_q + n_kv) * HD
    all_w = (n_q + 2 * n_kv) * HD
    o_at = all_w + n_q * HD
    resid = jnp.concatenate([msg[s * span : s * span + own, :width] for s in range(shares)], 0)
    starts = [jnp.bitwise_xor(idx[1], s) * span for s in range(shares)]
    logit = jnp.concatenate(
        [msg[pl.ds(pl.multiple_of(at, 16), own), width:] for at in starts], 0
    )
    gain_moe = jnp.zeros((1, width), F32)
    for s in range(shares):
        extra = msg[s * span + own : (s + 1) * span, :width].astype(F32)
        gain_moe = gain_moe + jnp.sum(extra, axis=0, keepdims=True)
    att_grad = jnp.dot(resid, wall[:, all_w:o_at], preferred_element_type=F32).astype(BF)
    allowed = allowed_pairs(seg_c[...], seg_r[...], length)
    group = n_q // n_kv
    lane = lax.broadcasted_iota(jnp.int32, (length, LANES), 1)
    log_all = logs[...]
    q_grads, k_grads, v_grads = [], [], []
    for g in range(n_kv):
        k_g = qkv[:, (n_q + g) * HD : (n_q + g + 1) * HD]
        v_g = qkv[:, qk_w + g * HD : qk_w + (g + 1) * HD]
        k_sum = jnp.zeros((length, HD), F32)
        v_sum = jnp.zeros((length, HD), F32)
        for h in range(g * group, (g + 1) * group):
            cut = slice(h * HD, (h + 1) * HD)
            q_h = qkv[:, cut]
            log_h = jnp.sum(jnp.where(lane == h, log_all, 0.0), axis=-1, keepdims=True)
            scores = mm(q_h, k_g, 1, 1) * score_scale
            probs = jnp.where(allowed, jnp.exp(scores - log_h), 0.0)
            a_h = att_grad[:, cut]
            delta = jnp.sum(
                a_h.astype(F32) * att[:, cut].astype(F32), axis=-1, keepdims=True
            )
            prob_grad = mm(a_h, v_g, 1, 1)
            s_grad = (probs * (prob_grad - delta) * score_scale).astype(BF)
            q_grads.append(jnp.dot(s_grad, k_g, preferred_element_type=F32))
            k_sum = k_sum + mm(s_grad, q_h, 0, 0)
            v_sum = v_sum + mm(probs.astype(BF), a_h, 0, 0)
        k_grads.append(k_sum)
        v_grads.append(v_sum)
    qk_grad = jnp.concatenate(q_grads + k_grads, 1)
    qk_low = rotate_lanes(qk_grad, cos[...], -sin[...]).astype(BF)
    low = jnp.concatenate([qk_low, jnp.concatenate(v_grads, 1).astype(BF)], 1)
    sums[:, :all_w] = mm(hid[...], low, 0, 0)
    sums[:, all_w:o_at] = mm(resid, att[...], 0, 0)
    place = lax.broadcasted_iota(jnp.int32, (LANES, width), 0)
    gain_hi = gain_moe.astype(BF).astype(F32)
    rows = jnp.where(place == 32, gain_hi, jnp.where(place == 33, gain_moe - gain_hi, 0.0))
    sums[:, o_at:] = mm(rows2[...], logit, 0, 0) + jnp.transpose(rows)
    depth = width // peers
    for k, m in enumerate(visit_order(TOKEN_BITS)):
        at = pl.multiple_of(jnp.bitwise_xor(idx[0], m) * depth, depth)
        out = g_out[k // (peers // 2)]
        k = k % (peers // 2)
        out[k * depth : (k + 1) * depth, :] = sums[pl.ds(at, depth), :].astype(BF)
    partial[...] = mm(low, wall[:, :all_w], 1, 1)
    normed, _ = norm_parts(x[...].astype(F32))
    extra = hi_lo_rows(jnp.sum(partial[...] * normed, axis=0, keepdims=True), span - own)
    scatter_rows(partial, [out.at[0:own, :] for out in msg2], idx[1])
    for out in msg2:
        out[own:, :] = extra


def input_grad_kernel(shares, *refs):
    msgs, (x, gains, rgrad, out, gain_out) = split_refs(refs, shares, 5)
    own, width = x.shape
    upstream = jnp.zeros((own, width), F32)
    gain_sum = jnp.zeros((1, width), F32)
    for msg in msgs:
        upstream = upstream + msg[0:own, :].astype(F32)
        gain_sum = gain_sum + jnp.sum(msg[own:, :].astype(F32), axis=0, keepdims=True)
    normed, inverse = norm_parts(x[...].astype(F32))
    through = norm_backward(upstream, normed, inverse, gains[0:1, :])
    out[...] = (rgrad[...] + through).astype(BF)
    gain_out[...] = jnp.broadcast_to(gain_sum, gain_out.shape)


def layer_out_kernel(first, second, res, out):
    total = first[...].astype(F32) + second[...].astype(F32)
    out[...] = (res[...] + total).astype(BF)


def swap(values, axis):
    got = [values[0]]
    for m in range(1, len(values)):
        got.append(lax.ppermute(values[m], axis, [(i, i ^ m) for i in range(len(values))]))
    return got


def permute(value, axis, bit):
    count = lax.axis_size(axis)
    return lax.ppermute(value, axis, [(i, i ^ bit) for i in range(count)])


def gather_dp(value, bits):
    for at, bit in enumerate(bits):
        got = permute(value, "dp", bit)
        if at == len(bits) - 1:
            return value, got
        value = jnp.concatenate([value, got], 0)


def gather_all(value):
    first = jnp.concatenate(gather_dp(value, TOKEN_BITS), 0)
    across = permute(first, "tensor", 2)
    beside = permute(first, "tensor", 1)
    return first, beside, across, permute(across, "tensor", 1)


def reduce_dp(even, odd, other=None):
    got = permute(odd, "dp", 1)
    even = even + got if other is None else even + other + got
    half = even.shape[0] // 2
    even = even[:half] + permute(even[half:], "dp", 2)
    half = half // 2
    return even[:half], permute(even[half:], "dp", 4)


def reduce_all(parts):
    half = parts[0].shape[0] // 2
    own = permute(parts[1], "tensor", 1)
    far = permute(parts[3], "tensor", 1)
    far_odd = permute(parts[2][half:] + far[half:], "tensor", 2)
    far_even = permute(parts[2][:half] + far[:half], "tensor", 2)
    odd = parts[0][half:] + own[half:] + far_odd
    return reduce_dp(parts[0][:half] + own[:half], odd, far_even)


def per_device(
    rep,
    layer_input,
    seq_ids,
    expert_ids,
    out_grad,
    gain_attn,
    gain_moe,
    w_query,
    w_key,
    w_value,
    w_output,
    w_router,
    w_gate,
    w_up,
    w_down,
):
    peers = lax.axis_size("dp")
    shares = lax.axis_size("tensor")
    own, width = layer_input.shape
    experts = w_gate.shape[0]
    length = seq_ids.shape[1]
    depth = width // peers
    q_w, kv_w = w_query.shape[1], w_key.shape[1]
    dims = (q_w // HD, kv_w // HD)
    all_w = q_w + 2 * kv_w
    pack_w = all_w + q_w + LANES
    slots = peers * CAP
    wide = width + LANES
    idx = jnp.stack([lax.axis_index("dp"), lax.axis_index("tensor")]).astype(jnp.int32)

    local = w_router.shape[0]
    pack_a = jnp.concatenate([w_query, w_key, w_value], axis=1)
    tail = [w_router, gain_attn[:, None], gain_moe[:, None]]
    tail.append(jnp.zeros((local, LANES - experts - 2), BF))
    pack_b = jnp.concatenate([w_output.T] + tail, axis=1)
    if rep > 1:
        pack_a = lax.all_gather(pack_a, "rep", axis=0, tiled=True)
        pack_b = lax.all_gather(pack_b, "rep", axis=0, tiled=True)
    packs = gather_dp(pack_a, QKV_BITS) + gather_dp(pack_b, REST_BITS)

    x_in = swap([layer_input] * shares, "tensor")

    if rep > 1:
        w_gate = lax.all_gather(w_gate, "rep", axis=1, tiled=True)
        w_up = lax.all_gather(w_up, "rep", axis=1, tiled=True)
        w_down = lax.all_gather(w_down, "rep", axis=2, tiled=True)
    weight_parts = call(
        functools.partial(weight_pack_kernel, peers, shares),
        [((peers, 384, LANES), BF)] * shares,
        smem=1,
    )(idx, w_gate, w_up, w_down)
    weight_parts = swap(weight_parts, "tensor")
    grads_in = gather_all(out_grad)

    segment = seq_ids[0]
    before = jnp.sum((segment[None, :] < segment[:, None]).astype(jnp.int32), axis=1)
    position = (jnp.arange(length, dtype=jnp.int32) - before).astype(F32)
    lane = jnp.arange(LANES, dtype=jnp.int32) % HD
    half = HD // 2
    frequency = rope_base ** (-2.0 * (lane % half).astype(F32) / HD)
    angles = position[:, None] * frequency[None, :]
    cosine = jnp.cos(angles)
    sine = jnp.where(lane[None, :] < half, -1.0, 1.0) * jnp.sin(angles)
    seg_c = segment[:, None]
    seg_r = segment[None, :]

    *parts, wall, gains, qkv, att, logs, hid, x_all, misc = call(
        functools.partial(attn_fwd_kernel, peers, shares, dims),
        [((own, width), BF)] * shares
        + [
            ((width, pack_w), BF),
            ((8, width), F32),
            ((length, all_w), BF),
            ((length, q_w), BF),
            ((length, LANES), F32),
            ((length, width), BF),
            ((length, width), BF),
            ((width, LANES), BF),
        ],
        scratch=[((length, width), F32)],
        smem=1,
    )(idx, *x_in, *packs, cosine, sine, seg_c, seg_r)

    ids_own = lax.dynamic_slice_in_dim(expert_ids, lax.axis_index("tensor") * own, own, 0)
    parts = swap(parts, "tensor")
    weight_parts = call(
        functools.partial(regroup_kernel, peers, shares), [((shares, 384, LANES), BF)] * peers
    )(*weight_parts)
    pieces = swap(weight_parts, "dp")
    res, router, msg = call(
        functools.partial(post_attn_kernel, experts, shares),
        [((own, width), F32), ((own, LANES), F32), ((own, wide), BF)],
    )(*parts, layer_input, ids_own, gains, misc)
    rows_in = gather_all(msg)

    ff = w_gate.shape[2] * shares
    outs = call(
        functools.partial(expert_main_kernel, peers, shares, experts),
        [((peers * own, wide), BF)] * shares
        + [
            ((slots, width), BF),
            ((slots, width), BF),
            ((slots, ff), BF),
            ((slots, 2 * ff), BF),
            ((peers * length, CAP), BF),
            ((slots, LANES), F32),
            ((length, width), BF),
        ],
        scratch=[((width, 2 * ff), BF), ((ff, width), BF)],
        smem=1,
    )(idx, *rows_in, *grads_in, *pieces)
    row_back, saved, rows_near = outs[:shares], outs[shares:-1], outs[-1]
    back = reduce_all(row_back)
    rest = call(
        functools.partial(expert_rest_kernel, peers, shares, 256),
        [((peers * own, width), BF)] * shares + [((peers, 384, LANES), BF)] * shares,
        scratch=[((ff, width), BF)],
        smem=1,
    )(idx, *pieces, *saved)
    y_parts, grad_parts = rest[:shares], rest[shares:]
    grad_parts = swap(grad_parts, "tensor")
    grad_parts = call(
        functools.partial(regroup_kernel, peers, shares), [((shares, 384, LANES), BF)] * peers
    )(*grad_parts)
    grad_parts = swap(grad_parts, "dp")
    rgrad, msg = call(
        moe_back_kernel, [((own, width), F32), ((own + 16, wide), BF)]
    )(*back, router, res, gains, misc, out_grad)
    msg_all = lax.all_gather(msg, "tensor", axis=0, tiled=True)
    y_parts, msg_all = lax.optimization_barrier((y_parts, msg_all))
    mixed = reduce_all(y_parts)

    outs = call(
        functools.partial(attn_bwd_kernel, peers, shares, dims),
        [((width // 2, pack_w), BF)] * 2 + [((own + 16, width), BF)] * shares,
        scratch=[((width, pack_w), F32), ((length, width), F32)],
        smem=1,
    )(idx, msg_all, wall, qkv, att, logs, cosine, sine, seg_c, seg_r, hid, rows_near, x_all)
    msg2 = outs[2:]
    w_sums = reduce_dp(outs[0], outs[1])
    total = w_sums[0].astype(F32) + w_sums[1].astype(F32)
    if rep > 1:
        total = lax.psum_scatter(total, "rep", scatter_dimension=0, tiled=True)

    msg2 = swap(msg2, "tensor")
    input_grad, gain_rows = call(
        functools.partial(input_grad_kernel, shares), [((own, width), BF), ((8, width), F32)]
    )(*msg2, layer_input, gains, rgrad)
    gain_cut = gain_rows[:1].reshape(peers, depth)
    gain_cut = lax.all_to_all(gain_cut, "dp", split_axis=0, concat_axis=0, tiled=True)
    gain_attn_grad = jnp.sum(gain_cut, axis=0)
    if rep > 1:
        gain_attn_grad = lax.psum_scatter(gain_attn_grad, "rep", scatter_dimension=0, tiled=True)

    (layer_output,) = call(layer_out_kernel, [((own, width), BF)])(*mixed, res)

    gate_grad, up_grad, down_grad = call(
        functools.partial(weight_grad_kernel, peers, shares),
        [((experts, 128, LANES), F32)] * 3,
        smem=1,
    )(idx, *grad_parts)
    if rep > 1:
        gate_grad = lax.psum_scatter(gate_grad, "rep", scatter_dimension=1, tiled=True)
        up_grad = lax.psum_scatter(up_grad, "rep", scatter_dimension=1, tiled=True)
        down_grad = lax.psum_scatter(down_grad, "rep", scatter_dimension=2, tiled=True)
    o_at = all_w + q_w
    return (
        layer_output,
        input_grad,
        gain_attn_grad,
        total[:, o_at + experts] + total[:, o_at + experts + 1],
        total[:, :q_w],
        total[:, q_w : q_w + kv_w],
        total[:, q_w + kv_w : all_w],
        total[:, all_w:o_at].T,
        total[:, o_at : o_at + experts],
        gate_grad,
        up_grad,
        down_grad,
    )


def solution(mesh):
    shares = mesh.shape["tensor"]
    peers = 32 // shares
    rep = mesh.shape["dp"] // peers
    dp = "dp"
    if rep > 1:
        devices = np.asarray(mesh.devices).reshape(peers, rep, shares)
        mesh = jax.sharding.Mesh(devices, ("dp", "rep", "tensor"))
        dp = ("dp", "rep")
    both = ("dp", "tensor") if rep == 1 else ("dp", "rep", "tensor")
    in_specs = (
        P(both, None),
        P(dp, None),
        P(dp, None),
        P(both, None),
        P(dp),
        P(dp),
        P(dp, "tensor"),
        P(dp, "tensor"),
        P(dp, "tensor"),
        P("tensor", dp),
        P(dp, None),
        P(None, dp, "tensor"),
        P(None, dp, "tensor"),
        P(None, "tensor", dp),
    )
    out_specs = (
        P(both, None),
        P(both, None),
        P(dp),
        P(dp),
        P(dp, "tensor"),
        P(dp, "tensor"),
        P(dp, "tensor"),
        P("tensor", dp),
        P(dp, None),
        P(None, dp, "tensor"),
        P(None, dp, "tensor"),
        P(None, "tensor", dp),
    )

    def body(*args):
        return per_device(rep, *args)

    return jax.shard_map(
        body, mesh=mesh, in_specs=in_specs, out_specs=out_specs, check_vma=False
    )
```

```python
import functools

import jax
import jax.numpy as jnp
import numpy as np
from jax import lax
from jax.experimental import pallas as pl
from jax.experimental.pallas import tpu as pltpu
from jax.sharding import PartitionSpec as P


HD = 64
CAP = 128
LANES = 128

eps_norm = 1e-05
score_scale = 0.125
rope_base = 10000.0

CHUNKS = ((0, 1, 4, 5), (2, 3, 6, 7))
TOKEN_BITS = (4, 2, 1)
QKV_BITS = (4, 2, 1)
REST_BITS = (1, 4, 2)

BF = jnp.bfloat16
F32 = jnp.float32


def mm(a, b, ca, cb):
    return lax.dot_general(a, b, (((ca,), (cb,)), ((), ())), preferred_element_type=F32)


def call(kernel, outs, scratch=(), smem=0):
    def run(*args):
        in_specs = [pl.BlockSpec(memory_space=pltpu.SMEM)] * smem
        in_specs += [pl.BlockSpec(memory_space=pltpu.VMEM)] * (len(args) - smem)
        return pl.pallas_call(
            kernel,
            out_shape=[jax.ShapeDtypeStruct(s, d) for s, d in outs],
            in_specs=in_specs,
            out_specs=[pl.BlockSpec(memory_space=pltpu.VMEM)] * len(outs),
            scratch_shapes=[pltpu.VMEM(s, d) for s, d in scratch],
        )(*args)

    return run


def split_refs(refs, *counts):
    parts, at = [], 0
    for count in counts:
        parts.append(refs[at : at + count])
        at += count
    return parts


def norm_parts(values):
    inverse = lax.rsqrt(jnp.mean(values * values, axis=-1, keepdims=True) + eps_norm)
    return values * inverse, inverse


def norm_backward(upstream, normed, inverse, gain):
    scaled = upstream * gain
    return inverse * (scaled - normed * jnp.mean(scaled * normed, axis=-1, keepdims=True))


def rotate_lanes(values, cosine, signed_sine):
    width = values.shape[1]
    half = HD // 2
    lane = lax.broadcasted_iota(jnp.int32, values.shape, 1)
    ahead = pltpu.roll(values, width - half, 1)
    behind = pltpu.roll(values, half, 1)
    partner = jnp.where(lane % HD < half, ahead, behind)
    copies = width // LANES
    return values * jnp.concatenate([cosine] * copies, 1) + partner * jnp.concatenate(
        [signed_sine] * copies, 1
    )


def allowed_pairs(seg_col, seg_row, length):
    rows = lax.broadcasted_iota(jnp.int32, (length, length), 0)
    cols = lax.broadcasted_iota(jnp.int32, (length, length), 1)
    return (seg_col == seg_row) & (rows >= cols)


def visit_order(bits):
    order = [0]
    for bit in bits:
        order = order + [m ^ bit for m in order]
    return order


def scatter_rows(whole, parts, own):
    span = parts[0].shape[0]
    for s, out in enumerate(parts):
        at = pl.multiple_of(jnp.bitwise_xor(own, s) * span, span)
        out[...] = whole[pl.ds(at, span), :].astype(out.dtype)


def attn_fwd_kernel(peers, shares, dims, *refs):
    n_q, n_kv = dims
    (idx,), x_in, w_in, (cos, sin, seg_c, seg_r), parts, outs, (part,) = split_refs(
        refs, 1, shares, 4, 4, shares, 8, 1
    )
    wall, gains, qkv, att, log_out, hid, x, misc = outs
    own = x_in[0].shape[0]
    for s, got in enumerate(x_in):
        at = pl.multiple_of(jnp.bitwise_xor(idx[1], s) * own, own)
        x[pl.ds(at, own), :] = got[...]
    rows = wall.shape[0] // peers
    column = 0
    for pair, bits in ((w_in[:2], QKV_BITS), (w_in[2:], REST_BITS)):
        cols = slice(column, column + pair[0].shape[1])
        column = column + pair[0].shape[1]
        for k, m in enumerate(visit_order(bits)):
            at = pl.multiple_of(jnp.bitwise_xor(idx[0], m) * rows, rows)
            got = pair[k // (peers // 2)]
            k = k % (peers // 2)
            wall[pl.ds(at, rows), cols] = got[k * rows : (k + 1) * rows, :]
    qk_w = (n_q + n_kv) * HD
    all_w = (n_q + 2 * n_kv) * HD
    o_at = all_w + n_q * HD
    misc[...] = wall[:, o_at : o_at + LANES]
    misc_t = jnp.transpose(wall[:, o_at : o_at + LANES].astype(F32))
    gains[...] = misc_t[32:40, :]
    gain = misc_t[32:33, :]
    normed, _ = norm_parts(x[...].astype(F32))
    hidden = (normed * gain).astype(BF)
    hid[...] = hidden
    pre = jnp.dot(hidden, wall[:, :all_w], preferred_element_type=F32)
    qk = rotate_lanes(pre[:, :qk_w], cos[...], sin[...]).astype(BF)
    value = pre[:, qk_w:].astype(BF)
    qkv[...] = jnp.concatenate([qk, value], 1)
    length = x.shape[0]
    allowed = allowed_pairs(seg_c[...], seg_r[...], length)
    group = n_q // n_kv
    outs_h, logs = [], []
    for h in range(n_q):
        g = h // group
        q_h = qk[:, h * HD : (h + 1) * HD]
        k_g = qk[:, (n_q + g) * HD : (n_q + g + 1) * HD]
        v_g = value[:, g * HD : (g + 1) * HD]
        scores = mm(q_h, k_g, 1, 1) * score_scale
        total = jnp.sum(jnp.where(allowed, jnp.exp(scores), 0.0), axis=-1, keepdims=True)
        log_total = jnp.log(total)
        probs = jnp.where(allowed, jnp.exp(scores - log_total), 0.0).astype(BF)
        outs_h.append(jnp.dot(probs, v_g, preferred_element_type=F32).astype(BF))
        logs.append(log_total)
    flat = jnp.concatenate(outs_h, 1)
    att[...] = flat
    lane = lax.broadcasted_iota(jnp.int32, (length, LANES), 1)
    packed = jnp.zeros((length, LANES), F32)
    for h in range(n_q):
        packed = jnp.where(lane == h, logs[h], packed)
    log_out[...] = packed
    part[...] = mm(flat, wall[:, all_w:o_at], 1, 1)
    scatter_rows(part, parts, idx[1])


def post_attn_kernel(experts, shares, *refs):
    parts, (x, ids, gains, misc, res, router, msg) = split_refs(refs, shares, 7)
    width = x.shape[1]
    total = x[...].astype(F32)
    for part in parts:
        total = total + part[...].astype(F32)
    res[...] = total
    normed, _ = norm_parts(total)
    h2 = (normed * gains[1:2, :]).astype(BF)
    logits = jnp.dot(h2, misc[...], preferred_element_type=F32)
    lane = lax.broadcasted_iota(jnp.int32, logits.shape, 1)
    exponent = jnp.where(lane < experts, jnp.exp(logits), 0.0)
    probs = exponent / jnp.sum(exponent, axis=-1, keepdims=True)
    router[...] = probs
    msg[:, :width] = h2
    ids_v = ids[...]
    member = jnp.zeros(probs.shape, F32)
    for k in range(ids_v.shape[1]):
        member = member + jnp.where(ids_v[:, k : k + 1] + experts == lane, 1.0, 0.0)
    msg[:, width:] = (probs + member).astype(BF)


def gate_column(router_cols, expert):
    values = router_cols.astype(F32)
    lane = lax.broadcasted_iota(jnp.int32, values.shape, 1)
    return jnp.sum(jnp.where(lane == expert, values, 0.0), axis=-1, keepdims=True)


def load_down(own, pieces, down, shares):
    for m, piece in enumerate(pieces):
        at = pl.ds(pl.multiple_of(jnp.bitwise_xor(own, m) * 128, 128), 128)
        for t in range(shares):
            down[t * 128 : (t + 1) * 128, at] = piece[t, 256:384, :]


def weight_pack_kernel(shares, idx, gate, up, down, *outs):
    for c, chunk in enumerate(CHUNKS):
        for s in range(shares):
            for j, m in enumerate(chunk):
                e = jnp.bitwise_xor(idx[0], m) * shares + jnp.bitwise_xor(idx[1], s)
                for k, w in enumerate((gate, up, down)):
                    outs[c * shares + s][j, k * 128 : (k + 1) * 128, :] = w[e]


def regroup_kernel(shares, *refs):
    ins, outs = split_refs(refs, shares, len(refs) - shares)
    for j, out in enumerate(outs):
        for s in range(shares):
            out[s] = ins[s][j]


def weight_grad_kernel(peers, shares, idx, *refs):
    ins, outs = split_refs(refs, peers, 3)
    for m in range(peers):
        for s in range(shares):
            e = jnp.bitwise_xor(idx[0], m) * shares + jnp.bitwise_xor(idx[1], s)
            for k in range(3):
                outs[k][e] = ins[m][s, k * 128 : (k + 1) * 128, :].astype(F32)


def expert_main_kernel(peers, shares, experts, *refs):
    (idx,), rows_in, grads_in, pieces, back, outs, (wgu, down) = split_refs(
        refs, 1, shares, shares, peers, shares, 7, 2
    )
    rows_out, scaled_out, hid, gpu, hot_out, gate_out, near_out = outs
    ff = shares * 128
    width = grads_in[0].shape[1]
    span = rows_in[0].shape[0] // peers
    block = shares * span
    for m, piece in enumerate(pieces):
        at = pl.ds(pl.multiple_of(jnp.bitwise_xor(idx[0], m) * 128, 128), 128)
        for t in range(shares):
            wgu[at, t * 128 : (t + 1) * 128] = piece[t, 0:128, :]
            wgu[at, ff + t * 128 : ff + (t + 1) * 128] = piece[t, 128:256, :]
    load_down(idx[0], pieces, down, shares)
    for s in range(shares):
        near_out[s * span : (s + 1) * span, :] = rows_in[s][0:span, :width]
    expert = idx[0] * shares + idx[1]
    r = lax.broadcasted_iota(jnp.int32, (block, block), 0)
    c = lax.broadcasted_iota(jnp.int32, (block, block), 1)
    lower = jnp.where(r > c, 1.0, 0.0).astype(BF)
    slot = lax.broadcasted_iota(jnp.int32, (block, CAP), 1)
    lane = lax.broadcasted_iota(jnp.int32, (2 * CAP, LANES), 1)

    def body(step, carry):
        slots, grads = [], []
        for half in range(2):
            k = step * 2 + half
            at = pl.ds(pl.multiple_of(k * span, span), span)
            tokens = jnp.concatenate([ref[at, :] for ref in rows_in], 0)
            cotangents = jnp.concatenate([ref[at, :] for ref in grads_in], 0)
            tail = tokens[:, width:].astype(F32)
            member = jnp.where(slot == expert + experts, tail, 0.0)
            rank = jnp.dot(lower, member.astype(BF), preferred_element_type=F32)
            rank = jnp.sum(jnp.where(slot == expert + experts, rank, 0.0), -1, keepdims=True)
            is_member = jnp.sum(member, axis=-1, keepdims=True) > 0.0
            place = jnp.where(is_member, rank, -1.0)
            hot = jnp.where(place == slot.astype(F32), 1.0, 0.0).astype(BF)
            hot_out[pl.ds(pl.multiple_of(k * block, block), block), :] = hot
            slots.append(mm(hot, tokens, 0, 0).astype(BF))
            grads.append(mm(hot, cotangents, 0, 0).astype(BF))
        rows = jnp.concatenate(slots, 0)
        grad_rows = jnp.concatenate(grads, 0)
        at = pl.ds(pl.multiple_of(step * 2 * CAP, 2 * CAP), 2 * CAP)
        gate = gate_column(rows[:, width:], expert)
        rows = rows[:, :width]
        rows_out[at, :] = rows
        scaled_out[at, :] = (grad_rows.astype(F32) * gate).astype(BF)
        gate_out[at, :] = jnp.broadcast_to(gate, (2 * CAP, LANES))
        pre = jnp.dot(rows, wgu[...], preferred_element_type=F32)
        raw = mm(grad_rows, down[...], 1, 1)
        gate_pre = pre[:, :ff]
        up_pre = pre[:, ff:]
        sig = jax.nn.sigmoid(gate_pre)
        silu = gate_pre * sig
        hidden = (silu * up_pre).astype(BF)
        hid[at, :] = hidden
        gate_grad = jnp.sum(hidden.astype(F32) * raw, axis=-1, keepdims=True)
        hidden_grad = raw * gate
        gp = (hidden_grad * up_pre * sig * (1.0 + gate_pre * (1.0 - sig))).astype(BF)
        up = (hidden_grad * silu).astype(BF)
        both = jnp.concatenate([gp, up], 1)
        gpu[at, :] = both
        row_grad = mm(both, wgu[...], 1, 1).astype(BF)
        tail_grad = jnp.where(lane == expert, gate_grad, 0.0).astype(BF)
        for half in range(2):
            k = step * 2 + half
            hot = hot_out[pl.ds(pl.multiple_of(k * block, block), block), :]
            cut = slice(half * CAP, (half + 1) * CAP)
            to = pl.ds(pl.multiple_of(k * span, span), span)
            spread = jnp.dot(hot, row_grad[cut, :], preferred_element_type=F32).astype(BF)
            tail = jnp.dot(hot, tail_grad[cut, :], preferred_element_type=F32).astype(BF)
            for s in range(shares):
                back[s][to, :width] = spread[s * span : (s + 1) * span, :]
                back[s][to, width:] = tail[s * span : (s + 1) * span, :]
        return carry

    lax.fori_loop(0, peers // 2, body, 0)


def expert_rest_kernel(peers, shares, step, *refs):
    (idx,), pieces, ins, y_out, grad_out, (down,) = split_refs(
        refs, 1, peers, 6, shares, len(CHUNKS) * shares, 1
    )
    rows, scaled, hid, gpu, hot_in, gate_in = ins
    span = y_out[0].shape[0] // peers
    block = shares * span
    load_down(idx[0], pieces, down, shares)

    def out_rows(k, carry):
        at = pl.ds(pl.multiple_of(k * CAP, CAP), CAP)
        out = jnp.dot(hid[at, :], down[...], preferred_element_type=F32)
        out = (out * gate_in[at, 0:1]).astype(BF)
        hot = hot_in[pl.ds(pl.multiple_of(k * block, block), block), :]
        spread = jnp.dot(hot, out, preferred_element_type=F32).astype(BF)
        to = pl.ds(pl.multiple_of(k * span, span), span)
        for s in range(shares):
            y_out[s][to, :] = spread[s * span : (s + 1) * span, :]
        return carry

    lax.fori_loop(0, peers, out_rows, 0)

    for c in range(len(CHUNKS)):
        outs = grad_out[c * shares : (c + 1) * shares]

        def body(pair, carry):
            q = jnp.bitwise_xor(pair * 2 + c, idx[0] // 2)
            at = pl.ds(pl.multiple_of(q * step, step), step)
            both = mm(rows[:, at], gpu[...], 0, 0).astype(BF)
            down_g = mm(hid[...], scaled[:, at], 0, 0).astype(BF)
            for s in range(2):
                j = pair * 2 + jnp.bitwise_xor(idx[0] % 2, s)
                r = slice(s * 128, (s + 1) * 128)
                for t in range(shares):
                    out = outs[t]
                    out[j, 0:128, :] = both[r, t * 128 : (t + 1) * 128]
                    out[j, 128:256, :] = both[r, (shares + t) * 128 : (shares + t + 1) * 128]
                    out[j, 256:384, :] = down_g[t * 128 : (t + 1) * 128, r]
            return carry

        lax.fori_loop(0, 2, body, 0)


def hi_lo_rows(row, count):
    hi = row.astype(BF)
    lo = (row - hi.astype(F32)).astype(BF)
    place = lax.broadcasted_iota(jnp.int32, (count, row.shape[1]), 0)
    out = jnp.where(place == 0, hi.astype(F32), jnp.where(place == 1, lo.astype(F32), 0.0))
    return out.astype(BF)


def moe_back_kernel(*refs):
    backs, (router, res, gains, misc, out_grad, rgrad, msg) = split_refs(refs, 2, 7)
    own, width = res.shape
    total = backs[0][...].astype(F32) + backs[1][...].astype(F32)
    upstream = total[:, :width]
    prob_grad = total[:, width:]
    probs = router[...]
    logit = (probs * (prob_grad - jnp.sum(probs * prob_grad, axis=-1, keepdims=True))).astype(BF)
    upstream = upstream + mm(logit, misc[...], 1, 1)
    normed, inverse = norm_parts(res[...])
    gain_grad = jnp.sum(upstream * normed, axis=0, keepdims=True)
    grad = out_grad[...].astype(F32) + norm_backward(upstream, normed, inverse, gains[1:2, :])
    rgrad[...] = grad
    msg[0:own, :width] = grad.astype(BF)
    msg[0:own, width:] = logit
    msg[own:, :width] = hi_lo_rows(gain_grad, msg.shape[0] - own)
    msg[own:, width:] = jnp.zeros((msg.shape[0] - own, LANES), BF)


def attn_bwd_kernel(peers, shares, dims, *refs):
    n_q, n_kv = dims
    (idx,), msgs, ins, g_out, msg2, (sums, partial, resid) = split_refs(
        refs, 1, shares, 11, 2, shares, 3
    )
    wall, qkv, att, logs, cos, sin, seg_c, seg_r, hid, rows2, x = ins
    length, width = x.shape
    own = length // shares
    span = msgs[0].shape[0]
    qk_w = (n_q + n_kv) * HD
    all_w = (n_q + 2 * n_kv) * HD
    o_at = all_w + n_q * HD
    for s, msg in enumerate(msgs):
        at = pl.multiple_of(jnp.bitwise_xor(idx[1], s) * own, own)
        resid[pl.ds(at, own), :] = msg[0:own, :width]
    logit = jnp.concatenate([msg[0:own, width:] for msg in msgs], 0)
    gain_moe = jnp.zeros((1, width), F32)
    for msg in msgs:
        extra = msg[own:, :width].astype(F32)
        gain_moe = gain_moe + jnp.sum(extra, axis=0, keepdims=True)
    att_grad = jnp.dot(resid[...], wall[:, all_w:o_at], preferred_element_type=F32).astype(BF)
    allowed = allowed_pairs(seg_c[...], seg_r[...], length)
    group = n_q // n_kv
    lane = lax.broadcasted_iota(jnp.int32, (length, LANES), 1)
    log_all = logs[...]
    q_grads, k_grads, v_grads = [], [], []
    for g in range(n_kv):
        k_g = qkv[:, (n_q + g) * HD : (n_q + g + 1) * HD]
        v_g = qkv[:, qk_w + g * HD : qk_w + (g + 1) * HD]
        k_sum = jnp.zeros((length, HD), F32)
        v_sum = jnp.zeros((length, HD), F32)
        for h in range(g * group, (g + 1) * group):
            cut = slice(h * HD, (h + 1) * HD)
            q_h = qkv[:, cut]
            log_h = jnp.sum(jnp.where(lane == h, log_all, 0.0), axis=-1, keepdims=True)
            scores = mm(q_h, k_g, 1, 1) * score_scale
            probs = jnp.where(allowed, jnp.exp(scores - log_h), 0.0)
            a_h = att_grad[:, cut]
            delta = jnp.sum(
                a_h.astype(F32) * att[:, cut].astype(F32), axis=-1, keepdims=True
            )
            prob_grad = mm(a_h, v_g, 1, 1)
            s_grad = (probs * (prob_grad - delta) * score_scale).astype(BF)
            q_grads.append(jnp.dot(s_grad, k_g, preferred_element_type=F32))
            k_sum = k_sum + mm(s_grad, q_h, 0, 0)
            v_sum = v_sum + mm(probs.astype(BF), a_h, 0, 0)
        k_grads.append(k_sum)
        v_grads.append(v_sum)
    qk_grad = jnp.concatenate(q_grads + k_grads, 1)
    qk_low = rotate_lanes(qk_grad, cos[...], -sin[...]).astype(BF)
    low = jnp.concatenate([qk_low, jnp.concatenate(v_grads, 1).astype(BF)], 1)
    sums[:, :all_w] = mm(hid[...], low, 0, 0)
    sums[:, all_w:o_at] = mm(resid[...], att[...], 0, 0)
    place = lax.broadcasted_iota(jnp.int32, (LANES, width), 0)
    gain_hi = gain_moe.astype(BF).astype(F32)
    rows = jnp.where(place == 32, gain_hi, jnp.where(place == 33, gain_moe - gain_hi, 0.0))
    sums[:, o_at:] = mm(rows2[...], logit, 0, 0) + jnp.transpose(rows)
    depth = width // peers
    for k, m in enumerate(visit_order(TOKEN_BITS)):
        at = pl.multiple_of(jnp.bitwise_xor(idx[0], m) * depth, depth)
        out = g_out[k // (peers // 2)]
        k = k % (peers // 2)
        out[k * depth : (k + 1) * depth, :] = sums[pl.ds(at, depth), :].astype(BF)
    partial[...] = mm(low, wall[:, :all_w], 1, 1)
    normed, _ = norm_parts(x[...].astype(F32))
    extra = hi_lo_rows(jnp.sum(partial[...] * normed, axis=0, keepdims=True), span - own)
    scatter_rows(partial, [out.at[0:own, :] for out in msg2], idx[1])
    for out in msg2:
        out[own:, :] = extra


def input_grad_kernel(shares, *refs):
    msgs, (x, gains, rgrad, out, gain_out) = split_refs(refs, shares, 5)
    own, width = x.shape
    upstream = jnp.zeros((own, width), F32)
    gain_sum = jnp.zeros((1, width), F32)
    for msg in msgs:
        upstream = upstream + msg[0:own, :].astype(F32)
        gain_sum = gain_sum + jnp.sum(msg[own:, :].astype(F32), axis=0, keepdims=True)
    normed, inverse = norm_parts(x[...].astype(F32))
    through = norm_backward(upstream, normed, inverse, gains[0:1, :])
    out[...] = (rgrad[...] + through).astype(BF)
    gain_out[...] = jnp.broadcast_to(gain_sum, gain_out.shape)


def attn_grad_kernel(terms, widths, *refs):
    ins, (query, key, value, output, router, gain) = split_refs(refs, terms, 6)
    q_w, kv_w, experts = widths
    total = ins[0][...].astype(F32)
    for ref in ins[1:]:
        total = total + ref[...].astype(F32)
    all_w = q_w + 2 * kv_w
    query[...] = total[:, :q_w]
    key[...] = total[:, q_w : q_w + kv_w]
    value[...] = total[:, q_w + kv_w : all_w]
    output[...] = jnp.transpose(total[:, all_w : all_w + q_w])
    tail = total[:, all_w + q_w :]
    router[...] = tail[:, :experts]
    tail_t = jnp.transpose(tail)
    gain[...] = tail_t[experts : experts + 1, :] + tail_t[experts + 1 : experts + 2, :]


def layer_out_kernel(first, second, res, out):
    total = first[...].astype(F32) + second[...].astype(F32)
    out[...] = (res[...] + total).astype(BF)


def swap(values, axis):
    got = [values[0]]
    for m in range(1, len(values)):
        got.append(lax.ppermute(values[m], axis, [(i, i ^ m) for i in range(len(values))]))
    return got


def permute(value, axis, bit):
    count = lax.axis_size(axis)
    return lax.ppermute(value, axis, [(i, i ^ bit) for i in range(count)])


def gather_dp(value, bits):
    for at, bit in enumerate(bits):
        got = permute(value, "dp", bit)
        if at == len(bits) - 1:
            return value, got
        value = jnp.concatenate([value, got], 0)


def gather_all(value):
    first = jnp.concatenate(gather_dp(value, TOKEN_BITS), 0)
    across = permute(first, "tensor", 2)
    beside = permute(first, "tensor", 1)
    return first, beside, across, permute(across, "tensor", 1)


def reduce_dp(even, odd, other=None):
    got = permute(odd, "dp", 1)
    even = even + got if other is None else even + other + got
    half = even.shape[0] // 2
    even = even[:half] + permute(even[half:], "dp", 2)
    half = half // 2
    return even[:half], permute(even[half:], "dp", 4)


def reduce_all(parts):
    half = parts[0].shape[0] // 2
    own = permute(parts[1], "tensor", 1)
    far = permute(parts[3], "tensor", 1)
    far_odd = permute(parts[2][half:] + far[half:], "tensor", 2)
    far_even = permute(parts[2][:half] + far[:half], "tensor", 2)
    odd = parts[0][half:] + own[half:] + far_odd
    return reduce_dp(parts[0][:half] + own[:half], odd, far_even)


def move_chunks(parts):
    pieces = {}
    for c, chunk in enumerate(CHUNKS):
        shape = parts[c][0].shape
        groups = call(
            functools.partial(regroup_kernel, len(parts[c])),
            [((len(parts[c]),) + shape[1:], BF)] * len(chunk),
        )(*parts[c])
        for m, group in zip(chunk, groups):
            pieces[m] = permute(group, "dp", m) if m else group
    return [pieces[m] for m in sorted(pieces)]


def per_device(
    rep,
    layer_input,
    seq_ids,
    expert_ids,
    out_grad,
    gain_attn,
    gain_moe,
    w_query,
    w_key,
    w_value,
    w_output,
    w_router,
    w_gate,
    w_up,
    w_down,
):
    peers = lax.axis_size("dp")
    shares = lax.axis_size("tensor")
    own, width = layer_input.shape
    experts = w_gate.shape[0]
    length = seq_ids.shape[1]
    depth = width // peers
    q_w, kv_w = w_query.shape[1], w_key.shape[1]
    dims = (q_w // HD, kv_w // HD)
    all_w = q_w + 2 * kv_w
    pack_w = all_w + q_w + LANES
    slots = peers * CAP
    wide = width + LANES
    idx = jnp.stack([lax.axis_index("dp"), lax.axis_index("tensor")]).astype(jnp.int32)

    local = w_router.shape[0]
    pack_a = jnp.concatenate([w_query, w_key, w_value], axis=1)
    tail = [w_router, gain_attn[:, None], gain_moe[:, None]]
    tail.append(jnp.zeros((local, LANES - experts - 2), BF))
    pack_b = jnp.concatenate([w_output.T] + tail, axis=1)
    if rep > 1:
        pack_a = lax.all_gather(pack_a, "rep", axis=0, tiled=True)
        pack_b = lax.all_gather(pack_b, "rep", axis=0, tiled=True)
    packs = gather_dp(pack_a, QKV_BITS) + gather_dp(pack_b, REST_BITS)

    x_in = swap([layer_input] * shares, "tensor")

    if rep > 1:
        w_gate = lax.all_gather(w_gate, "rep", axis=1, tiled=True)
        w_up = lax.all_gather(w_up, "rep", axis=1, tiled=True)
        w_down = lax.all_gather(w_down, "rep", axis=2, tiled=True)
    weight_parts = call(
        functools.partial(weight_pack_kernel, shares),
        [((peers // 2, 384, LANES), BF)] * (2 * shares),
        smem=1,
    )(idx, w_gate, w_up, w_down)
    pieces = move_chunks(
        [swap(weight_parts[c * shares : (c + 1) * shares], "tensor") for c in range(len(CHUNKS))],
    )
    grads_in = gather_all(out_grad)

    segment = seq_ids[0]
    before = jnp.sum((segment[None, :] < segment[:, None]).astype(jnp.int32), axis=1)
    position = (jnp.arange(length, dtype=jnp.int32) - before).astype(F32)
    lane = jnp.arange(LANES, dtype=jnp.int32) % HD
    half = HD // 2
    frequency = rope_base ** (-2.0 * (lane % half).astype(F32) / HD)
    angles = position[:, None] * frequency[None, :]
    cosine = jnp.cos(angles)
    sine = jnp.where(lane[None, :] < half, -1.0, 1.0) * jnp.sin(angles)
    seg_c = segment[:, None]
    seg_r = segment[None, :]

    *parts, wall, gains, qkv, att, logs, hid, x_all, misc = call(
        functools.partial(attn_fwd_kernel, peers, shares, dims),
        [((own, width), BF)] * shares
        + [
            ((width, pack_w), BF),
            ((8, width), F32),
            ((length, all_w), BF),
            ((length, q_w), BF),
            ((length, LANES), F32),
            ((length, width), BF),
            ((length, width), BF),
            ((width, LANES), BF),
        ],
        scratch=[((length, width), F32)],
        smem=1,
    )(idx, *x_in, *packs, cosine, sine, seg_c, seg_r)

    ids_own = lax.dynamic_slice_in_dim(expert_ids, lax.axis_index("tensor") * own, own, 0)
    parts = swap(parts, "tensor")
    ids_own = lax.dynamic_slice_in_dim(expert_ids, lax.axis_index("tensor") * own, own, 0)
    res, router, msg = call(
        functools.partial(post_attn_kernel, experts, shares),
        [((own, width), F32), ((own, LANES), F32), ((own, wide), BF)],
    )(*parts, layer_input, ids_own, gains, misc)
    rows_in = gather_all(msg)

    ff = w_gate.shape[2] * shares
    outs = call(
        functools.partial(expert_main_kernel, peers, shares, experts),
        [((peers * own, wide), BF)] * shares
        + [
            ((slots, width), BF),
            ((slots, width), BF),
            ((slots, ff), BF),
            ((slots, 2 * ff), BF),
            ((peers * length, CAP), BF),
            ((slots, LANES), F32),
            ((length, width), BF),
        ],
        scratch=[((width, 2 * ff), BF), ((ff, width), BF)],
        smem=1,
    )(idx, *rows_in, *grads_in, *pieces)
    row_back, saved, rows_near = outs[:shares], outs[shares:-1], outs[-1]
    back = reduce_all(row_back)
    rest = call(
        functools.partial(expert_rest_kernel, peers, shares, 256),
        [((peers * own, width), BF)] * shares
        + [((peers // 2, 384, LANES), BF)] * (2 * shares),
        scratch=[((ff, width), BF)],
        smem=1,
    )(idx, *pieces, *saved)
    y_parts, grad_parts = rest[:shares], rest[shares:]
    grad_parts = [
        swap(grad_parts[c * shares : (c + 1) * shares], "tensor")
        for c in range(len(CHUNKS))
    ]
    grad_parts = move_chunks(grad_parts)
    rgrad, msg = call(
        moe_back_kernel, [((own, width), F32), ((own + 16, wide), BF)]
    )(*back, router, res, gains, misc, out_grad)
    msgs = swap([msg] * shares, "tensor")

    outs = call(
        functools.partial(attn_bwd_kernel, peers, shares, dims),
        [((width // 2, pack_w), BF)] * 2 + [((own + 16, width), BF)] * shares,
        scratch=[((width, pack_w), F32), ((length, width), F32), ((length, width), BF)],
        smem=1,
    )(idx, *msgs, wall, qkv, att, logs, cosine, sine, seg_c, seg_r, hid, rows_near, x_all)
    msg2 = outs[2:]
    y_parts, msg2 = lax.optimization_barrier((y_parts, msg2))
    mixed = reduce_all(y_parts)
    terms = reduce_dp(outs[0], outs[1])
    if rep > 1:
        total = terms[0].astype(F32) + terms[1].astype(F32)
        terms = (lax.psum_scatter(total, "rep", scatter_dimension=0, tiled=True),)
    rows_own = terms[0].shape[0]
    q_grad, k_grad, v_grad, o_grad, router_grad, gain_moe_grad = call(
        functools.partial(attn_grad_kernel, len(terms), (q_w, kv_w, experts)),
        [
            ((rows_own, q_w), F32),
            ((rows_own, kv_w), F32),
            ((rows_own, kv_w), F32),
            ((q_w, rows_own), F32),
            ((rows_own, experts), F32),
            ((1, rows_own), F32),
        ],
    )(*terms)

    msg2 = swap(msg2, "tensor")
    input_grad, gain_rows = call(
        functools.partial(input_grad_kernel, shares), [((own, width), BF), ((8, width), F32)]
    )(*msg2, layer_input, gains, rgrad)
    gain_cut = gain_rows[:1].reshape(peers, depth)
    gain_cut = lax.all_to_all(gain_cut, "dp", split_axis=0, concat_axis=0, tiled=True)
    gain_attn_grad = jnp.sum(gain_cut, axis=0)
    if rep > 1:
        gain_attn_grad = lax.psum_scatter(gain_attn_grad, "rep", scatter_dimension=0, tiled=True)

    (layer_output,) = call(layer_out_kernel, [((own, width), BF)])(*mixed, res)

    gate_grad, up_grad, down_grad = call(
        functools.partial(weight_grad_kernel, peers, shares),
        [((experts, 128, LANES), F32)] * 3,
        smem=1,
    )(idx, *grad_parts)
    if rep > 1:
        gate_grad = lax.psum_scatter(gate_grad, "rep", scatter_dimension=1, tiled=True)
        up_grad = lax.psum_scatter(up_grad, "rep", scatter_dimension=1, tiled=True)
        down_grad = lax.psum_scatter(down_grad, "rep", scatter_dimension=2, tiled=True)
    return (
        layer_output,
        input_grad,
        gain_attn_grad,
        gain_moe_grad.reshape(-1),
        q_grad,
        k_grad,
        v_grad,
        o_grad,
        router_grad,
        gate_grad,
        up_grad,
        down_grad,
    )


def solution(mesh):
    shares = mesh.shape["tensor"]
    peers = 32 // shares
    rep = mesh.shape["dp"] // peers
    dp = "dp"
    if rep > 1:
        devices = np.asarray(mesh.devices).reshape(peers, rep, shares)
        mesh = jax.sharding.Mesh(devices, ("dp", "rep", "tensor"))
        dp = ("dp", "rep")
    both = ("dp", "tensor") if rep == 1 else ("dp", "rep", "tensor")
    in_specs = (
        P(both, None),
        P(dp, None),
        P(dp, None),
        P(both, None),
        P(dp),
        P(dp),
        P(dp, "tensor"),
        P(dp, "tensor"),
        P(dp, "tensor"),
        P("tensor", dp),
        P(dp, None),
        P(None, dp, "tensor"),
        P(None, dp, "tensor"),
        P(None, "tensor", dp),
    )
    out_specs = (
        P(both, None),
        P(both, None),
        P(dp),
        P(dp),
        P(dp, "tensor"),
        P(dp, "tensor"),
        P(dp, "tensor"),
        P("tensor", dp),
        P(dp, None),
        P(None, dp, "tensor"),
        P(None, dp, "tensor"),
        P(None, "tensor", dp),
    )

    def body(*args):
        return per_device(rep, *args)

    return jax.shard_map(
        body, mesh=mesh, in_specs=in_specs, out_specs=out_specs, check_vma=False
    )
```

```python
import functools

import jax
import jax.numpy as jnp
import numpy as np
from jax import lax
from jax.experimental import pallas as pl
from jax.experimental.pallas import tpu as pltpu
from jax.sharding import PartitionSpec as P


HD = 64
CAP = 128
LANES = 128

eps_norm = 1e-05
score_scale = 0.125
rope_base = 10000.0

CHUNKS = ((0, 1, 4, 5), (2, 3, 6, 7))
TOKEN_BITS = (4, 2, 1)
QKV_BITS = (4, 2, 1)
REST_BITS = (1, 4, 2)

BF = jnp.bfloat16
F32 = jnp.float32


def mm(a, b, ca, cb):
    return lax.dot_general(a, b, (((ca,), (cb,)), ((), ())), preferred_element_type=F32)


def call(kernel, outs, scratch=(), smem=0):
    def run(*args):
        in_specs = [pl.BlockSpec(memory_space=pltpu.SMEM)] * smem
        in_specs += [pl.BlockSpec(memory_space=pltpu.VMEM)] * (len(args) - smem)
        return pl.pallas_call(
            kernel,
            out_shape=[jax.ShapeDtypeStruct(s, d) for s, d in outs],
            in_specs=in_specs,
            out_specs=[pl.BlockSpec(memory_space=pltpu.VMEM)] * len(outs),
            scratch_shapes=[pltpu.VMEM(s, d) for s, d in scratch],
        )(*args)

    return run


def split_refs(refs, *counts):
    parts, at = [], 0
    for count in counts:
        parts.append(refs[at : at + count])
        at += count
    return parts


def norm_parts(values):
    inverse = lax.rsqrt(jnp.mean(values * values, axis=-1, keepdims=True) + eps_norm)
    return values * inverse, inverse


def norm_backward(upstream, normed, inverse, gain):
    scaled = upstream * gain
    return inverse * (scaled - normed * jnp.mean(scaled * normed, axis=-1, keepdims=True))


def rotate_lanes(values, cosine, signed_sine):
    width = values.shape[1]
    half = HD // 2
    lane = lax.broadcasted_iota(jnp.int32, values.shape, 1)
    ahead = pltpu.roll(values, width - half, 1)
    behind = pltpu.roll(values, half, 1)
    partner = jnp.where(lane % HD < half, ahead, behind)
    copies = width // LANES
    return values * jnp.concatenate([cosine] * copies, 1) + partner * jnp.concatenate(
        [signed_sine] * copies, 1
    )


def allowed_pairs(seg_col, seg_row, length):
    rows = lax.broadcasted_iota(jnp.int32, (length, length), 0)
    cols = lax.broadcasted_iota(jnp.int32, (length, length), 1)
    return (seg_col == seg_row) & (rows >= cols)


def visit_order(bits):
    order = [0]
    for bit in bits:
        order = order + [m ^ bit for m in order]
    return order


def scatter_rows(whole, parts, own):
    span = parts[0].shape[0]
    for s, out in enumerate(parts):
        at = pl.multiple_of(jnp.bitwise_xor(own, s) * span, span)
        out[...] = whole[pl.ds(at, span), :].astype(out.dtype)


def attn_fwd_kernel(peers, shares, dims, *refs):
    n_q, n_kv = dims
    (idx,), x_in, w_in, (cos, sin, seg_c, seg_r), parts, outs, (part,) = split_refs(
        refs, 1, shares, 4, 4, shares, 8, 1
    )
    wall, gains, qkv, att, log_out, hid, x, misc = outs
    own = x_in[0].shape[0]
    for s, got in enumerate(x_in):
        at = pl.multiple_of(jnp.bitwise_xor(idx[1], s) * own, own)
        x[pl.ds(at, own), :] = got[...]
    rows = wall.shape[0] // peers
    column = 0
    for pair, bits in ((w_in[:2], QKV_BITS), (w_in[2:], REST_BITS)):
        cols = slice(column, column + pair[0].shape[1])
        column = column + pair[0].shape[1]
        for k, m in enumerate(visit_order(bits)):
            at = pl.multiple_of(jnp.bitwise_xor(idx[0], m) * rows, rows)
            got = pair[k // (peers // 2)]
            k = k % (peers // 2)
            wall[pl.ds(at, rows), cols] = got[k * rows : (k + 1) * rows, :]
    qk_w = (n_q + n_kv) * HD
    all_w = (n_q + 2 * n_kv) * HD
    o_at = all_w + n_q * HD
    misc[...] = wall[:, o_at : o_at + LANES]
    misc_t = jnp.transpose(wall[:, o_at : o_at + LANES].astype(F32))
    gains[...] = misc_t[32:40, :]
    gain = misc_t[32:33, :]
    normed, _ = norm_parts(x[...].astype(F32))
    hidden = (normed * gain).astype(BF)
    hid[...] = hidden
    pre = jnp.dot(hidden, wall[:, :all_w], preferred_element_type=F32)
    qk = rotate_lanes(pre[:, :qk_w], cos[...], sin[...]).astype(BF)
    value = pre[:, qk_w:].astype(BF)
    qkv[...] = jnp.concatenate([qk, value], 1)
    length = x.shape[0]
    allowed = allowed_pairs(seg_c[...], seg_r[...], length)
    group = n_q // n_kv
    outs_h, logs = [], []
    for h in range(n_q):
        g = h // group
        q_h = qk[:, h * HD : (h + 1) * HD]
        k_g = qk[:, (n_q + g) * HD : (n_q + g + 1) * HD]
        v_g = value[:, g * HD : (g + 1) * HD]
        scores = mm(q_h, k_g, 1, 1) * score_scale
        total = jnp.sum(jnp.where(allowed, jnp.exp(scores), 0.0), axis=-1, keepdims=True)
        log_total = jnp.log(total)
        probs = jnp.where(allowed, jnp.exp(scores - log_total), 0.0).astype(BF)
        outs_h.append(jnp.dot(probs, v_g, preferred_element_type=F32).astype(BF))
        logs.append(log_total)
    flat = jnp.concatenate(outs_h, 1)
    att[...] = flat
    lane = lax.broadcasted_iota(jnp.int32, (length, LANES), 1)
    packed = jnp.zeros((length, LANES), F32)
    for h in range(n_q):
        packed = jnp.where(lane == h, logs[h], packed)
    log_out[...] = packed
    part[...] = mm(flat, wall[:, all_w:o_at], 1, 1)
    scatter_rows(part, parts, idx[1])


def post_attn_kernel(experts, shares, *refs):
    parts, (x, gains, misc, res, router, msg) = split_refs(refs, shares, 6)
    width = x.shape[1]
    total = x[...].astype(F32)
    for part in parts:
        total = total + part[...].astype(F32)
    res[...] = total
    normed, _ = norm_parts(total)
    h2 = (normed * gains[1:2, :]).astype(BF)
    logits = jnp.dot(h2, misc[...], preferred_element_type=F32)
    lane = lax.broadcasted_iota(jnp.int32, logits.shape, 1)
    exponent = jnp.where(lane < experts, jnp.exp(logits), 0.0)
    probs = exponent / jnp.sum(exponent, axis=-1, keepdims=True)
    router[...] = probs
    msg[:, :width] = h2
    msg[:, width:] = probs.astype(BF)


def gate_column(router_cols, expert):
    values = router_cols.astype(F32)
    lane = lax.broadcasted_iota(jnp.int32, values.shape, 1)
    return jnp.sum(jnp.where(lane == expert, values, 0.0), axis=-1, keepdims=True)


def load_down(own, pieces, down, shares):
    for m, piece in enumerate(pieces):
        at = pl.ds(pl.multiple_of(jnp.bitwise_xor(own, m) * 128, 128), 128)
        for t in range(shares):
            down[t * 128 : (t + 1) * 128, at] = piece[t, 256:384, :]


def weight_pack_kernel(shares, idx, gate, up, down, *outs):
    for c, chunk in enumerate(CHUNKS):
        for s in range(shares):
            for j, m in enumerate(chunk):
                e = jnp.bitwise_xor(idx[0], m) * shares + jnp.bitwise_xor(idx[1], s)
                for k, w in enumerate((gate, up, down)):
                    outs[c * shares + s][j, k * 128 : (k + 1) * 128, :] = w[e]


def regroup_kernel(shares, *refs):
    ins, outs = split_refs(refs, shares, len(refs) - shares)
    for j, out in enumerate(outs):
        for s in range(shares):
            out[s] = ins[s][j]


def weight_grad_kernel(shares, idx, *refs):
    first, second, outs = split_refs(refs, shares, len(CHUNKS[1]), 3)
    for c, chunk in enumerate(CHUNKS):
        for j, m in enumerate(chunk):
            for s in range(shares):
                e = jnp.bitwise_xor(idx[0], m) * shares + jnp.bitwise_xor(idx[1], s)
                got = first[s].at[j] if c == 0 else second[j].at[s]
                for k in range(3):
                    outs[k][e] = got[k * 128 : (k + 1) * 128, :].astype(F32)


def expert_pre_kernel(peers, shares, *refs):
    (idx,), grads_in, pieces, (hot_out, grads_out, raw, wgu, down) = split_refs(
        refs, 1, shares, peers, 5
    )
    ff = shares * 128
    width = grads_out.shape[1]
    span = grads_in[0].shape[0] // peers
    block = shares * span
    for m, piece in enumerate(pieces):
        at = pl.ds(pl.multiple_of(jnp.bitwise_xor(idx[0], m) * 128, 128), 128)
        for t in range(shares):
            wgu[at, t * 128 : (t + 1) * 128] = piece[t, 0:128, :]
            wgu[at, ff + t * 128 : ff + (t + 1) * 128] = piece[t, 128:256, :]
    load_down(idx[0], pieces, down, shares)
    expert = idx[0] * shares + idx[1]
    r = lax.broadcasted_iota(jnp.int32, (block, block), 0)
    c = lax.broadcasted_iota(jnp.int32, (block, block), 1)
    lower = jnp.where(r > c, 1.0, 0.0).astype(BF)
    slot = lax.broadcasted_iota(jnp.int32, (block, CAP), 1)

    def body(step, carry):
        grads = []
        for half in range(2):
            k = step * 2 + half
            at = pl.ds(pl.multiple_of(k * span, span), span)
            tokens = jnp.concatenate([ref[at, :] for ref in grads_in], 0)
            member = jnp.where(slot == expert, tokens[:, width:].astype(F32), 0.0)
            rank = jnp.dot(lower, member.astype(BF), preferred_element_type=F32)
            rank = jnp.sum(jnp.where(slot == expert, rank, 0.0), -1, keepdims=True)
            is_member = jnp.sum(member, axis=-1, keepdims=True) > 0.0
            place = jnp.where(is_member, rank, -1.0)
            hot = jnp.where(place == slot.astype(F32), 1.0, 0.0).astype(BF)
            hot_out[pl.ds(pl.multiple_of(k * block, block), block), :] = hot
            grads.append(mm(hot, tokens[:, :width], 0, 0).astype(BF))
        grad_rows = jnp.concatenate(grads, 0)
        at = pl.ds(pl.multiple_of(step * 2 * CAP, 2 * CAP), 2 * CAP)
        grads_out[at, :] = grad_rows
        raw[at, :] = mm(grad_rows, down[...], 1, 1)
        return carry

    lax.fori_loop(0, peers // 2, body, 0)


def expert_main_kernel(peers, shares, *refs):
    (idx,), rows_in, (hot_in, raw_in, wgu), back, outs = split_refs(
        refs, 1, shares, 3, shares, 5
    )
    rows_out, hid, gpu, gate_out, near_out = outs
    ff = raw_in.shape[1]
    width = rows_out.shape[1]
    span = rows_in[0].shape[0] // peers
    block = shares * span
    for s in range(shares):
        near_out[s * span : (s + 1) * span, :] = rows_in[s][0:span, :width]
    expert = idx[0] * shares + idx[1]
    lane = lax.broadcasted_iota(jnp.int32, (2 * CAP, LANES), 1)

    def body(step, carry):
        slots, hots = [], []
        for half in range(2):
            k = step * 2 + half
            at = pl.ds(pl.multiple_of(k * span, span), span)
            tokens = jnp.concatenate([ref[at, :] for ref in rows_in], 0)
            hot = hot_in[pl.ds(pl.multiple_of(k * block, block), block), :]
            hots.append(hot)
            slots.append(mm(hot, tokens, 0, 0).astype(BF))
        rows = jnp.concatenate(slots, 0)
        at = pl.ds(pl.multiple_of(step * 2 * CAP, 2 * CAP), 2 * CAP)
        gate = gate_column(rows[:, width:], expert)
        rows = rows[:, :width]
        rows_out[at, :] = rows
        gate_out[at, :] = jnp.broadcast_to(gate, (2 * CAP, LANES))
        pre = jnp.dot(rows, wgu[...], preferred_element_type=F32)
        raw = raw_in[at, :]
        gate_pre = pre[:, :ff]
        up_pre = pre[:, ff:]
        sig = jax.nn.sigmoid(gate_pre)
        silu = gate_pre * sig
        hidden = (silu * up_pre).astype(BF)
        hid[at, :] = hidden
        gate_grad = jnp.sum(hidden.astype(F32) * raw, axis=-1, keepdims=True)
        hidden_grad = raw * gate
        gp = (hidden_grad * up_pre * sig * (1.0 + gate_pre * (1.0 - sig))).astype(BF)
        up = (hidden_grad * silu).astype(BF)
        both = jnp.concatenate([gp, up], 1)
        gpu[at, :] = both
        row_grad = mm(both, wgu[...], 1, 1).astype(BF)
        tail_grad = jnp.where(lane == expert, gate_grad, 0.0).astype(BF)
        for half, hot in enumerate(hots):
            k = step * 2 + half
            cut = slice(half * CAP, (half + 1) * CAP)
            to = pl.ds(pl.multiple_of(k * span, span), span)
            spread = jnp.dot(hot, row_grad[cut, :], preferred_element_type=F32).astype(BF)
            tail = jnp.dot(hot, tail_grad[cut, :], preferred_element_type=F32).astype(BF)
            for s in range(shares):
                back[s][to, :width] = spread[s * span : (s + 1) * span, :]
                back[s][to, width:] = tail[s * span : (s + 1) * span, :]
        return carry

    lax.fori_loop(0, peers // 2, body, 0)


def expert_rest_kernel(peers, shares, step, *refs):
    (idx,), ins, y_out, first_out, second_out, (scaled,) = split_refs(
        refs, 1, 7, shares, len(CHUNKS[0]), shares, 1
    )
    rows, hid, gpu, gate_in, hot_in, grads, down = ins
    span = y_out[0].shape[0] // peers
    block = shares * span
    scaled[...] = (grads[...].astype(F32) * gate_in[:, 0:1]).astype(BF)

    def out_rows(k, carry):
        at = pl.ds(pl.multiple_of(k * CAP, CAP), CAP)
        out = jnp.dot(hid[at, :], down[...], preferred_element_type=F32)
        out = (out * gate_in[at, 0:1]).astype(BF)
        hot = hot_in[pl.ds(pl.multiple_of(k * block, block), block), :]
        spread = jnp.dot(hot, out, preferred_element_type=F32).astype(BF)
        to = pl.ds(pl.multiple_of(k * span, span), span)
        for s in range(shares):
            y_out[s][to, :] = spread[s * span : (s + 1) * span, :]
        return carry

    lax.fori_loop(0, peers, out_rows, 0)

    def model_rows(p):
        q = jnp.bitwise_xor(p, idx[0] // 2)
        at = pl.ds(pl.multiple_of(q * step, step), step)
        both = mm(rows[:, at], gpu[...], 0, 0).astype(BF)
        return both, mm(hid[...], scaled[:, at], 0, 0).astype(BF)

    def store(to, both, down_g, s, t):
        r = slice(s * 128, (s + 1) * 128)
        to[0:128, :] = both[r, t * 128 : (t + 1) * 128]
        to[128:256, :] = both[r, (shares + t) * 128 : (shares + t + 1) * 128]
        to[256:384, :] = down_g[t * 128 : (t + 1) * 128, r]

    low = idx[0] % 2
    for pair in range(2):
        both, down_g = model_rows(CHUNKS[0][pair * 2] // 2)
        for s in range(2):
            for odd in range(2):

                @pl.when(jnp.bitwise_xor(low, s) == odd)
                def _():
                    for t in range(shares):
                        store(first_out[pair * 2 + odd].at[t], both, down_g, s, t)

    def body(pair, carry):
        both, down_g = model_rows(pair * 2 + 1)
        for s in range(2):
            j = pair * 2 + jnp.bitwise_xor(low, s)
            for t in range(shares):
                store(second_out[t].at[j], both, down_g, s, t)
        return carry

    lax.fori_loop(0, 2, body, 0)


def hi_lo_rows(row, count):
    hi = row.astype(BF)
    lo = (row - hi.astype(F32)).astype(BF)
    place = lax.broadcasted_iota(jnp.int32, (count, row.shape[1]), 0)
    out = jnp.where(place == 0, hi.astype(F32), jnp.where(place == 1, lo.astype(F32), 0.0))
    return out.astype(BF)


def moe_back_kernel(*refs):
    backs, (router, res, gains, misc, out_grad, rgrad, msg) = split_refs(refs, 2, 7)
    own, width = res.shape
    total = backs[0][...].astype(F32) + backs[1][...].astype(F32)
    upstream = total[:, :width]
    prob_grad = total[:, width:]
    probs = router[...]
    logit = (probs * (prob_grad - jnp.sum(probs * prob_grad, axis=-1, keepdims=True))).astype(BF)
    upstream = upstream + mm(logit, misc[...], 1, 1)
    normed, inverse = norm_parts(res[...])
    gain_grad = jnp.sum(upstream * normed, axis=0, keepdims=True)
    grad = out_grad[...].astype(F32) + norm_backward(upstream, normed, inverse, gains[1:2, :])
    rgrad[...] = grad
    msg[0:own, :width] = grad.astype(BF)
    msg[0:own, width:] = logit
    msg[own:, :width] = hi_lo_rows(gain_grad, msg.shape[0] - own)
    msg[own:, width:] = jnp.zeros((msg.shape[0] - own, LANES), BF)


def attn_bwd_kernel(peers, shares, dims, *refs):
    n_q, n_kv = dims
    (idx,), msgs, ins, g_out, msg2, (sums, partial, resid) = split_refs(
        refs, 1, shares, 11, 2, shares, 3
    )
    wall, qkv, att, logs, cos, sin, seg_c, seg_r, hid, rows2, x = ins
    length, width = x.shape
    own = length // shares
    qk_w = (n_q + n_kv) * HD
    all_w = (n_q + 2 * n_kv) * HD
    o_at = all_w + n_q * HD
    for s, msg in enumerate(msgs):
        at = pl.multiple_of(jnp.bitwise_xor(idx[1], s) * own, own)
        resid[pl.ds(at, own), :] = msg[0:own, :width]
    logit = jnp.concatenate([msg[0:own, width:] for msg in msgs], 0)
    gain_moe = jnp.zeros((1, width), F32)
    for msg in msgs:
        extra = msg[own:, :width].astype(F32)
        gain_moe = gain_moe + jnp.sum(extra, axis=0, keepdims=True)
    att_grad = jnp.dot(resid[...], wall[:, all_w:o_at], preferred_element_type=F32).astype(BF)
    allowed = allowed_pairs(seg_c[...], seg_r[...], length)
    group = n_q // n_kv
    lane = lax.broadcasted_iota(jnp.int32, (length, LANES), 1)
    log_all = logs[...]
    q_grads, k_grads, v_grads = [], [], []
    for g in range(n_kv):
        k_g = qkv[:, (n_q + g) * HD : (n_q + g + 1) * HD]
        v_g = qkv[:, qk_w + g * HD : qk_w + (g + 1) * HD]
        k_sum = jnp.zeros((length, HD), F32)
        v_sum = jnp.zeros((length, HD), F32)
        for h in range(g * group, (g + 1) * group):
            cut = slice(h * HD, (h + 1) * HD)
            q_h = qkv[:, cut]
            log_h = jnp.sum(jnp.where(lane == h, log_all, 0.0), axis=-1, keepdims=True)
            scores = mm(q_h, k_g, 1, 1) * score_scale
            probs = jnp.where(allowed, jnp.exp(scores - log_h), 0.0)
            a_h = att_grad[:, cut]
            delta = jnp.sum(
                a_h.astype(F32) * att[:, cut].astype(F32), axis=-1, keepdims=True
            )
            prob_grad = mm(a_h, v_g, 1, 1)
            s_grad = (probs * (prob_grad - delta) * score_scale).astype(BF)
            q_grads.append(jnp.dot(s_grad, k_g, preferred_element_type=F32))
            k_sum = k_sum + mm(s_grad, q_h, 0, 0)
            v_sum = v_sum + mm(probs.astype(BF), a_h, 0, 0)
        k_grads.append(k_sum)
        v_grads.append(v_sum)
    qk_grad = jnp.concatenate(q_grads + k_grads, 1)
    qk_low = rotate_lanes(qk_grad, cos[...], -sin[...]).astype(BF)
    low = jnp.concatenate([qk_low, jnp.concatenate(v_grads, 1).astype(BF)], 1)
    sums[:, :all_w] = mm(hid[...], low, 0, 0)
    sums[:, all_w:o_at] = mm(resid[...], att[...], 0, 0)
    place = lax.broadcasted_iota(jnp.int32, (LANES, width), 0)
    gain_hi = gain_moe.astype(BF).astype(F32)
    partial[...] = mm(low, wall[:, :all_w], 1, 1)
    normed, _ = norm_parts(x[...].astype(F32))
    gain_attn = jnp.sum(partial[...] * normed, axis=0, keepdims=True)
    attn_hi = gain_attn.astype(BF).astype(F32)
    rows = jnp.zeros((LANES, width), F32)
    gain_rows = (gain_hi, gain_moe - gain_hi, attn_hi, gain_attn - attn_hi)
    for at, row in enumerate(gain_rows):
        rows = jnp.where(place == 32 + at, row, rows)
    sums[:, o_at:] = mm(rows2[...], logit, 0, 0) + jnp.transpose(rows)
    depth = width // peers
    for k, m in enumerate(visit_order(TOKEN_BITS)):
        at = pl.multiple_of(jnp.bitwise_xor(idx[0], m) * depth, depth)
        out = g_out[k // (peers // 2)]
        k = k % (peers // 2)
        out[k * depth : (k + 1) * depth, :] = sums[pl.ds(at, depth), :].astype(BF)
    scatter_rows(partial, msg2, idx[1])


def input_grad_kernel(shares, *refs):
    parts, (x, gains, rgrad, out) = split_refs(refs, shares, 4)
    upstream = parts[0][...].astype(F32)
    for part in parts[1:]:
        upstream = upstream + part[...].astype(F32)
    normed, inverse = norm_parts(x[...].astype(F32))
    through = norm_backward(upstream, normed, inverse, gains[0:1, :])
    out[...] = (rgrad[...] + through).astype(BF)


def attn_grad_kernel(terms, widths, *refs):
    ins, (query, key, value, output, router, gain, gain_part) = split_refs(refs, terms, 7)
    q_w, kv_w, experts = widths
    total = ins[0][...].astype(F32)
    for ref in ins[1:]:
        total = total + ref[...].astype(F32)
    all_w = q_w + 2 * kv_w
    query[...] = total[:, :q_w]
    key[...] = total[:, q_w : q_w + kv_w]
    value[...] = total[:, q_w + kv_w : all_w]
    output[...] = jnp.transpose(total[:, all_w : all_w + q_w])
    tail = total[:, all_w + q_w :]
    router[...] = tail[:, :experts]
    tail_t = jnp.transpose(tail)
    gain[...] = tail_t[experts : experts + 1, :] + tail_t[experts + 1 : experts + 2, :]
    part = tail_t[experts + 2 : experts + 3, :] + tail_t[experts + 3 : experts + 4, :]
    gain_part[...] = jnp.broadcast_to(part, gain_part.shape)


def layer_out_kernel(first, second, res, out):
    total = first[...].astype(F32) + second[...].astype(F32)
    out[...] = (res[...] + total).astype(BF)


def swap(values, axis):
    got = [values[0]]
    for m in range(1, len(values)):
        got.append(lax.ppermute(values[m], axis, [(i, i ^ m) for i in range(len(values))]))
    return got


def permute(value, axis, bit):
    count = lax.axis_size(axis)
    return lax.ppermute(value, axis, [(i, i ^ bit) for i in range(count)])


def gather_dp(value, bits):
    for at, bit in enumerate(bits):
        got = permute(value, "dp", bit)
        if at == len(bits) - 1:
            return value, got
        value = jnp.concatenate([value, got], 0)


def gather_all(value):
    first = jnp.concatenate(gather_dp(value, TOKEN_BITS), 0)
    across = permute(first, "tensor", 2)
    beside = permute(first, "tensor", 1)
    return first, beside, across, permute(across, "tensor", 1)


def reduce_dp(even, odd, other=None):
    got = permute(odd, "dp", 1)
    even = even + got if other is None else even + other + got
    half = even.shape[0] // 2
    even = even[:half] + permute(even[half:], "dp", 2)
    half = half // 2
    return even[:half], permute(even[half:], "dp", 4)


def reduce_all(parts):
    half = parts[0].shape[0] // 2
    own = permute(parts[1], "tensor", 1)
    far = permute(parts[3], "tensor", 1)
    far_odd = permute(parts[2][half:] + far[half:], "tensor", 2)
    far_even = permute(parts[2][:half] + far[:half], "tensor", 2)
    odd = parts[0][half:] + own[half:] + far_odd
    return reduce_dp(parts[0][:half] + own[:half], odd, far_even)


def regroup(parts):
    shape = parts[0].shape
    return call(
        functools.partial(regroup_kernel, len(parts)), [((len(parts),) + shape[1:], BF)] * shape[0]
    )(*parts)


def move_chunks(parts):
    pieces = {}
    for c, chunk in enumerate(CHUNKS):
        for m, group in zip(chunk, regroup(parts[c])):
            pieces[m] = permute(group, "dp", m) if m else group
    return [pieces[m] for m in sorted(pieces)]


def per_device(
    rep,
    layer_input,
    seq_ids,
    expert_ids,
    out_grad,
    gain_attn,
    gain_moe,
    w_query,
    w_key,
    w_value,
    w_output,
    w_router,
    w_gate,
    w_up,
    w_down,
):
    peers = lax.axis_size("dp")
    shares = lax.axis_size("tensor")
    own, width = layer_input.shape
    experts = w_gate.shape[0]
    length = seq_ids.shape[1]
    q_w, kv_w = w_query.shape[1], w_key.shape[1]
    dims = (q_w // HD, kv_w // HD)
    all_w = q_w + 2 * kv_w
    pack_w = all_w + q_w + LANES
    slots = peers * CAP
    wide = width + LANES
    idx = jnp.stack([lax.axis_index("dp"), lax.axis_index("tensor")]).astype(jnp.int32)

    local = w_router.shape[0]
    pack_a = jnp.concatenate([w_query, w_key, w_value], axis=1)
    tail = [w_router, gain_attn[:, None], gain_moe[:, None]]
    tail.append(jnp.zeros((local, LANES - experts - 2), BF))
    pack_b = jnp.concatenate([w_output.T] + tail, axis=1)
    if rep > 1:
        pack_a = lax.all_gather(pack_a, "rep", axis=0, tiled=True)
        pack_b = lax.all_gather(pack_b, "rep", axis=0, tiled=True)
    packs = gather_dp(pack_a, QKV_BITS) + gather_dp(pack_b, REST_BITS)

    x_in = swap([layer_input] * shares, "tensor")

    if rep > 1:
        w_gate = lax.all_gather(w_gate, "rep", axis=1, tiled=True)
        w_up = lax.all_gather(w_up, "rep", axis=1, tiled=True)
        w_down = lax.all_gather(w_down, "rep", axis=2, tiled=True)
    weight_parts = call(
        functools.partial(weight_pack_kernel, shares),
        [((peers // 2, 384, LANES), BF)] * (2 * shares),
        smem=1,
    )(idx, w_gate, w_up, w_down)
    pieces = move_chunks(
        [swap(weight_parts[c * shares : (c + 1) * shares], "tensor") for c in range(len(CHUNKS))],
    )
    ids_own = lax.dynamic_slice_in_dim(expert_ids, lax.axis_index("tensor") * own, own, 0)
    lanes = jnp.arange(LANES, dtype=jnp.int32)
    member = jnp.sum((ids_own[:, :, None] == lanes).astype(F32), axis=1).astype(BF)
    grads_in = gather_all(jnp.concatenate([out_grad, member], axis=1))

    segment = seq_ids[0]
    before = jnp.sum((segment[None, :] < segment[:, None]).astype(jnp.int32), axis=1)
    position = (jnp.arange(length, dtype=jnp.int32) - before).astype(F32)
    lane = jnp.arange(LANES, dtype=jnp.int32) % HD
    half = HD // 2
    frequency = rope_base ** (-2.0 * (lane % half).astype(F32) / HD)
    angles = position[:, None] * frequency[None, :]
    cosine = jnp.cos(angles)
    sine = jnp.where(lane[None, :] < half, -1.0, 1.0) * jnp.sin(angles)
    seg_c = segment[:, None]
    seg_r = segment[None, :]

    *parts, wall, gains, qkv, att, logs, hid, x_all, misc = call(
        functools.partial(attn_fwd_kernel, peers, shares, dims),
        [((own, width), BF)] * shares
        + [
            ((width, pack_w), BF),
            ((8, width), F32),
            ((length, all_w), BF),
            ((length, q_w), BF),
            ((length, LANES), F32),
            ((length, width), BF),
            ((length, width), BF),
            ((width, LANES), BF),
        ],
        scratch=[((length, width), F32)],
        smem=1,
    )(idx, *x_in, *packs, cosine, sine, seg_c, seg_r)

    parts = swap(parts, "tensor")
    res, router, msg = call(
        functools.partial(post_attn_kernel, experts, shares),
        [((own, width), F32), ((own, LANES), F32), ((own, wide), BF)],
    )(*parts, layer_input, gains, misc)
    rows_in = gather_all(msg)

    ff = w_gate.shape[2] * shares
    hots, grad_rows, raw, wgu, down = call(
        functools.partial(expert_pre_kernel, peers, shares),
        [
            ((peers * length, CAP), BF),
            ((slots, width), BF),
            ((slots, ff), F32),
            ((width, 2 * ff), BF),
            ((ff, width), BF),
        ],
        smem=1,
    )(idx, *grads_in, *pieces)
    outs = call(
        functools.partial(expert_main_kernel, peers, shares),
        [((peers * own, wide), BF)] * shares
        + [
            ((slots, width), BF),
            ((slots, ff), BF),
            ((slots, 2 * ff), BF),
            ((slots, LANES), F32),
            ((length, width), BF),
        ],
        smem=1,
    )(idx, *rows_in, hots, raw, wgu)
    row_back, saved, rows_near = outs[:shares], outs[shares:-1], outs[-1]
    back = reduce_all(row_back)
    rest = call(
        functools.partial(expert_rest_kernel, peers, shares, 256),
        [((peers * own, width), BF)] * shares
        + [((shares, 384, LANES), BF)] * len(CHUNKS[0])
        + [((len(CHUNKS[1]), 384, LANES), BF)] * shares,
        scratch=[((slots, width), BF)],
        smem=1,
    )(idx, *saved, hots, grad_rows, down)
    y_parts, first, second = rest[:shares], rest[shares : shares + 4], rest[shares + 4 :]
    first = [permute(v, "dp", m) if m else v for m, v in zip(CHUNKS[0], first)]
    first = swap(regroup(first), "tensor")
    second = regroup(swap(second, "tensor"))
    second = [permute(v, "dp", m) for m, v in zip(CHUNKS[1], second)]
    mixed = reduce_all(y_parts)
    rgrad, msg = call(
        moe_back_kernel, [((own, width), F32), ((own + 16, wide), BF)]
    )(*back, router, res, gains, misc, out_grad)
    msgs = swap([msg] * shares, "tensor")

    outs = call(
        functools.partial(attn_bwd_kernel, peers, shares, dims),
        [((width // 2, pack_w), BF)] * 2 + [((own, width), BF)] * shares,
        scratch=[((width, pack_w), F32), ((length, width), F32), ((length, width), BF)],
        smem=1,
    )(idx, *msgs, wall, qkv, att, logs, cosine, sine, seg_c, seg_r, hid, rows_near, x_all)
    msg2 = outs[2:]
    terms = reduce_dp(outs[0], outs[1])
    if rep > 1:
        total = terms[0].astype(F32) + terms[1].astype(F32)
        terms = (lax.psum_scatter(total, "rep", scatter_dimension=0, tiled=True),)
    rows_own = terms[0].shape[0]
    q_grad, k_grad, v_grad, o_grad, router_grad, gain_moe_grad, gain_part = call(
        functools.partial(attn_grad_kernel, len(terms), (q_w, kv_w, experts)),
        [
            ((rows_own, q_w), F32),
            ((rows_own, kv_w), F32),
            ((rows_own, kv_w), F32),
            ((q_w, rows_own), F32),
            ((rows_own, experts), F32),
            ((1, rows_own), F32),
            ((8, rows_own), F32),
        ],
    )(*terms)
    gain_attn_grad = sum(swap([gain_part] * shares, "tensor"))[0]

    msg2 = swap(msg2, "tensor")
    (input_grad,) = call(
        functools.partial(input_grad_kernel, shares), [((own, width), BF)]
    )(*msg2, layer_input, gains, rgrad)

    (layer_output,) = call(layer_out_kernel, [((own, width), BF)])(*mixed, res)

    gate_grad, up_grad, down_grad = call(
        functools.partial(weight_grad_kernel, shares), [((experts, 128, LANES), F32)] * 3, smem=1
    )(idx, *first, *second)
    if rep > 1:
        gate_grad = lax.psum_scatter(gate_grad, "rep", scatter_dimension=1, tiled=True)
        up_grad = lax.psum_scatter(up_grad, "rep", scatter_dimension=1, tiled=True)
        down_grad = lax.psum_scatter(down_grad, "rep", scatter_dimension=2, tiled=True)
    return (
        layer_output,
        input_grad,
        gain_attn_grad,
        gain_moe_grad.reshape(-1),
        q_grad,
        k_grad,
        v_grad,
        o_grad,
        router_grad,
        gate_grad,
        up_grad,
        down_grad,
    )


def solution(mesh):
    shares = mesh.shape["tensor"]
    peers = 32 // shares
    rep = mesh.shape["dp"] // peers
    dp = "dp"
    if rep > 1:
        devices = np.asarray(mesh.devices).reshape(peers, rep, shares)
        mesh = jax.sharding.Mesh(devices, ("dp", "rep", "tensor"))
        dp = ("dp", "rep")
    both = ("dp", "tensor") if rep == 1 else ("dp", "rep", "tensor")
    in_specs = (
        P(both, None),
        P(dp, None),
        P(dp, None),
        P(both, None),
        P(dp),
        P(dp),
        P(dp, "tensor"),
        P(dp, "tensor"),
        P(dp, "tensor"),
        P("tensor", dp),
        P(dp, None),
        P(None, dp, "tensor"),
        P(None, dp, "tensor"),
        P(None, "tensor", dp),
    )
    out_specs = (
        P(both, None),
        P(both, None),
        P(dp),
        P(dp),
        P(dp, "tensor"),
        P(dp, "tensor"),
        P(dp, "tensor"),
        P("tensor", dp),
        P(dp, None),
        P(None, dp, "tensor"),
        P(None, dp, "tensor"),
        P(None, "tensor", dp),
    )

    def body(*args):
        return per_device(rep, *args)

    return jax.shard_map(
        body, mesh=mesh, in_specs=in_specs, out_specs=out_specs, check_vma=False
    )
```

```python
import functools

import jax
import jax.numpy as jnp
import numpy as np
from jax import lax
from jax.experimental import pallas as pl
from jax.experimental.pallas import tpu as pltpu
from jax.sharding import PartitionSpec as P


HD = 64
CAP = 128
LANES = 128

eps_norm = 1e-05
score_scale = 0.125
rope_base = 10000.0

CHUNKS = ((0, 2, 4, 6), (1, 3, 5, 7))
TOKEN_BITS = (4, 2, 1)
QKV_BITS = (4, 2, 1)
REST_BITS = (1, 4, 2)
GRAD_BITS = (4, 1, 2)

BF = jnp.bfloat16
F32 = jnp.float32


def mm(a, b, ca, cb):
    return lax.dot_general(a, b, (((ca,), (cb,)), ((), ())), preferred_element_type=F32)


def call(kernel, outs, scratch=(), smem=0):
    def run(*args):
        in_specs = [pl.BlockSpec(memory_space=pltpu.SMEM)] * smem
        in_specs += [pl.BlockSpec(memory_space=pltpu.VMEM)] * (len(args) - smem)
        return pl.pallas_call(
            kernel,
            out_shape=[jax.ShapeDtypeStruct(s, d) for s, d in outs],
            in_specs=in_specs,
            out_specs=[pl.BlockSpec(memory_space=pltpu.VMEM)] * len(outs),
            scratch_shapes=[pltpu.VMEM(s, d) for s, d in scratch],
        )(*args)

    return run


def split_refs(refs, *counts):
    parts, at = [], 0
    for count in counts:
        parts.append(refs[at : at + count])
        at += count
    return parts


def norm_parts(values):
    inverse = lax.rsqrt(jnp.mean(values * values, axis=-1, keepdims=True) + eps_norm)
    return values * inverse, inverse


def norm_backward(upstream, normed, inverse, gain):
    scaled = upstream * gain
    return inverse * (scaled - normed * jnp.mean(scaled * normed, axis=-1, keepdims=True))


def rotate_lanes(values, cosine, signed_sine):
    width = values.shape[1]
    half = HD // 2
    lane = lax.broadcasted_iota(jnp.int32, values.shape, 1)
    ahead = pltpu.roll(values, width - half, 1)
    behind = pltpu.roll(values, half, 1)
    partner = jnp.where(lane % HD < half, ahead, behind)
    copies = width // LANES
    return values * jnp.concatenate([cosine] * copies, 1) + partner * jnp.concatenate(
        [signed_sine] * copies, 1
    )


def allowed_pairs(seg_col, seg_row, length):
    rows = lax.broadcasted_iota(jnp.int32, (length, length), 0)
    cols = lax.broadcasted_iota(jnp.int32, (length, length), 1)
    return (seg_col == seg_row) & (rows >= cols)


def visit_order(bits):
    order = [0]
    for bit in bits:
        order = order + [m ^ bit for m in order]
    return order


def scatter_rows(whole, parts, own):
    span = parts[0].shape[0]
    for s, out in enumerate(parts):
        at = pl.multiple_of(jnp.bitwise_xor(own, s) * span, span)
        out[...] = whole[pl.ds(at, span), :].astype(out.dtype)


def attn_fwd_kernel(peers, shares, dims, *refs):
    n_q, n_kv = dims
    (idx,), x_in, w_in, (cos, sin, seg_c, seg_r), parts, outs, (part,) = split_refs(
        refs, 1, shares, 4, 4, shares, 8, 1
    )
    wall, gains, qkv, att, log_out, hid, x, misc = outs
    own = x_in[0].shape[0]
    for s, got in enumerate(x_in):
        at = pl.multiple_of(jnp.bitwise_xor(idx[1], s) * own, own)
        x[pl.ds(at, own), :] = got[...]
    rows = wall.shape[0] // peers
    column = 0
    for pair, bits in ((w_in[:2], QKV_BITS), (w_in[2:], REST_BITS)):
        cols = slice(column, column + pair[0].shape[1])
        column = column + pair[0].shape[1]
        for k, m in enumerate(visit_order(bits)):
            at = pl.multiple_of(jnp.bitwise_xor(idx[0], m) * rows, rows)
            got = pair[k // (peers // 2)]
            k = k % (peers // 2)
            wall[pl.ds(at, rows), cols] = got[k * rows : (k + 1) * rows, :]
    qk_w = (n_q + n_kv) * HD
    all_w = (n_q + 2 * n_kv) * HD
    o_at = all_w + n_q * HD
    misc[...] = wall[:, o_at : o_at + LANES]
    misc_t = jnp.transpose(wall[:, o_at : o_at + LANES].astype(F32))
    gains[...] = misc_t[32:40, :]
    gain = misc_t[32:33, :]
    normed, _ = norm_parts(x[...].astype(F32))
    hidden = (normed * gain).astype(BF)
    hid[...] = hidden
    pre = jnp.dot(hidden, wall[:, :all_w], preferred_element_type=F32)
    qk = rotate_lanes(pre[:, :qk_w], cos[...], sin[...]).astype(BF)
    value = pre[:, qk_w:].astype(BF)
    qkv[...] = jnp.concatenate([qk, value], 1)
    length = x.shape[0]
    allowed = allowed_pairs(seg_c[...], seg_r[...], length)
    group = n_q // n_kv
    outs_h, logs = [], []
    for h in range(n_q):
        g = h // group
        q_h = qk[:, h * HD : (h + 1) * HD]
        k_g = qk[:, (n_q + g) * HD : (n_q + g + 1) * HD]
        v_g = value[:, g * HD : (g + 1) * HD]
        scores = mm(q_h, k_g, 1, 1) * score_scale
        total = jnp.sum(jnp.where(allowed, jnp.exp(scores), 0.0), axis=-1, keepdims=True)
        log_total = jnp.log(total)
        probs = jnp.where(allowed, jnp.exp(scores - log_total), 0.0).astype(BF)
        outs_h.append(jnp.dot(probs, v_g, preferred_element_type=F32).astype(BF))
        logs.append(log_total)
    flat = jnp.concatenate(outs_h, 1)
    att[...] = flat
    lane = lax.broadcasted_iota(jnp.int32, (length, LANES), 1)
    packed = jnp.zeros((length, LANES), F32)
    for h in range(n_q):
        packed = jnp.where(lane == h, logs[h], packed)
    log_out[...] = packed
    part[...] = mm(flat, wall[:, all_w:o_at], 1, 1)
    scatter_rows(part, parts, idx[1])


def post_attn_kernel(experts, shares, *refs):
    parts, (x, gains, misc, res, router, msg) = split_refs(refs, shares, 6)
    width = x.shape[1]
    total = x[...].astype(F32)
    for part in parts:
        total = total + part[...].astype(F32)
    res[...] = total
    normed, _ = norm_parts(total)
    h2 = (normed * gains[1:2, :]).astype(BF)
    logits = jnp.dot(h2, misc[...], preferred_element_type=F32)
    lane = lax.broadcasted_iota(jnp.int32, logits.shape, 1)
    exponent = jnp.where(lane < experts, jnp.exp(logits), 0.0)
    probs = exponent / jnp.sum(exponent, axis=-1, keepdims=True)
    router[...] = probs
    msg[:, :width] = h2
    msg[:, width:] = probs.astype(BF)


def gate_column(router_cols, expert):
    values = router_cols.astype(F32)
    lane = lax.broadcasted_iota(jnp.int32, values.shape, 1)
    return jnp.sum(jnp.where(lane == expert, values, 0.0), axis=-1, keepdims=True)


def load_down(own, pieces, down, shares):
    for m, piece in enumerate(pieces):
        at = pl.ds(pl.multiple_of(jnp.bitwise_xor(own, m) * 128, 128), 128)
        for t in range(shares):
            down[t * 128 : (t + 1) * 128, at] = piece[t, 256:384, :]


def weight_pack_kernel(shares, idx, gate, up, down, *outs):
    for c, chunk in enumerate(CHUNKS):
        for s in range(shares):
            for j, m in enumerate(chunk):
                e = jnp.bitwise_xor(idx[0], m) * shares + jnp.bitwise_xor(idx[1], s)
                for k, w in enumerate((gate, up, down)):
                    outs[c * shares + s][j, k * 128 : (k + 1) * 128, :] = w[e]


def regroup_kernel(shares, *refs):
    ins, outs = split_refs(refs, shares, len(refs) - shares)
    for j, out in enumerate(outs):
        for s in range(shares):
            out[s] = ins[s][j]


def weight_grad_kernel(shares, idx, *refs):
    first, second, outs = split_refs(refs, shares, len(CHUNKS[1]), 3)
    for c, chunk in enumerate(CHUNKS):
        for j, m in enumerate(chunk):
            for s in range(shares):
                e = jnp.bitwise_xor(idx[0], m) * shares + jnp.bitwise_xor(idx[1], s)
                got = first[s].at[j] if c == 0 else second[j].at[s]
                for k in range(3):
                    outs[k][e] = got[k * 128 : (k + 1) * 128, :].astype(F32)


def expert_pre_kernel(peers, shares, *refs):
    (idx,), grads_in, pieces, (hot_out, grads_out, raw, wgu, down) = split_refs(
        refs, 1, shares, peers, 5
    )
    ff = shares * 128
    width = grads_out.shape[1]
    span = grads_in[0].shape[0] // peers
    block = shares * span
    for m, piece in enumerate(pieces):
        at = pl.ds(pl.multiple_of(jnp.bitwise_xor(idx[0], m) * 128, 128), 128)
        for t in range(shares):
            wgu[at, t * 128 : (t + 1) * 128] = piece[t, 0:128, :]
            wgu[at, ff + t * 128 : ff + (t + 1) * 128] = piece[t, 128:256, :]
    load_down(idx[0], pieces, down, shares)
    expert = idx[0] * shares + idx[1]
    r = lax.broadcasted_iota(jnp.int32, (block, block), 0)
    c = lax.broadcasted_iota(jnp.int32, (block, block), 1)
    lower = jnp.where(r > c, 1.0, 0.0).astype(BF)
    slot = lax.broadcasted_iota(jnp.int32, (block, CAP), 1)

    def body(step, carry):
        grads = []
        for half in range(2):
            k = step * 2 + half
            at = pl.ds(pl.multiple_of(k * span, span), span)
            tokens = jnp.concatenate([ref[at, :] for ref in grads_in], 0)
            member = jnp.where(slot == expert, tokens[:, width:].astype(F32), 0.0)
            rank = jnp.dot(lower, member.astype(BF), preferred_element_type=F32)
            rank = jnp.sum(jnp.where(slot == expert, rank, 0.0), -1, keepdims=True)
            is_member = jnp.sum(member, axis=-1, keepdims=True) > 0.0
            place = jnp.where(is_member, rank, -1.0)
            hot = jnp.where(place == slot.astype(F32), 1.0, 0.0).astype(BF)
            hot_out[pl.ds(pl.multiple_of(k * block, block), block), :] = hot
            grads.append(mm(hot, tokens[:, :width], 0, 0).astype(BF))
        grad_rows = jnp.concatenate(grads, 0)
        at = pl.ds(pl.multiple_of(step * 2 * CAP, 2 * CAP), 2 * CAP)
        grads_out[at, :] = grad_rows
        raw[at, :] = mm(grad_rows, down[...], 1, 1)
        return carry

    lax.fori_loop(0, peers // 2, body, 0)


def expert_main_kernel(peers, shares, *refs):
    (idx,), rows_in, (hot_in, raw_in, wgu), back, outs = split_refs(
        refs, 1, shares, 3, shares, 5
    )
    rows_out, hid, gpu, gate_out, near_out = outs
    ff = raw_in.shape[1]
    width = rows_out.shape[1]
    span = rows_in[0].shape[0] // peers
    block = shares * span
    for s in range(shares):
        near_out[s * span : (s + 1) * span, :] = rows_in[s][0:span, :width]
    expert = idx[0] * shares + idx[1]
    lane = lax.broadcasted_iota(jnp.int32, (2 * CAP, LANES), 1)

    def body(step, carry):
        slots, hots = [], []
        for half in range(2):
            k = step * 2 + half
            at = pl.ds(pl.multiple_of(k * span, span), span)
            tokens = jnp.concatenate([ref[at, :] for ref in rows_in], 0)
            hot = hot_in[pl.ds(pl.multiple_of(k * block, block), block), :]
            hots.append(hot)
            slots.append(mm(hot, tokens, 0, 0).astype(BF))
        rows = jnp.concatenate(slots, 0)
        at = pl.ds(pl.multiple_of(step * 2 * CAP, 2 * CAP), 2 * CAP)
        gate = gate_column(rows[:, width:], expert)
        rows = rows[:, :width]
        rows_out[at, :] = rows
        gate_out[at, :] = jnp.broadcast_to(gate, (2 * CAP, LANES))
        pre = jnp.dot(rows, wgu[...], preferred_element_type=F32)
        raw = raw_in[at, :]
        gate_pre = pre[:, :ff]
        up_pre = pre[:, ff:]
        sig = jax.nn.sigmoid(gate_pre)
        silu = gate_pre * sig
        hidden = (silu * up_pre).astype(BF)
        hid[at, :] = hidden
        gate_grad = jnp.sum(hidden.astype(F32) * raw, axis=-1, keepdims=True)
        hidden_grad = raw * gate
        gp = (hidden_grad * up_pre * sig * (1.0 + gate_pre * (1.0 - sig))).astype(BF)
        up = (hidden_grad * silu).astype(BF)
        both = jnp.concatenate([gp, up], 1)
        gpu[at, :] = both
        row_grad = mm(both, wgu[...], 1, 1).astype(BF)
        tail_grad = jnp.where(lane == expert, gate_grad, 0.0).astype(BF)
        for half, hot in enumerate(hots):
            k = step * 2 + half
            cut = slice(half * CAP, (half + 1) * CAP)
            to = pl.ds(pl.multiple_of(k * span, span), span)
            spread = jnp.dot(hot, row_grad[cut, :], preferred_element_type=F32).astype(BF)
            tail = jnp.dot(hot, tail_grad[cut, :], preferred_element_type=F32).astype(BF)
            for s in range(shares):
                back[s][to, :width] = spread[s * span : (s + 1) * span, :]
                back[s][to, width:] = tail[s * span : (s + 1) * span, :]
        return carry

    lax.fori_loop(0, peers // 2, body, 0)


def expert_rest_kernel(peers, shares, step, *refs):
    (idx,), ins, y_out, first_out, second_out, scratch = split_refs(
        refs, 1, 7, shares, len(CHUNKS[0]), shares, 3
    )
    rows, hid, gpu, gate_in, hot_in, grads, down = ins
    scaled, both_s, down_s = scratch
    span = y_out[0].shape[0] // peers
    block = shares * span
    scaled[...] = (grads[...].astype(F32) * gate_in[:, 0:1]).astype(BF)

    def out_rows(k, carry):
        at = pl.ds(pl.multiple_of(k * CAP, CAP), CAP)
        out = jnp.dot(hid[at, :], down[...], preferred_element_type=F32)
        out = (out * gate_in[at, 0:1]).astype(BF)
        hot = hot_in[pl.ds(pl.multiple_of(k * block, block), block), :]
        spread = jnp.dot(hot, out, preferred_element_type=F32).astype(BF)
        to = pl.ds(pl.multiple_of(k * span, span), span)
        for s in range(shares):
            y_out[s][to, :] = spread[s * span : (s + 1) * span, :]
        return carry

    lax.fori_loop(0, peers, out_rows, 0)

    low = idx[0] % 2
    for pair in range(peers // 2):
        q = jnp.bitwise_xor(pair, idx[0] // 2)
        at = pl.ds(pl.multiple_of(q * step, step), step)
        both_s[...] = mm(rows[:, at], gpu[...], 0, 0).astype(BF)
        down_s[...] = mm(hid[...], scaled[:, at], 0, 0).astype(BF)
        for odd in range(2):
            r = pl.ds(pl.multiple_of(jnp.bitwise_xor(low, odd) * 128, 128), 128)
            for t in range(shares):
                to = second_out[t].at[pair] if odd else first_out[pair].at[t]
                to[0:128, :] = both_s[r, t * 128 : (t + 1) * 128]
                to[128:256, :] = both_s[r, (shares + t) * 128 : (shares + t + 1) * 128]
                to[256:384, :] = down_s[t * 128 : (t + 1) * 128, r]


def hi_lo_rows(row, count):
    hi = row.astype(BF)
    lo = (row - hi.astype(F32)).astype(BF)
    place = lax.broadcasted_iota(jnp.int32, (count, row.shape[1]), 0)
    out = jnp.where(place == 0, hi.astype(F32), jnp.where(place == 1, lo.astype(F32), 0.0))
    return out.astype(BF)


def moe_back_kernel(*refs):
    backs, (router, res, gains, misc, out_grad, rgrad, msg) = split_refs(refs, 2, 7)
    own, width = res.shape
    total = backs[0][...].astype(F32) + backs[1][...].astype(F32)
    upstream = total[:, :width]
    prob_grad = total[:, width:]
    probs = router[...]
    logit = (probs * (prob_grad - jnp.sum(probs * prob_grad, axis=-1, keepdims=True))).astype(BF)
    upstream = upstream + mm(logit, misc[...], 1, 1)
    normed, inverse = norm_parts(res[...])
    gain_grad = jnp.sum(upstream * normed, axis=0, keepdims=True)
    grad = out_grad[...].astype(F32) + norm_backward(upstream, normed, inverse, gains[1:2, :])
    rgrad[...] = grad
    msg[0:own, :width] = grad.astype(BF)
    msg[0:own, width:] = logit
    msg[own:, :width] = hi_lo_rows(gain_grad, msg.shape[0] - own)
    msg[own:, width:] = jnp.zeros((msg.shape[0] - own, LANES), BF)


def attn_bwd_kernel(peers, shares, dims, *refs):
    n_q, n_kv = dims
    (idx,), msgs, ins, g_out, msg2, (sums, partial, resid) = split_refs(
        refs, 1, shares, 11, 2, shares, 3
    )
    wall, qkv, att, logs, cos, sin, seg_c, seg_r, hid, rows2, x = ins
    length, width = x.shape
    own = length // shares
    qk_w = (n_q + n_kv) * HD
    all_w = (n_q + 2 * n_kv) * HD
    o_at = all_w + n_q * HD
    for s, msg in enumerate(msgs):
        at = pl.multiple_of(jnp.bitwise_xor(idx[1], s) * own, own)
        resid[pl.ds(at, own), :] = msg[0:own, :width]
    logit = jnp.concatenate([msg[0:own, width:] for msg in msgs], 0)
    gain_moe = jnp.zeros((1, width), F32)
    for msg in msgs:
        extra = msg[own:, :width].astype(F32)
        gain_moe = gain_moe + jnp.sum(extra, axis=0, keepdims=True)
    att_grad = jnp.dot(resid[...], wall[:, all_w:o_at], preferred_element_type=F32).astype(BF)
    allowed = allowed_pairs(seg_c[...], seg_r[...], length)
    group = n_q // n_kv
    lane = lax.broadcasted_iota(jnp.int32, (length, LANES), 1)
    log_all = logs[...]
    q_grads, k_grads, v_grads = [], [], []
    for g in range(n_kv):
        k_g = qkv[:, (n_q + g) * HD : (n_q + g + 1) * HD]
        v_g = qkv[:, qk_w + g * HD : qk_w + (g + 1) * HD]
        k_sum = jnp.zeros((length, HD), F32)
        v_sum = jnp.zeros((length, HD), F32)
        for h in range(g * group, (g + 1) * group):
            cut = slice(h * HD, (h + 1) * HD)
            q_h = qkv[:, cut]
            log_h = jnp.sum(jnp.where(lane == h, log_all, 0.0), axis=-1, keepdims=True)
            scores = mm(q_h, k_g, 1, 1) * score_scale
            probs = jnp.where(allowed, jnp.exp(scores - log_h), 0.0)
            a_h = att_grad[:, cut]
            delta = jnp.sum(
                a_h.astype(F32) * att[:, cut].astype(F32), axis=-1, keepdims=True
            )
            prob_grad = mm(a_h, v_g, 1, 1)
            s_grad = (probs * (prob_grad - delta) * score_scale).astype(BF)
            q_grads.append(jnp.dot(s_grad, k_g, preferred_element_type=F32))
            k_sum = k_sum + mm(s_grad, q_h, 0, 0)
            v_sum = v_sum + mm(probs.astype(BF), a_h, 0, 0)
        k_grads.append(k_sum)
        v_grads.append(v_sum)
    qk_grad = jnp.concatenate(q_grads + k_grads, 1)
    qk_low = rotate_lanes(qk_grad, cos[...], -sin[...]).astype(BF)
    low = jnp.concatenate([qk_low, jnp.concatenate(v_grads, 1).astype(BF)], 1)
    sums[:, :all_w] = mm(hid[...], low, 0, 0)
    sums[:, all_w:o_at] = mm(resid[...], att[...], 0, 0)
    place = lax.broadcasted_iota(jnp.int32, (LANES, width), 0)
    gain_hi = gain_moe.astype(BF).astype(F32)
    partial[...] = mm(low, wall[:, :all_w], 1, 1)
    normed, _ = norm_parts(x[...].astype(F32))
    gain_attn = jnp.sum(partial[...] * normed, axis=0, keepdims=True)
    attn_hi = gain_attn.astype(BF).astype(F32)
    rows = jnp.zeros((LANES, width), F32)
    gain_rows = (gain_hi, gain_moe - gain_hi, attn_hi, gain_attn - attn_hi)
    for at, row in enumerate(gain_rows):
        rows = jnp.where(place == 32 + at, row, rows)
    sums[:, o_at:] = mm(rows2[...], logit, 0, 0) + jnp.transpose(rows)
    depth = width // peers
    for k, m in enumerate(visit_order(GRAD_BITS)):
        at = pl.multiple_of(jnp.bitwise_xor(idx[0], m) * depth, depth)
        out = g_out[k // (peers // 2)]
        k = k % (peers // 2)
        out[k * depth : (k + 1) * depth, :] = sums[pl.ds(at, depth), :].astype(BF)
    scatter_rows(partial, msg2, idx[1])


def input_grad_kernel(shares, *refs):
    parts, (x, gains, rgrad, out) = split_refs(refs, shares, 4)
    upstream = parts[0][...].astype(F32)
    for part in parts[1:]:
        upstream = upstream + part[...].astype(F32)
    normed, inverse = norm_parts(x[...].astype(F32))
    through = norm_backward(upstream, normed, inverse, gains[0:1, :])
    out[...] = (rgrad[...] + through).astype(BF)


def attn_grad_kernel(terms, widths, *refs):
    ins, (query, key, value, output, router, gain, gain_part) = split_refs(refs, terms, 7)
    q_w, kv_w, experts = widths
    total = ins[0][...].astype(F32)
    for ref in ins[1:]:
        total = total + ref[...].astype(F32)
    all_w = q_w + 2 * kv_w
    query[...] = total[:, :q_w]
    key[...] = total[:, q_w : q_w + kv_w]
    value[...] = total[:, q_w + kv_w : all_w]
    output[...] = jnp.transpose(total[:, all_w : all_w + q_w])
    tail = total[:, all_w + q_w :]
    router[...] = tail[:, :experts]
    tail_t = jnp.transpose(tail)
    gain[...] = tail_t[experts : experts + 1, :] + tail_t[experts + 1 : experts + 2, :]
    part = tail_t[experts + 2 : experts + 3, :] + tail_t[experts + 3 : experts + 4, :]
    gain_part[...] = jnp.broadcast_to(part, gain_part.shape)


def layer_out_kernel(first, second, res, out):
    total = first[...].astype(F32) + second[...].astype(F32)
    out[...] = (res[...] + total).astype(BF)


def swap(values, axis):
    got = [values[0]]
    for m in range(1, len(values)):
        got.append(lax.ppermute(values[m], axis, [(i, i ^ m) for i in range(len(values))]))
    return got


def permute(value, axis, bit):
    count = lax.axis_size(axis)
    return lax.ppermute(value, axis, [(i, i ^ bit) for i in range(count)])


def gather_dp(value, bits):
    for at, bit in enumerate(bits):
        got = permute(value, "dp", bit)
        if at == len(bits) - 1:
            return value, got
        value = jnp.concatenate([value, got], 0)


def gather_all(value):
    first = jnp.concatenate(gather_dp(value, TOKEN_BITS), 0)
    across = permute(first, "tensor", 2)
    beside = permute(first, "tensor", 1)
    return first, beside, across, permute(across, "tensor", 1)


def reduce_dp(near, far, bits, other=None):
    got = permute(far, "dp", bits[2])
    near = near + got if other is None else near + other + got
    half = near.shape[0] // 2
    near = near[:half] + permute(near[half:], "dp", bits[1])
    half = half // 2
    return near[:half], permute(near[half:], "dp", bits[0])


def reduce_all(parts):
    half = parts[0].shape[0] // 2
    own = permute(parts[1], "tensor", 1)
    far = permute(parts[3], "tensor", 1)
    far_odd = permute(parts[2][half:] + far[half:], "tensor", 2)
    far_even = permute(parts[2][:half] + far[:half], "tensor", 2)
    odd = parts[0][half:] + own[half:] + far_odd
    return reduce_dp(parts[0][:half] + own[:half], odd, TOKEN_BITS, far_even)


def regroup(parts):
    shape = parts[0].shape
    return call(
        functools.partial(regroup_kernel, len(parts)), [((len(parts),) + shape[1:], BF)] * shape[0]
    )(*parts)


def move_chunks(parts):
    pieces = {}
    for c, chunk in enumerate(CHUNKS):
        for m, group in zip(chunk, regroup(parts[c])):
            pieces[m] = permute(group, "dp", m) if m else group
    return [pieces[m] for m in sorted(pieces)]


def per_device(
    rep,
    layer_input,
    seq_ids,
    expert_ids,
    out_grad,
    gain_attn,
    gain_moe,
    w_query,
    w_key,
    w_value,
    w_output,
    w_router,
    w_gate,
    w_up,
    w_down,
):
    peers = lax.axis_size("dp")
    shares = lax.axis_size("tensor")
    own, width = layer_input.shape
    experts = w_gate.shape[0]
    length = seq_ids.shape[1]
    q_w, kv_w = w_query.shape[1], w_key.shape[1]
    dims = (q_w // HD, kv_w // HD)
    all_w = q_w + 2 * kv_w
    pack_w = all_w + q_w + LANES
    slots = peers * CAP
    wide = width + LANES
    idx = jnp.stack([lax.axis_index("dp"), lax.axis_index("tensor")]).astype(jnp.int32)

    local = w_router.shape[0]
    pack_a = jnp.concatenate([w_query, w_key, w_value], axis=1)
    tail = [w_router, gain_attn[:, None], gain_moe[:, None]]
    tail.append(jnp.zeros((local, LANES - experts - 2), BF))
    pack_b = jnp.concatenate([w_output.T] + tail, axis=1)
    if rep > 1:
        pack_a = lax.all_gather(pack_a, "rep", axis=0, tiled=True)
        pack_b = lax.all_gather(pack_b, "rep", axis=0, tiled=True)
    packs = gather_dp(pack_a, QKV_BITS) + gather_dp(pack_b, REST_BITS)

    x_in = swap([layer_input] * shares, "tensor")

    if rep > 1:
        w_gate = lax.all_gather(w_gate, "rep", axis=1, tiled=True)
        w_up = lax.all_gather(w_up, "rep", axis=1, tiled=True)
        w_down = lax.all_gather(w_down, "rep", axis=2, tiled=True)
    weight_parts = call(
        functools.partial(weight_pack_kernel, shares),
        [((peers // 2, 384, LANES), BF)] * (2 * shares),
        smem=1,
    )(idx, w_gate, w_up, w_down)
    pieces = move_chunks(
        [swap(weight_parts[c * shares : (c + 1) * shares], "tensor") for c in range(len(CHUNKS))],
    )
    ids_own = lax.dynamic_slice_in_dim(expert_ids, lax.axis_index("tensor") * own, own, 0)
    lanes = jnp.arange(LANES, dtype=jnp.int32)
    member = jnp.sum((ids_own[:, :, None] == lanes).astype(F32), axis=1).astype(BF)
    grads_in = gather_all(jnp.concatenate([out_grad, member], axis=1))

    segment = seq_ids[0]
    before = jnp.sum((segment[None, :] < segment[:, None]).astype(jnp.int32), axis=1)
    position = (jnp.arange(length, dtype=jnp.int32) - before).astype(F32)
    lane = jnp.arange(LANES, dtype=jnp.int32) % HD
    half = HD // 2
    frequency = rope_base ** (-2.0 * (lane % half).astype(F32) / HD)
    angles = position[:, None] * frequency[None, :]
    cosine = jnp.cos(angles)
    sine = jnp.where(lane[None, :] < half, -1.0, 1.0) * jnp.sin(angles)
    seg_c = segment[:, None]
    seg_r = segment[None, :]

    *parts, wall, gains, qkv, att, logs, hid, x_all, misc = call(
        functools.partial(attn_fwd_kernel, peers, shares, dims),
        [((own, width), BF)] * shares
        + [
            ((width, pack_w), BF),
            ((8, width), F32),
            ((length, all_w), BF),
            ((length, q_w), BF),
            ((length, LANES), F32),
            ((length, width), BF),
            ((length, width), BF),
            ((width, LANES), BF),
        ],
        scratch=[((length, width), F32)],
        smem=1,
    )(idx, *x_in, *packs, cosine, sine, seg_c, seg_r)

    parts = swap(parts, "tensor")
    res, router, msg = call(
        functools.partial(post_attn_kernel, experts, shares),
        [((own, width), F32), ((own, LANES), F32), ((own, wide), BF)],
    )(*parts, layer_input, gains, misc)
    rows_in = gather_all(msg)

    ff = w_gate.shape[2] * shares
    hots, grad_rows, raw, wgu, down = call(
        functools.partial(expert_pre_kernel, peers, shares),
        [
            ((peers * length, CAP), BF),
            ((slots, width), BF),
            ((slots, ff), F32),
            ((width, 2 * ff), BF),
            ((ff, width), BF),
        ],
        smem=1,
    )(idx, *grads_in, *pieces)
    outs = call(
        functools.partial(expert_main_kernel, peers, shares),
        [((peers * own, wide), BF)] * shares
        + [
            ((slots, width), BF),
            ((slots, ff), BF),
            ((slots, 2 * ff), BF),
            ((slots, LANES), F32),
            ((length, width), BF),
        ],
        smem=1,
    )(idx, *rows_in, hots, raw, wgu)
    row_back, saved, rows_near = outs[:shares], outs[shares:-1], outs[-1]
    back = reduce_all(row_back)
    rest = call(
        functools.partial(expert_rest_kernel, peers, shares, 256),
        [((peers * own, width), BF)] * shares
        + [((shares, 384, LANES), BF)] * len(CHUNKS[0])
        + [((len(CHUNKS[1]), 384, LANES), BF)] * shares,
        scratch=[((slots, width), BF), ((256, 2 * ff), BF), ((ff, 256), BF)],
        smem=1,
    )(idx, *saved, hots, grad_rows, down)
    y_parts, first, second = rest[:shares], rest[shares : shares + 4], rest[shares + 4 :]
    first = [permute(v, "dp", m) if m else v for m, v in zip(CHUNKS[0], first)]
    first = swap(regroup(first), "tensor")
    second = regroup(swap(second, "tensor"))
    second = [permute(v, "dp", m) for m, v in zip(CHUNKS[1], second)]
    mixed = reduce_all(y_parts)
    rgrad, msg = call(
        moe_back_kernel, [((own, width), F32), ((own + 16, wide), BF)]
    )(*back, router, res, gains, misc, out_grad)
    msgs = swap([msg] * shares, "tensor")

    outs = call(
        functools.partial(attn_bwd_kernel, peers, shares, dims),
        [((width // 2, pack_w), BF)] * 2 + [((own, width), BF)] * shares,
        scratch=[((width, pack_w), F32), ((length, width), F32), ((length, width), BF)],
        smem=1,
    )(idx, *msgs, wall, qkv, att, logs, cosine, sine, seg_c, seg_r, hid, rows_near, x_all)
    msg2 = outs[2:]
    terms = reduce_dp(outs[0], outs[1], GRAD_BITS)
    if rep > 1:
        total = terms[0].astype(F32) + terms[1].astype(F32)
        terms = (lax.psum_scatter(total, "rep", scatter_dimension=0, tiled=True),)
    rows_own = terms[0].shape[0]
    q_grad, k_grad, v_grad, o_grad, router_grad, gain_moe_grad, gain_part = call(
        functools.partial(attn_grad_kernel, len(terms), (q_w, kv_w, experts)),
        [
            ((rows_own, q_w), F32),
            ((rows_own, kv_w), F32),
            ((rows_own, kv_w), F32),
            ((q_w, rows_own), F32),
            ((rows_own, experts), F32),
            ((1, rows_own), F32),
            ((8, rows_own), F32),
        ],
    )(*terms)
    gain_attn_grad = sum(swap([gain_part] * shares, "tensor"))[0]

    msg2 = swap(msg2, "tensor")
    (input_grad,) = call(
        functools.partial(input_grad_kernel, shares), [((own, width), BF)]
    )(*msg2, layer_input, gains, rgrad)

    (layer_output,) = call(layer_out_kernel, [((own, width), BF)])(*mixed, res)

    gate_grad, up_grad, down_grad = call(
        functools.partial(weight_grad_kernel, shares), [((experts, 128, LANES), F32)] * 3, smem=1
    )(idx, *first, *second)
    if rep > 1:
        gate_grad = lax.psum_scatter(gate_grad, "rep", scatter_dimension=1, tiled=True)
        up_grad = lax.psum_scatter(up_grad, "rep", scatter_dimension=1, tiled=True)
        down_grad = lax.psum_scatter(down_grad, "rep", scatter_dimension=2, tiled=True)
    return (
        layer_output,
        input_grad,
        gain_attn_grad,
        gain_moe_grad.reshape(-1),
        q_grad,
        k_grad,
        v_grad,
        o_grad,
        router_grad,
        gate_grad,
        up_grad,
        down_grad,
    )


def solution(mesh):
    shares = mesh.shape["tensor"]
    peers = 32 // shares
    rep = mesh.shape["dp"] // peers
    dp = "dp"
    if rep > 1:
        devices = np.asarray(mesh.devices).reshape(peers, rep, shares)
        mesh = jax.sharding.Mesh(devices, ("dp", "rep", "tensor"))
        dp = ("dp", "rep")
    both = ("dp", "tensor") if rep == 1 else ("dp", "rep", "tensor")
    in_specs = (
        P(both, None),
        P(dp, None),
        P(dp, None),
        P(both, None),
        P(dp),
        P(dp),
        P(dp, "tensor"),
        P(dp, "tensor"),
        P(dp, "tensor"),
        P("tensor", dp),
        P(dp, None),
        P(None, dp, "tensor"),
        P(None, dp, "tensor"),
        P(None, "tensor", dp),
    )
    out_specs = (
        P(both, None),
        P(both, None),
        P(dp),
        P(dp),
        P(dp, "tensor"),
        P(dp, "tensor"),
        P(dp, "tensor"),
        P("tensor", dp),
        P(dp, None),
        P(None, dp, "tensor"),
        P(None, dp, "tensor"),
        P(None, "tensor", dp),
    )

    def body(*args):
        return per_device(rep, *args)

    return jax.shard_map(
        body, mesh=mesh, in_specs=in_specs, out_specs=out_specs, check_vma=False
    )
```

```python
import functools

import jax
import jax.numpy as jnp
import numpy as np
from jax import lax
from jax.experimental import pallas as pl
from jax.experimental.pallas import tpu as pltpu
from jax.sharding import PartitionSpec as P


HD = 64
CAP = 128
LANES = 128

eps_norm = 1e-05
score_scale = 0.125
rope_base = 10000.0

CHUNKS = ((0, 2, 4, 6), (1, 3, 5, 7))
TOKEN_BITS = (4, 2, 1)
QKV_BITS = (4, 2, 1)
REST_BITS = (1, 4, 2)
GRAD_BITS = (4, 1, 2)

BF = jnp.bfloat16
F32 = jnp.float32


def mm(a, b, ca, cb):
    return lax.dot_general(a, b, (((ca,), (cb,)), ((), ())), preferred_element_type=F32)


def call(kernel, outs, scratch=(), smem=0):
    def run(*args):
        in_specs = [pl.BlockSpec(memory_space=pltpu.SMEM)] * smem
        in_specs += [pl.BlockSpec(memory_space=pltpu.VMEM)] * (len(args) - smem)
        return pl.pallas_call(
            kernel,
            out_shape=[jax.ShapeDtypeStruct(s, d) for s, d in outs],
            in_specs=in_specs,
            out_specs=[pl.BlockSpec(memory_space=pltpu.VMEM)] * len(outs),
            scratch_shapes=[pltpu.VMEM(s, d) for s, d in scratch],
        )(*args)

    return run


def split_refs(refs, *counts):
    parts, at = [], 0
    for count in counts:
        parts.append(refs[at : at + count])
        at += count
    return parts


def norm_parts(values):
    inverse = lax.rsqrt(jnp.mean(values * values, axis=-1, keepdims=True) + eps_norm)
    return values * inverse, inverse


def norm_backward(upstream, normed, inverse, gain):
    scaled = upstream * gain
    return inverse * (scaled - normed * jnp.mean(scaled * normed, axis=-1, keepdims=True))


def rotate_lanes(values, cosine, signed_sine):
    width = values.shape[1]
    half = HD // 2
    lane = lax.broadcasted_iota(jnp.int32, values.shape, 1)
    ahead = pltpu.roll(values, width - half, 1)
    behind = pltpu.roll(values, half, 1)
    partner = jnp.where(lane % HD < half, ahead, behind)
    copies = width // LANES
    return values * jnp.concatenate([cosine] * copies, 1) + partner * jnp.concatenate(
        [signed_sine] * copies, 1
    )


def allowed_pairs(seg_col, seg_row, length):
    rows = lax.broadcasted_iota(jnp.int32, (length, length), 0)
    cols = lax.broadcasted_iota(jnp.int32, (length, length), 1)
    return (seg_col == seg_row) & (rows >= cols)


def visit_order(bits):
    order = [0]
    for bit in bits:
        order = order + [m ^ bit for m in order]
    return order


def scatter_rows(whole, parts, own):
    span = parts[0].shape[0]
    for s, out in enumerate(parts):
        at = pl.multiple_of(jnp.bitwise_xor(own, s) * span, span)
        out[...] = whole[pl.ds(at, span), :].astype(out.dtype)


def attn_fwd_kernel(peers, shares, dims, *refs):
    n_q, n_kv = dims
    (idx,), x_in, w_in, (cos, sin, seg_c, seg_r), parts, outs, (part,) = split_refs(
        refs, 1, shares, 4, 4, shares, 8, 1
    )
    wall, gains, qkv, att, log_out, hid, x, misc = outs
    own = x_in[0].shape[0]
    for s, got in enumerate(x_in):
        at = pl.multiple_of(jnp.bitwise_xor(idx[1], s) * own, own)
        x[pl.ds(at, own), :] = got[...]
    rows = wall.shape[0] // peers
    column = 0
    for pair, bits in ((w_in[:2], QKV_BITS), (w_in[2:], REST_BITS)):
        cols = slice(column, column + pair[0].shape[1])
        column = column + pair[0].shape[1]
        for k, m in enumerate(visit_order(bits)):
            at = pl.multiple_of(jnp.bitwise_xor(idx[0], m) * rows, rows)
            got = pair[k // (peers // 2)]
            k = k % (peers // 2)
            wall[pl.ds(at, rows), cols] = got[k * rows : (k + 1) * rows, :]
    qk_w = (n_q + n_kv) * HD
    all_w = (n_q + 2 * n_kv) * HD
    o_at = all_w + n_q * HD
    misc[...] = wall[:, o_at : o_at + LANES]
    misc_t = jnp.transpose(wall[:, o_at : o_at + LANES].astype(F32))
    gains[...] = misc_t[32:40, :]
    gain = misc_t[32:33, :]
    normed, _ = norm_parts(x[...].astype(F32))
    hidden = (normed * gain).astype(BF)
    hid[...] = hidden
    pre = jnp.dot(hidden, wall[:, :all_w], preferred_element_type=F32)
    qk = rotate_lanes(pre[:, :qk_w], cos[...], sin[...]).astype(BF)
    value = pre[:, qk_w:].astype(BF)
    qkv[...] = jnp.concatenate([qk, value], 1)
    length = x.shape[0]
    allowed = allowed_pairs(seg_c[...], seg_r[...], length)
    group = n_q // n_kv
    outs_h, logs = [], []
    for h in range(n_q):
        g = h // group
        q_h = qk[:, h * HD : (h + 1) * HD]
        k_g = qk[:, (n_q + g) * HD : (n_q + g + 1) * HD]
        v_g = value[:, g * HD : (g + 1) * HD]
        scores = mm(q_h, k_g, 1, 1) * score_scale
        total = jnp.sum(jnp.where(allowed, jnp.exp(scores), 0.0), axis=-1, keepdims=True)
        log_total = jnp.log(total)
        probs = jnp.where(allowed, jnp.exp(scores - log_total), 0.0).astype(BF)
        outs_h.append(jnp.dot(probs, v_g, preferred_element_type=F32).astype(BF))
        logs.append(log_total)
    flat = jnp.concatenate(outs_h, 1)
    att[...] = flat
    lane = lax.broadcasted_iota(jnp.int32, (length, LANES), 1)
    packed = jnp.zeros((length, LANES), F32)
    for h in range(n_q):
        packed = jnp.where(lane == h, logs[h], packed)
    log_out[...] = packed
    part[...] = mm(flat, wall[:, all_w:o_at], 1, 1)
    scatter_rows(part, parts, idx[1])


def post_attn_kernel(experts, shares, *refs):
    parts, (x, gains, misc, res, router, msg) = split_refs(refs, shares, 6)
    width = x.shape[1]
    total = x[...].astype(F32)
    for part in parts:
        total = total + part[...].astype(F32)
    res[...] = total
    normed, _ = norm_parts(total)
    h2 = (normed * gains[1:2, :]).astype(BF)
    logits = jnp.dot(h2, misc[...], preferred_element_type=F32)
    lane = lax.broadcasted_iota(jnp.int32, logits.shape, 1)
    exponent = jnp.where(lane < experts, jnp.exp(logits), 0.0)
    probs = exponent / jnp.sum(exponent, axis=-1, keepdims=True)
    router[...] = probs
    msg[:, :width] = h2
    msg[:, width:] = probs.astype(BF)


def gate_column(router_cols, expert):
    values = router_cols.astype(F32)
    lane = lax.broadcasted_iota(jnp.int32, values.shape, 1)
    return jnp.sum(jnp.where(lane == expert, values, 0.0), axis=-1, keepdims=True)


def load_down(own, pieces, down, shares):
    for m, piece in enumerate(pieces):
        at = pl.ds(pl.multiple_of(jnp.bitwise_xor(own, m) * 128, 128), 128)
        for t in range(shares):
            down[t * 128 : (t + 1) * 128, at] = piece[t, 256:384, :]


def weight_pack_kernel(shares, idx, gate, up, down, *outs):
    for c, chunk in enumerate(CHUNKS):
        for s in range(shares):
            for j, m in enumerate(chunk):
                e = jnp.bitwise_xor(idx[0], m) * shares + jnp.bitwise_xor(idx[1], s)
                for k, w in enumerate((gate, up, down)):
                    outs[c * shares + s][j, k * 128 : (k + 1) * 128, :] = w[e]


def regroup_kernel(shares, *refs):
    ins, outs = split_refs(refs, shares, len(refs) - shares)
    for j, out in enumerate(outs):
        for s in range(shares):
            out[s] = ins[s][j]


def weight_grad_kernel(shares, idx, *refs):
    first, second, outs = split_refs(refs, shares, len(CHUNKS[1]), 3)
    for c, chunk in enumerate(CHUNKS):
        for j, m in enumerate(chunk):
            for s in range(shares):
                e = jnp.bitwise_xor(idx[0], m) * shares + jnp.bitwise_xor(idx[1], s)
                got = first[s].at[j] if c == 0 else second[j].at[s]
                for k in range(3):
                    outs[k][e] = got[k * 128 : (k + 1) * 128, :].astype(F32)


def expert_pre_kernel(peers, shares, *refs):
    (idx,), grads_in, pieces, (hot_out, grads_out, raw, wgu, down) = split_refs(
        refs, 1, 2 * shares, peers, 5
    )
    ff = shares * 128
    width = grads_out.shape[1]
    span = 2 * grads_in[0].shape[0] // peers
    block = shares * span
    for m, piece in enumerate(pieces):
        at = pl.ds(pl.multiple_of(jnp.bitwise_xor(idx[0], m) * 128, 128), 128)
        for t in range(shares):
            wgu[at, t * 128 : (t + 1) * 128] = piece[t, 0:128, :]
            wgu[at, ff + t * 128 : ff + (t + 1) * 128] = piece[t, 128:256, :]
    load_down(idx[0], pieces, down, shares)
    expert = idx[0] * shares + idx[1]
    r = lax.broadcasted_iota(jnp.int32, (block, block), 0)
    c = lax.broadcasted_iota(jnp.int32, (block, block), 1)
    lower = jnp.where(r > c, 1.0, 0.0).astype(BF)
    slot = lax.broadcasted_iota(jnp.int32, (block, CAP), 1)

    def body(part, step, carry):
        grads = []
        for half in range(2):
            k = step * 2 + half
            at = pl.ds(pl.multiple_of(k * span, span), span)
            tokens = jnp.concatenate([ref[at, :] for ref in grads_in[part::2]], 0)
            k = k + part * (peers // 2)
            member = jnp.where(slot == expert, tokens[:, width:].astype(F32), 0.0)
            rank = jnp.dot(lower, member.astype(BF), preferred_element_type=F32)
            rank = jnp.sum(jnp.where(slot == expert, rank, 0.0), -1, keepdims=True)
            is_member = jnp.sum(member, axis=-1, keepdims=True) > 0.0
            place = jnp.where(is_member, rank, -1.0)
            hot = jnp.where(place == slot.astype(F32), 1.0, 0.0).astype(BF)
            hot_out[pl.ds(pl.multiple_of(k * block, block), block), :] = hot
            grads.append(mm(hot, tokens[:, :width], 0, 0).astype(BF))
        grad_rows = jnp.concatenate(grads, 0)
        step = step + part * (peers // 4)
        at = pl.ds(pl.multiple_of(step * 2 * CAP, 2 * CAP), 2 * CAP)
        grads_out[at, :] = grad_rows
        raw[at, :] = mm(grad_rows, down[...], 1, 1)
        return carry

    for part in range(2):
        lax.fori_loop(0, peers // 4, functools.partial(body, part), 0)


def expert_main_kernel(peers, shares, *refs):
    (idx,), rows_in, (hot_in, raw_in, wgu), back, outs = split_refs(
        refs, 1, 2 * shares, 3, shares, 5
    )
    rows_out, hid, gpu, gate_out, near_out = outs
    ff = raw_in.shape[1]
    width = rows_out.shape[1]
    span = 2 * rows_in[0].shape[0] // peers
    block = shares * span
    for s in range(shares):
        near_out[s * span : (s + 1) * span, :] = rows_in[2 * s][0:span, :width]
    expert = idx[0] * shares + idx[1]
    lane = lax.broadcasted_iota(jnp.int32, (2 * CAP, LANES), 1)

    def body(part, step, carry):
        slots, hots = [], []
        for half in range(2):
            k = step * 2 + half
            at = pl.ds(pl.multiple_of(k * span, span), span)
            tokens = jnp.concatenate([ref[at, :] for ref in rows_in[part::2]], 0)
            k = k + part * (peers // 2)
            hot = hot_in[pl.ds(pl.multiple_of(k * block, block), block), :]
            hots.append(hot)
            slots.append(mm(hot, tokens, 0, 0).astype(BF))
        rows = jnp.concatenate(slots, 0)
        step = step + part * (peers // 4)
        at = pl.ds(pl.multiple_of(step * 2 * CAP, 2 * CAP), 2 * CAP)
        gate = gate_column(rows[:, width:], expert)
        rows = rows[:, :width]
        rows_out[at, :] = rows
        gate_out[at, :] = jnp.broadcast_to(gate, (2 * CAP, LANES))
        pre = jnp.dot(rows, wgu[...], preferred_element_type=F32)
        raw = raw_in[at, :]
        gate_pre = pre[:, :ff]
        up_pre = pre[:, ff:]
        sig = jax.nn.sigmoid(gate_pre)
        silu = gate_pre * sig
        hidden = (silu * up_pre).astype(BF)
        hid[at, :] = hidden
        gate_grad = jnp.sum(hidden.astype(F32) * raw, axis=-1, keepdims=True)
        hidden_grad = raw * gate
        gp = (hidden_grad * up_pre * sig * (1.0 + gate_pre * (1.0 - sig))).astype(BF)
        up = (hidden_grad * silu).astype(BF)
        both = jnp.concatenate([gp, up], 1)
        gpu[at, :] = both
        row_grad = mm(both, wgu[...], 1, 1).astype(BF)
        tail_grad = jnp.where(lane == expert, gate_grad, 0.0).astype(BF)
        for half, hot in enumerate(hots):
            k = step * 2 + half
            cut = slice(half * CAP, (half + 1) * CAP)
            to = pl.ds(pl.multiple_of(k * span, span), span)
            spread = jnp.dot(hot, row_grad[cut, :], preferred_element_type=F32).astype(BF)
            tail = jnp.dot(hot, tail_grad[cut, :], preferred_element_type=F32).astype(BF)
            for s in range(shares):
                back[s][to, :width] = spread[s * span : (s + 1) * span, :]
                back[s][to, width:] = tail[s * span : (s + 1) * span, :]
        return carry

    for part in range(2):
        lax.fori_loop(0, peers // 4, functools.partial(body, part), 0)


def expert_rest_kernel(peers, shares, step, *refs):
    (idx,), ins, y_out, first_out, second_out, scratch = split_refs(
        refs, 1, 7, shares, len(CHUNKS[0]), shares, 3
    )
    rows, hid, gpu, gate_in, hot_in, grads, down = ins
    scaled, both_s, down_s = scratch
    span = y_out[0].shape[0] // peers
    block = shares * span
    scaled[...] = (grads[...].astype(F32) * gate_in[:, 0:1]).astype(BF)

    def out_rows(k, carry):
        at = pl.ds(pl.multiple_of(k * CAP, CAP), CAP)
        out = jnp.dot(hid[at, :], down[...], preferred_element_type=F32)
        out = (out * gate_in[at, 0:1]).astype(BF)
        hot = hot_in[pl.ds(pl.multiple_of(k * block, block), block), :]
        spread = jnp.dot(hot, out, preferred_element_type=F32).astype(BF)
        to = pl.ds(pl.multiple_of(k * span, span), span)
        for s in range(shares):
            y_out[s][to, :] = spread[s * span : (s + 1) * span, :]
        return carry

    lax.fori_loop(0, peers, out_rows, 0)

    low = idx[0] % 2
    for pair in range(peers // 2):
        q = jnp.bitwise_xor(pair, idx[0] // 2)
        at = pl.ds(pl.multiple_of(q * step, step), step)
        both_s[...] = mm(rows[:, at], gpu[...], 0, 0).astype(BF)
        down_s[...] = mm(hid[...], scaled[:, at], 0, 0).astype(BF)
        for odd in range(2):
            r = pl.ds(pl.multiple_of(jnp.bitwise_xor(low, odd) * 128, 128), 128)
            for t in range(shares):
                to = second_out[t].at[pair] if odd else first_out[pair].at[t]
                to[0:128, :] = both_s[r, t * 128 : (t + 1) * 128]
                to[128:256, :] = both_s[r, (shares + t) * 128 : (shares + t + 1) * 128]
                to[256:384, :] = down_s[t * 128 : (t + 1) * 128, r]


def hi_lo_rows(row, count):
    hi = row.astype(BF)
    lo = (row - hi.astype(F32)).astype(BF)
    place = lax.broadcasted_iota(jnp.int32, (count, row.shape[1]), 0)
    out = jnp.where(place == 0, hi.astype(F32), jnp.where(place == 1, lo.astype(F32), 0.0))
    return out.astype(BF)


def moe_back_kernel(*refs):
    backs, (router, res, gains, misc, out_grad, rgrad, msg) = split_refs(refs, 2, 7)
    own, width = res.shape
    total = backs[0][...].astype(F32) + backs[1][...].astype(F32)
    upstream = total[:, :width]
    prob_grad = total[:, width:]
    probs = router[...]
    logit = (probs * (prob_grad - jnp.sum(probs * prob_grad, axis=-1, keepdims=True))).astype(BF)
    upstream = upstream + mm(logit, misc[...], 1, 1)
    normed, inverse = norm_parts(res[...])
    gain_grad = jnp.sum(upstream * normed, axis=0, keepdims=True)
    grad = out_grad[...].astype(F32) + norm_backward(upstream, normed, inverse, gains[1:2, :])
    rgrad[...] = grad
    msg[0:own, :width] = grad.astype(BF)
    msg[0:own, width:] = logit
    msg[own:, :width] = hi_lo_rows(gain_grad, msg.shape[0] - own)
    msg[own:, width:] = jnp.zeros((msg.shape[0] - own, LANES), BF)


def attn_bwd_kernel(peers, shares, dims, *refs):
    n_q, n_kv = dims
    (idx,), msgs, ins, g_out, msg2, (sums, partial, resid) = split_refs(
        refs, 1, shares, 11, 2, shares, 3
    )
    wall, qkv, att, logs, cos, sin, seg_c, seg_r, hid, rows2, x = ins
    length, width = x.shape
    own = length // shares
    qk_w = (n_q + n_kv) * HD
    all_w = (n_q + 2 * n_kv) * HD
    o_at = all_w + n_q * HD
    for s, msg in enumerate(msgs):
        at = pl.multiple_of(jnp.bitwise_xor(idx[1], s) * own, own)
        resid[pl.ds(at, own), :] = msg[0:own, :width]
    logit = jnp.concatenate([msg[0:own, width:] for msg in msgs], 0)
    gain_moe = jnp.zeros((1, width), F32)
    for msg in msgs:
        extra = msg[own:, :width].astype(F32)
        gain_moe = gain_moe + jnp.sum(extra, axis=0, keepdims=True)
    att_grad = jnp.dot(resid[...], wall[:, all_w:o_at], preferred_element_type=F32).astype(BF)
    allowed = allowed_pairs(seg_c[...], seg_r[...], length)
    group = n_q // n_kv
    lane = lax.broadcasted_iota(jnp.int32, (length, LANES), 1)
    log_all = logs[...]
    q_grads, k_grads, v_grads = [], [], []
    for g in range(n_kv):
        k_g = qkv[:, (n_q + g) * HD : (n_q + g + 1) * HD]
        v_g = qkv[:, qk_w + g * HD : qk_w + (g + 1) * HD]
        k_sum = jnp.zeros((length, HD), F32)
        v_sum = jnp.zeros((length, HD), F32)
        for h in range(g * group, (g + 1) * group):
            cut = slice(h * HD, (h + 1) * HD)
            q_h = qkv[:, cut]
            log_h = jnp.sum(jnp.where(lane == h, log_all, 0.0), axis=-1, keepdims=True)
            scores = mm(q_h, k_g, 1, 1) * score_scale
            probs = jnp.where(allowed, jnp.exp(scores - log_h), 0.0)
            a_h = att_grad[:, cut]
            delta = jnp.sum(
                a_h.astype(F32) * att[:, cut].astype(F32), axis=-1, keepdims=True
            )
            prob_grad = mm(a_h, v_g, 1, 1)
            s_grad = (probs * (prob_grad - delta) * score_scale).astype(BF)
            q_grads.append(jnp.dot(s_grad, k_g, preferred_element_type=F32))
            k_sum = k_sum + mm(s_grad, q_h, 0, 0)
            v_sum = v_sum + mm(probs.astype(BF), a_h, 0, 0)
        k_grads.append(k_sum)
        v_grads.append(v_sum)
    qk_grad = jnp.concatenate(q_grads + k_grads, 1)
    qk_low = rotate_lanes(qk_grad, cos[...], -sin[...]).astype(BF)
    low = jnp.concatenate([qk_low, jnp.concatenate(v_grads, 1).astype(BF)], 1)
    sums[:, :all_w] = mm(hid[...], low, 0, 0)
    sums[:, all_w:o_at] = mm(resid[...], att[...], 0, 0)
    place = lax.broadcasted_iota(jnp.int32, (LANES, width), 0)
    gain_hi = gain_moe.astype(BF).astype(F32)
    partial[...] = mm(low, wall[:, :all_w], 1, 1)
    normed, _ = norm_parts(x[...].astype(F32))
    gain_attn = jnp.sum(partial[...] * normed, axis=0, keepdims=True)
    attn_hi = gain_attn.astype(BF).astype(F32)
    rows = jnp.zeros((LANES, width), F32)
    gain_rows = (gain_hi, gain_moe - gain_hi, attn_hi, gain_attn - attn_hi)
    for at, row in enumerate(gain_rows):
        rows = jnp.where(place == 32 + at, row, rows)
    sums[:, o_at:] = mm(rows2[...], logit, 0, 0) + jnp.transpose(rows)
    depth = width // peers
    for k, m in enumerate(visit_order(GRAD_BITS)):
        at = pl.multiple_of(jnp.bitwise_xor(idx[0], m) * depth, depth)
        out = g_out[k // (peers // 2)]
        k = k % (peers // 2)
        out[k * depth : (k + 1) * depth, :] = sums[pl.ds(at, depth), :].astype(BF)
    scatter_rows(partial, msg2, idx[1])


def input_grad_kernel(shares, *refs):
    parts, (x, gains, rgrad, out) = split_refs(refs, shares, 4)
    upstream = parts[0][...].astype(F32)
    for part in parts[1:]:
        upstream = upstream + part[...].astype(F32)
    normed, inverse = norm_parts(x[...].astype(F32))
    through = norm_backward(upstream, normed, inverse, gains[0:1, :])
    out[...] = (rgrad[...] + through).astype(BF)


def attn_grad_kernel(terms, widths, *refs):
    ins, (query, key, value, output, router, gain, gain_part) = split_refs(refs, terms, 7)
    q_w, kv_w, experts = widths
    total = ins[0][...].astype(F32)
    for ref in ins[1:]:
        total = total + ref[...].astype(F32)
    all_w = q_w + 2 * kv_w
    query[...] = total[:, :q_w]
    key[...] = total[:, q_w : q_w + kv_w]
    value[...] = total[:, q_w + kv_w : all_w]
    output[...] = jnp.transpose(total[:, all_w : all_w + q_w])
    tail = total[:, all_w + q_w :]
    router[...] = tail[:, :experts]
    tail_t = jnp.transpose(tail)
    gain[...] = tail_t[experts : experts + 1, :] + tail_t[experts + 1 : experts + 2, :]
    part = tail_t[experts + 2 : experts + 3, :] + tail_t[experts + 3 : experts + 4, :]
    gain_part[...] = jnp.broadcast_to(part, gain_part.shape)


def layer_out_kernel(first, second, res, out):
    total = first[...].astype(F32) + second[...].astype(F32)
    out[...] = (res[...] + total).astype(BF)


def swap(values, axis):
    got = [values[0]]
    for m in range(1, len(values)):
        got.append(lax.ppermute(values[m], axis, [(i, i ^ m) for i in range(len(values))]))
    return got


def permute(value, axis, bit):
    count = lax.axis_size(axis)
    return lax.ppermute(value, axis, [(i, i ^ bit) for i in range(count)])


def gather_dp(value, bits):
    for at, bit in enumerate(bits):
        got = permute(value, "dp", bit)
        if at == len(bits) - 1:
            return value, got
        value = jnp.concatenate([value, got], 0)


def gather_all(value):
    near = gather_dp(value, TOKEN_BITS)
    across = [permute(v, "tensor", 2) for v in near]
    beside = [permute(v, "tensor", 1) for v in near]
    corner = [permute(v, "tensor", 1) for v in across]
    return *near, *beside, *across, *corner


def reduce_dp(near, far, bits, other=None):
    got = permute(far, "dp", bits[2])
    near = near + got if other is None else near + other + got
    half = near.shape[0] // 2
    near = near[:half] + permute(near[half:], "dp", bits[1])
    half = half // 2
    return near[:half], permute(near[half:], "dp", bits[0])


def reduce_all(parts):
    half = parts[0].shape[0] // 2
    own = permute(parts[1], "tensor", 1)
    far = permute(parts[3], "tensor", 1)
    far_odd = permute(parts[2][half:] + far[half:], "tensor", 2)
    far_even = permute(parts[2][:half] + far[:half], "tensor", 2)
    odd = parts[0][half:] + own[half:] + far_odd
    return reduce_dp(parts[0][:half] + own[:half], odd, TOKEN_BITS, far_even)


def regroup(parts):
    shape = parts[0].shape
    return call(
        functools.partial(regroup_kernel, len(parts)),
        [((len(parts),) + shape[1:], BF)] * shape[0],
    )(*parts)


def move_chunks(parts):
    pieces = {}
    for c, chunk in enumerate(CHUNKS):
        for m, group in zip(chunk, regroup(parts[c])):
            pieces[m] = permute(group, "dp", m) if m else group
    return [pieces[m] for m in sorted(pieces)]


def per_device(
    rep,
    layer_input,
    seq_ids,
    expert_ids,
    out_grad,
    gain_attn,
    gain_moe,
    w_query,
    w_key,
    w_value,
    w_output,
    w_router,
    w_gate,
    w_up,
    w_down,
):
    peers = lax.axis_size("dp")
    shares = lax.axis_size("tensor")
    own, width = layer_input.shape
    experts = w_gate.shape[0]
    length = seq_ids.shape[1]
    q_w, kv_w = w_query.shape[1], w_key.shape[1]
    dims = (q_w // HD, kv_w // HD)
    all_w = q_w + 2 * kv_w
    pack_w = all_w + q_w + LANES
    slots = peers * CAP
    wide = width + LANES
    idx = jnp.stack([lax.axis_index("dp"), lax.axis_index("tensor")]).astype(jnp.int32)

    local = w_router.shape[0]
    pack_a = jnp.concatenate([w_query, w_key, w_value], axis=1)
    tail = [w_router, gain_attn[:, None], gain_moe[:, None]]
    tail.append(jnp.zeros((local, LANES - experts - 2), BF))
    pack_b = jnp.concatenate([w_output.T] + tail, axis=1)
    if rep > 1:
        pack_a = lax.all_gather(pack_a, "rep", axis=0, tiled=True)
        pack_b = lax.all_gather(pack_b, "rep", axis=0, tiled=True)
    packs = gather_dp(pack_a, QKV_BITS) + gather_dp(pack_b, REST_BITS)

    x_in = swap([layer_input] * shares, "tensor")

    if rep > 1:
        w_gate = lax.all_gather(w_gate, "rep", axis=1, tiled=True)
        w_up = lax.all_gather(w_up, "rep", axis=1, tiled=True)
        w_down = lax.all_gather(w_down, "rep", axis=2, tiled=True)
    weight_parts = call(
        functools.partial(weight_pack_kernel, shares),
        [((peers // 2, 384, LANES), BF)] * (2 * shares),
        smem=1,
    )(idx, w_gate, w_up, w_down)
    pieces = move_chunks(
        [
            swap(weight_parts[c * shares : (c + 1) * shares], "tensor")
            for c in range(len(CHUNKS))
        ],
    )
    ids_own = lax.dynamic_slice_in_dim(expert_ids, lax.axis_index("tensor") * own, own, 0)
    lanes = jnp.arange(LANES, dtype=jnp.int32)
    member = jnp.sum((ids_own[:, :, None] == lanes).astype(F32), axis=1).astype(BF)
    grads_in = gather_all(jnp.concatenate([out_grad, member], axis=1))

    segment = seq_ids[0]
    before = jnp.sum((segment[None, :] < segment[:, None]).astype(jnp.int32), axis=1)
    position = (jnp.arange(length, dtype=jnp.int32) - before).astype(F32)
    lane = jnp.arange(LANES, dtype=jnp.int32) % HD
    half = HD // 2
    frequency = rope_base ** (-2.0 * (lane % half).astype(F32) / HD)
    angles = position[:, None] * frequency[None, :]
    cosine = jnp.cos(angles)
    sine = jnp.where(lane[None, :] < half, -1.0, 1.0) * jnp.sin(angles)
    seg_c = segment[:, None]
    seg_r = segment[None, :]

    *parts, wall, gains, qkv, att, logs, hid, x_all, misc = call(
        functools.partial(attn_fwd_kernel, peers, shares, dims),
        [((own, width), BF)] * shares
        + [
            ((width, pack_w), BF),
            ((8, width), F32),
            ((length, all_w), BF),
            ((length, q_w), BF),
            ((length, LANES), F32),
            ((length, width), BF),
            ((length, width), BF),
            ((width, LANES), BF),
        ],
        scratch=[((length, width), F32)],
        smem=1,
    )(idx, *x_in, *packs, cosine, sine, seg_c, seg_r)

    parts = swap(parts, "tensor")
    res, router, msg = call(
        functools.partial(post_attn_kernel, experts, shares),
        [((own, width), F32), ((own, LANES), F32), ((own, wide), BF)],
    )(*parts, layer_input, gains, misc)
    rows_in = gather_all(msg)

    ff = w_gate.shape[2] * shares
    hots, grad_rows, raw, wgu, down = call(
        functools.partial(expert_pre_kernel, peers, shares),
        [
            ((peers * length, CAP), BF),
            ((slots, width), BF),
            ((slots, ff), F32),
            ((width, 2 * ff), BF),
            ((ff, width), BF),
        ],
        smem=1,
    )(idx, *grads_in, *pieces)
    outs = call(
        functools.partial(expert_main_kernel, peers, shares),
        [((peers * own, wide), BF)] * shares
        + [
            ((slots, width), BF),
            ((slots, ff), BF),
            ((slots, 2 * ff), BF),
            ((slots, LANES), F32),
            ((length, width), BF),
        ],
        smem=1,
    )(idx, *rows_in, hots, raw, wgu)
    row_back, saved, rows_near = outs[:shares], outs[shares:-1], outs[-1]
    back = reduce_all(row_back)
    rest = call(
        functools.partial(expert_rest_kernel, peers, shares, 256),
        [((peers * own, width), BF)] * shares
        + [((shares, 384, LANES), BF)] * len(CHUNKS[0])
        + [((len(CHUNKS[1]), 384, LANES), BF)] * shares,
        scratch=[((slots, width), BF), ((256, 2 * ff), BF), ((ff, 256), BF)],
        smem=1,
    )(idx, *saved, hots, grad_rows, down)
    y_parts, first, second = rest[:shares], rest[shares : shares + 4], rest[shares + 4 :]
    first = [permute(v, "dp", m) if m else v for m, v in zip(CHUNKS[0], first)]
    first = swap(regroup(first), "tensor")
    second = regroup(swap(second, "tensor"))
    second = [permute(v, "dp", m) for m, v in zip(CHUNKS[1], second)]
    mixed = reduce_all(y_parts)
    rgrad, msg = call(
        moe_back_kernel, [((own, width), F32), ((own + 16, wide), BF)]
    )(*back, router, res, gains, misc, out_grad)
    msgs = swap([msg] * shares, "tensor")

    outs = call(
        functools.partial(attn_bwd_kernel, peers, shares, dims),
        [((width // 2, pack_w), BF)] * 2 + [((own, width), BF)] * shares,
        scratch=[((width, pack_w), F32), ((length, width), F32), ((length, width), BF)],
        smem=1,
    )(idx, *msgs, wall, qkv, att, logs, cosine, sine, seg_c, seg_r, hid, rows_near, x_all)
    msg2 = outs[2:]
    terms = reduce_dp(outs[0], outs[1], GRAD_BITS)
    if rep > 1:
        total = terms[0].astype(F32) + terms[1].astype(F32)
        terms = (lax.psum_scatter(total, "rep", scatter_dimension=0, tiled=True),)
    rows_own = terms[0].shape[0]
    q_grad, k_grad, v_grad, o_grad, router_grad, gain_moe_grad, gain_part = call(
        functools.partial(attn_grad_kernel, len(terms), (q_w, kv_w, experts)),
        [
            ((rows_own, q_w), F32),
            ((rows_own, kv_w), F32),
            ((rows_own, kv_w), F32),
            ((q_w, rows_own), F32),
            ((rows_own, experts), F32),
            ((1, rows_own), F32),
            ((8, rows_own), F32),
        ],
    )(*terms)
    gain_attn_grad = sum(swap([gain_part] * shares, "tensor"))[0]

    msg2 = swap(msg2, "tensor")
    (input_grad,) = call(
        functools.partial(input_grad_kernel, shares), [((own, width), BF)]
    )(*msg2, layer_input, gains, rgrad)

    (layer_output,) = call(layer_out_kernel, [((own, width), BF)])(*mixed, res)

    gate_grad, up_grad, down_grad = call(
        functools.partial(weight_grad_kernel, shares),
        [((experts, 128, LANES), F32)] * 3,
        smem=1,
    )(idx, *first, *second)
    if rep > 1:
        gate_grad = lax.psum_scatter(gate_grad, "rep", scatter_dimension=1, tiled=True)
        up_grad = lax.psum_scatter(up_grad, "rep", scatter_dimension=1, tiled=True)
        down_grad = lax.psum_scatter(down_grad, "rep", scatter_dimension=2, tiled=True)
    return (
        layer_output,
        input_grad,
        gain_attn_grad,
        gain_moe_grad.reshape(-1),
        q_grad,
        k_grad,
        v_grad,
        o_grad,
        router_grad,
        gate_grad,
        up_grad,
        down_grad,
    )


def solution(mesh):
    shares = mesh.shape["tensor"]
    peers = 32 // shares
    rep = mesh.shape["dp"] // peers
    dp = "dp"
    if rep > 1:
        devices = np.asarray(mesh.devices).reshape(peers, rep, shares)
        mesh = jax.sharding.Mesh(devices, ("dp", "rep", "tensor"))
        dp = ("dp", "rep")
    both = ("dp", "tensor") if rep == 1 else ("dp", "rep", "tensor")
    in_specs = (
        P(both, None),
        P(dp, None),
        P(dp, None),
        P(both, None),
        P(dp),
        P(dp),
        P(dp, "tensor"),
        P(dp, "tensor"),
        P(dp, "tensor"),
        P("tensor", dp),
        P(dp, None),
        P(None, dp, "tensor"),
        P(None, dp, "tensor"),
        P(None, "tensor", dp),
    )
    out_specs = (
        P(both, None),
        P(both, None),
        P(dp),
        P(dp),
        P(dp, "tensor"),
        P(dp, "tensor"),
        P(dp, "tensor"),
        P("tensor", dp),
        P(dp, None),
        P(None, dp, "tensor"),
        P(None, dp, "tensor"),
        P(None, "tensor", dp),
    )

    def body(*args):
        return per_device(rep, *args)

    return jax.shard_map(
        body, mesh=mesh, in_specs=in_specs, out_specs=out_specs, check_vma=False
    )
```
